32 devices in a mesh: dp: 8 (over z, x), tensor: 4 (over y, core).
Axes of the slice: x: 2, y: 2, z: 4, core: 2. Of those that a mesh axis runs over, the one named last changes fastest.
Arguments:
- tokens: bfloat16 [16384, 512], P(('dp', 'tensor')), may hold values from -6 to 6
- segment_ids: int32 [16384], P('dp'), may hold values from 0 to 63, never falling along the last dimension, each value on 1 to 8192 neighbouring positions
- query_weight: float32 [512, 512], P('dp', 'tensor'), may hold values from -0.25 to 0.25
- key_weight: float32 [512, 512], P('dp', 'tensor'), may hold values from -0.25 to 0.25
- value_weight: float32 [512, 512], P('dp', 'tensor'), may hold values from -0.25 to 0.25
- output_weight: float32 [512, 512], P('tensor', 'dp'), may hold values from -2.4 to 2.4
- inner_weight: float32 [512, 2048], P('dp', 'tensor'), may hold values from -0.25 to 0.25
- outer_weight: float32 [2048, 512], P('tensor', 'dp'), may hold values from -0.125 to 0.125
- inner_bias: float32 [2048], replicated, may hold values from -3 to 3
- first_gain: float32 [512], replicated, may hold values from 0.1 to 1.9
- first_shift: float32 [512], replicated, may hold values from -3 to 3
- second_gain: float32 [512], replicated, may hold values from 0.1 to 1.9
- second_shift: float32 [512], replicated, may hold values from -3 to 3
- mixer_bias: float32 [512], replicated, may hold values from -3 to 3
- outer_bias: float32 [512], replicated, may hold values from -3 to 3
- grad_out: bfloat16 [16384, 512], P(('dp', 'tensor')), may hold values from -6 to 6
Outputs:
- layer_out: bfloat16 [16384, 512], P(('dp', 'tensor'))
- grad_tokens: bfloat16 [16384, 512], P(('dp', 'tensor'))
- grad_query: float32 [512, 512], P('dp', 'tensor')
- grad_key: float32 [512, 512], P('dp', 'tensor')
- grad_value: float32 [512, 512], P('dp', 'tensor')
- grad_output: float32 [512, 512], P('tensor', 'dp')
- grad_inner: float32 [512, 2048], P('dp', 'tensor')
- grad_outer: float32 [2048, 512], P('tensor', 'dp')
- grad_inner_bias: float32 [2048], replicated
- grad_first_gain: float32 [512], replicated
- grad_first_shift: float32 [512], replicated
- grad_second_gain: float32 [512], replicated
- grad_second_shift: float32 [512], replicated
- grad_mixer_bias: float32 [512], replicated
- grad_outer_bias: float32 [512], replicated
The draws below stay inside these ranges and needn't reach their ends.
Inputs may be any that keep to these rules, and one draw needn't show every extreme that they name: `segment_ids`: segment ids never fall along the sequence; a document holds 1 to 8192 consecutive tokens, and one holds exactly 8192.
All inputs are finite; a program needn't handle non-finite values.
Results may differ from the reference program's by a relative error of at most 0.015.
Values may be sent and summed in bfloat16 or wider, within the bound.
A program may use at most 128 MiB of HBM per device.

```python
import math
import jax
import jax.numpy as jnp
import numpy as np
from jax import lax

D = 512
HEADS = 8
HEAD = 64
FF = 2048
TOKENS = 16384
DOCS = 64
DOC_MOST = 8192


def strengthened(values, rng, source, target, parts, factor):
    owner, partner = [(jnp.arange(values.shape[axis_at]) // (values.shape[axis_at] // parts)).reshape([-1 if axis == axis_at else 1 for axis in range(values.ndim)]) for axis_at in (source, target)]
    chosen = jax.random.permutation(rng, parts)[partner]
    strong = (owner == chosen) | (owner == (partner + parts // 2) % parts)
    return jnp.where(strong, factor * values, values)


def levels(own_key, extent, cuts, smallest, largest):
    level = 1.0
    for position, parts in cuts:
        steps = jax.random.uniform(jax.random.fold_in(jax.random.fold_in(own_key, 6), position), (parts,), jnp.float32, smallest / len(cuts), largest / len(cuts))
        level = level * jnp.repeat(jnp.exp(steps), extent[position] // parts).reshape((-1,) + (1,) * (len(extent) - 1 - position))
    return level


def split_up(number_of, total, limit, lean):
    loads = [(1 << 20) // math.isqrt(rank ** lean) + 1 for rank in range(2, number_of + 1)]
    spare, holding = total - limit - (number_of - 1), [1] * (number_of - 1)
    while spare > 0:
        movable = [i for i in range(number_of - 1) if holding[i] < limit]
        pool, budget = sum([loads[i] for i in movable]), spare
        for i in movable:
            addition = min(limit - holding[i], max(1, budget * loads[i] // pool), spare)
            holding[i] = holding[i] + addition
            spare = spare - addition
    return np.array([limit] + holding)


def uneven(rng, count, total, bound, slope):
    if count == 2:
        one = jax.random.randint(rng, (), max(1, total - bound), min(bound, total - 1) + 1)
        return jnp.stack([one, total - one])
    sizes = jnp.asarray(split_up(count, total, bound, slope), jnp.int32)
    couples = (count - 1) // 2
    donor, sink = sizes[1:1 + 2 * couples:2], sizes[2:2 + 2 * couples:2]
    room = jnp.minimum(donor - 1, bound - sink)
    moved = jax.random.randint(jax.random.fold_in(rng, 1), (couples,), 0, 1 << 20) % (room + 1)
    sizes = sizes.at[1:1 + 2 * couples:2].set(donor - moved).at[2:2 + 2 * couples:2].set(sink + moved)
    return sizes[jax.random.permutation(jax.random.fold_in(rng, 2), count)]


def noise(stream_key, dims, deviation, limit, cuts=(), held_as=jnp.bfloat16):
    loudness = levels(stream_key, dims, cuts, -0.22, 0.18) if cuts else 1.0
    values = jax.random.normal(stream_key, dims, jnp.float32) * deviation * loudness
    return jnp.minimum(jnp.maximum(values, -limit), limit).astype(held_as)


def noise_with(key, shape, scale, most, split, heavy, kind=jnp.bfloat16):
    values = scale * jax.random.normal(key, shape, jnp.float32)
    if split:
        values = values * levels(key, shape, split, -0.22, 0.18)
    return jnp.clip(strengthened(values, jax.random.fold_in(key, 3), *heavy), -most, most).astype(kind)


def setup_inputs(seed: int = 0) -> dict:
    arg_keys = jax.random.split(jax.random.key(seed), 17)
    return {
        "tokens": noise(arg_keys[0], (TOKENS, D), 1.0, 6.0, ((0, 32),)),
        "segment_ids": jnp.searchsorted(jnp.cumsum(uneven(arg_keys[1], DOCS, TOKENS, DOC_MOST, 2)), jnp.arange(TOKENS), side="right").astype(jnp.int32),
        "query_weight": noise(arg_keys[2], (D, D), D ** -0.5, 0.25, ((0, 8), (1, 4)), jnp.float32),
        "key_weight": noise(arg_keys[3], (D, D), D ** -0.5, 0.25, ((0, 8), (1, 4)), jnp.float32),
        "value_weight": noise(arg_keys[4], (D, D), D ** -0.5, 0.25, ((0, 8), (1, 4)), jnp.float32),
        "output_weight": noise(arg_keys[5], (D, D), 0.4, 2.4, ((0, 4), (1, 8)), jnp.float32),
        "inner_weight": noise(arg_keys[6], (D, FF), D ** -0.5, 0.25, ((0, 8), (1, 4)), jnp.float32),
        "outer_weight": noise(arg_keys[7], (FF, D), FF ** -0.5, 0.125, ((0, 4), (1, 8)), jnp.float32),
        "inner_bias": noise(arg_keys[8], (FF,), 0.5, 3.0, (), jnp.float32),
        "first_gain": jnp.clip(1.0 + 0.18 * jax.random.normal(arg_keys[9], (D,), jnp.float32), 0.1, 1.9),
        "first_shift": noise(arg_keys[10], (D,), 0.5, 3.0, (), jnp.float32),
        "second_gain": jnp.clip(1.0 + 0.18 * jax.random.normal(arg_keys[11], (D,), jnp.float32), 0.1, 1.9),
        "second_shift": noise(arg_keys[12], (D,), 0.5, 3.0, (), jnp.float32),
        "mixer_bias": noise(arg_keys[13], (D,), 0.5, 3.0, (), jnp.float32),
        "outer_bias": noise(arg_keys[14], (D,), 0.5, 3.0, (), jnp.float32),
        "grad_out": noise_with(arg_keys[15], (TOKENS, D), 1.0, 6.0, ((0, 32),), (0, 1, 32, 2.75)),
    }


EPSILON = 1e-05
HIGHEST = lax.Precision.HIGHEST

@jax.custom_vjp
def low(v):
    return lax.optimization_barrier(v.astype(jnp.bfloat16)).astype(jnp.float32)

@jax.custom_vjp
def low_back(v):
    return v

def low_keep(v):
    return (low(v), None)

def low_pass(kept, grad):
    return (grad,)

def back_keep(v):
    return (v, None)

def back_low(kept, grad):
    return (low(grad),)
low.defvjp(low_keep, low_pass)
low_back.defvjp(back_keep, back_low)

def layer_norm(values, gain, shift):
    center = values - lax.optimization_barrier(jnp.mean(values, axis=-1, keepdims=True))
    spread = lax.optimization_barrier(jnp.mean(center * center, axis=-1, keepdims=True))
    return center * lax.rsqrt(spread + EPSILON) * gain + shift

def feature(values):
    return jax.nn.elu(values) + 1.0

def causal_mask(block_segs):
    block_size = block_segs.shape[0]
    later_row = lax.broadcasted_iota(jnp.int32, (block_size, block_size), 0)
    earlier_col = lax.broadcasted_iota(jnp.int32, (block_size, block_size), 1)
    return (later_row >= earlier_col) & (block_segs[:, None] == block_segs[None, :])

def reference(tokens, segment_ids, query_weight, key_weight, value_weight, output_weight, inner_weight, outer_weight, inner_bias, first_gain, first_shift, second_gain, second_shift, mixer_bias, outer_bias, grad_out):
    block_rows = min(512, TOKENS)
    block_count = TOKENS // block_rows
    seg_blocks = segment_ids.reshape(block_count, block_rows)

    def forward(inputs_all, w_query, w_key, w_value, w_output, w_inner, w_outer, b_inner, gain_one, shift_one, gain_two, shift_two, b_mixer, b_outer):
        query_low = low(w_query)
        key_low = low(w_key)
        value_low = low(w_value)
        output_low = low(w_output)
        inner_low = low(w_inner)
        outer_low = low(w_outer)

        def block(carry, pieces):
            carry_state, carry_total, carry_key = carry
            rows_in, block_segs = pieces
            normed = low(layer_norm(rows_in, gain_one, shift_one))
            query_raw = low_back(jnp.dot(normed, query_low, precision=HIGHEST))
            key_raw = low_back(jnp.dot(normed, key_low, precision=HIGHEST))
            value_raw = low_back(jnp.dot(normed, value_low, precision=HIGHEST))
            head_shape = (block_rows, HEADS, HEAD)
            queries = low(feature(query_raw)).reshape(head_shape)
            keys_all = low(feature(key_raw)).reshape(head_shape)
            values_all = low(value_raw).reshape(head_shape)
            allowed = causal_mask(block_segs)[None]
            scores = jnp.einsum('thd,shd->hts', queries, keys_all, precision=HIGHEST)
            weights = jnp.where(allowed, scores, 0.0)
            carried = (block_segs == carry_key).astype(jnp.float32)
            numerator = jnp.einsum('hts,she->the', weights, values_all, precision=HIGHEST)
            numerator = numerator + carried[:, None, None] * jnp.einsum('thd,hde->the', queries, carry_state, precision=HIGHEST)
            denominator = lax.optimization_barrier(jnp.sum(weights, axis=-1)).T + carried[:, None] * jnp.einsum('thd,hd->th', queries, carry_total, precision=HIGHEST)
            mixed = low((numerator / denominator[..., None]).reshape(block_rows, D))
            residual = rows_in + low_back(jnp.dot(mixed, output_low, precision=HIGHEST) + b_mixer)
            second = low(layer_norm(residual, gain_two, shift_two))
            hidden = low_back(jnp.dot(second, inner_low, precision=HIGHEST) + b_inner)
            activated = low(jax.nn.gelu(hidden, approximate=False))
            result = residual + jnp.dot(activated, outer_low, precision=HIGHEST) + b_outer
            last_id = block_segs[-1]
            tail = (block_segs == last_id).astype(jnp.float32)
            tail_keys = keys_all * tail[:, None, None]
            next_state = jnp.where(carry_key == last_id, carry_state, 0.0) + jnp.einsum('thd,the->hde', tail_keys, values_all, precision=HIGHEST)
            next_total = jnp.where(carry_key == last_id, carry_total, 0.0) + lax.optimization_barrier(jnp.sum(tail_keys, axis=0))
            return ((next_state, next_total, last_id), result)
        start = (jnp.zeros((HEADS, HEAD, HEAD), jnp.float32), jnp.zeros((HEADS, HEAD), jnp.float32), jnp.full((), -1, jnp.int32))
        _, results = lax.scan(jax.checkpoint(block), start, (inputs_all.reshape(block_count, block_rows, D), seg_blocks))
        return results.reshape(TOKENS, D)
    result, pull = jax.vjp(forward, tokens.astype(jnp.float32), query_weight, key_weight, value_weight, output_weight, inner_weight, outer_weight, inner_bias, first_gain, first_shift, second_gain, second_shift, mixer_bias, outer_bias)
    grads = pull(grad_out.astype(jnp.float32))
    return (result.astype(jnp.bfloat16), grads[0].astype(jnp.bfloat16), grads[1], grads[2], grads[3], grads[4], grads[5], grads[6], grads[7], grads[8], grads[9], grads[10], grads[11], grads[12], grads[13])
```

```python
import functools

import jax
import jax.numpy as jnp
from jax import lax
from jax.experimental import pallas as pl
from jax.experimental.pallas import tpu as pltpu
from jax.sharding import PartitionSpec as P

HEAD = 64
LANES = 128
EPSILON = 1e-05
MESH = pl.DeviceIdType.MESH
F32 = jnp.float32
BF16 = jnp.bfloat16
OUTER = 4
STATE_ROWS = HEAD + 8
VMEM_LIMIT = 56 << 20


def nn(a, b):
    return lax.dot_general(a, b, (((1,), (0,)), ((), ())), preferred_element_type=F32)


def nt(a, b):
    return lax.dot_general(a, b, (((1,), (1,)), ((), ())), preferred_element_type=F32)


def tn(a, b):
    return lax.dot_general(a, b, (((0,), (0,)), ((), ())), preferred_element_type=F32)


class Place:
    def __init__(self, dp_size, tensor_size):
        self.nd, self.nt = dp_size, tensor_size
        self.inner, self.ny = dp_size // OUTER, tensor_size // 2
        self.d, self.t = lax.axis_index("dp"), lax.axis_index("tensor")
        self.o, self.i = self.d // self.inner, self.d % self.inner
        self.y, self.c = self.t // 2, self.t % 2

    def at(self, do=0, di=0, dy=0, dc=0):
        o, i = (self.o + do) % OUTER, (self.i + di) % self.inner
        y, c = (self.y + dy) % self.ny, (self.c + dc) % 2
        return (o * self.inner + i, y * 2 + c)

    def outer_peers(self):
        return [(k, 0, 0, 0) for k in range(1, OUTER)]

    def plane_peers(self):
        return [
            (0, di, dy, 0) for di in range(self.inner) for dy in range(self.ny) if di or dy
        ]

    def group_peers(self):
        return [(0, 0, dy, dc) for dy in range(self.ny) for dc in range(2) if dy or dc]

    def dp_peers(self):
        return [(do, di, 0, 0) for do in range(OUTER) for di in range(self.inner) if do or di]

    def greet(self):
        peers = []
        for peer in (
            self.outer_peers()
            + self.plane_peers()
            + self.group_peers()
            + self.dp_peers()
        ):
            if peer not in peers:
                peers.append(peer)
        barrier = pltpu.get_barrier_semaphore()
        for peer in peers:
            pl.semaphore_signal(
                barrier, inc=1, device_id=self.at(*peer), device_id_type=MESH
            )
        pl.semaphore_wait(barrier, len(peers))


def remote(src, dst, send, recv, peer):
    return pltpu.make_async_remote_copy(
        src_ref=src,
        dst_ref=dst,
        send_sem=send,
        recv_sem=recv,
        device_id=peer,
        device_id_type=MESH,
    )


class Gather:
    def __init__(self, place, mine, held, send, got_outer, got_plane, got_core):
        self.p, self.mine, self.held = place, mine, held
        self.send, self.got_outer = send, got_outer
        self.got_plane, self.got_core = got_plane, got_core
        self.started, self.count = [], 0

    def _go(self, src, dst, recv, peer):
        copy = remote(src, dst, self.send.at[self.count], recv, peer)
        self.count += 1
        copy.start()
        self.started.append(copy)
        return copy

    def start(self):
        p = self.p
        place = self.held.at[p.t, p.o, p.i]
        self.to_outer = [
            self._go(self.mine, place, self.got_outer.at[k - 1], p.at(*peer))
            for k, peer in enumerate(p.outer_peers(), 1)
        ]
        self._spread(0, self.mine)

    def _spread(self, k, src):
        p = self.p
        o = (p.o + OUTER - k) % OUTER
        for j, peer in enumerate(p.plane_peers()):
            self._go(src, self.held.at[p.t, o, p.i], self.got_plane.at[j, k], p.at(*peer))
        self._go(src, self.held.at[p.t, o, p.i], self.got_core.at[p.y], p.at(dc=1))

    def outer_step(self):
        p = self.p
        for k in range(1, OUTER):
            o = (p.o + OUTER - k) % OUTER
            block = self.held.at[p.t, o, p.i]
            remote(block, block, self.send.at[0], self.got_outer.at[k - 1], p.at()).wait_recv()
            self._spread(k, block)

    def plane_step(self):
        p = self.p
        for k in range(OUTER):
            o = (p.o + OUTER - k) % OUTER
            for j, (_, di, dy, _) in enumerate(p.plane_peers()):
                i, y = (p.i + p.inner - di) % p.inner, (p.y + p.ny - dy) % p.ny
                block = self.held.at[y * 2 + p.c, o, i]
                remote(block, block, self.send.at[0], self.got_plane.at[j, k], p.at()).wait_recv()
                self._go(block, block, self.got_core.at[y], p.at(dc=1))

    def core_step(self):
        p = self.p
        for y in range(p.ny):
            block = self.held.at[y * 2 + 1 - p.c]
            remote(block, block, self.send.at[0], self.got_core.at[y], p.at()).wait_recv()

    def finish(self):
        for copy in self.started:
            copy.wait_send()

    @staticmethod
    def semaphores(nd, nt):
        plane = (nd // OUTER) * (nt // 2) - 1
        sends = (OUTER - 1) + OUTER * (plane + 1) + OUTER * plane
        return [
            pltpu.SemaphoreType.DMA((sends,)),
            pltpu.SemaphoreType.DMA((OUTER - 1,)),
            pltpu.SemaphoreType.DMA((plane, OUTER)),
            pltpu.SemaphoreType.DMA((nt // 2,)),
        ]


class Exchange:
    def __init__(self, place, firsts, lasts, back, own, near, far, made, entering, sems):
        self.p, self.back = place, back
        self.own, self.near, self.far = own, near, far
        self.made, self.entering = made, entering
        self.edge, self.inlet = (firsts, lasts) if back else (lasts, firsts)
        self.s_send, self.s_near, self.s_far, self.s_enter = sems
        self.started, self.count = [], 0

    def _go(self, src, dst, recv, peer):
        copy = remote(src, dst, self.s_send.at[self.count], recv, peer)
        self.count += 1
        copy.start()
        self.started.append(copy)

    def step_near(self):
        p = self.p
        for peer in p.group_peers():
            to = p.at(*peer)
            self._go(self.own.at[to[1]], self.near.at[p.t], self.s_near.at[p.t], to)
        self.near[p.t] = self.own[p.t]

    def step_far(self):
        p = self.p
        for _, _, dy, dc in p.group_peers():
            t = ((p.y + p.ny - dy) % p.ny) * 2 + (p.c + dc) % 2
            block = self.near.at[t]
            remote(block, block, self.s_send.at[0], self.s_near.at[t], p.at()).wait_recv()
        border = 0 if self.back else p.nt - 1
        ids = self.edge[border : border + 1, :]
        total = jnp.zeros((STATE_ROWS, LANES), F32)
        for j in range(p.nt):
            total = total + jnp.where(self.edge[j : j + 1, :] == ids, self.near[j], 0.0)
        rows = lax.broadcasted_iota(jnp.int32, (STATE_ROWS, LANES), 0)
        self.far[p.d] = jnp.where(rows > HEAD, jnp.broadcast_to(ids, rows.shape), total)
        for peer in p.dp_peers():
            self._go(self.far.at[p.d], self.far.at[p.d], self.s_far.at[p.d], p.at(*peer))

    def step_enter(self):
        p = self.p
        for do, di, _, _ in p.dp_peers():
            o, i = (p.o + OUTER - do) % OUTER, (p.i + p.inner - di) % p.inner
            d = o * p.inner + i
            block = self.far.at[d]
            remote(block, block, self.s_send.at[0], self.s_far.at[d], p.at()).wait_recv()
        for j in range(p.nt):
            inlet = self.inlet[j : j + 1, :]
            total = jnp.zeros((STATE_ROWS, LANES), F32)
            for d in range(p.nd):
                ids = self.far[d, HEAD + 1 : HEAD + 2, :]
                wanted = jnp.where(d > p.d if self.back else d < p.d, ids, -1.0)
                total = total + jnp.where(wanted == inlet, self.far[d], 0.0)
            for k in range(j + 1, p.nt) if self.back else range(j):
                total = total + jnp.where(self.edge[k : k + 1, :] == inlet, self.near[k], 0.0)
            self.made[j] = total
        for peer in p.group_peers():
            to = p.at(*peer)
            self._go(self.made.at[to[1]], self.entering.at[p.t], self.s_enter.at[p.t], to)
        self.entering[p.t] = self.made[p.t]

    def arrive(self):
        p = self.p
        for _, _, dy, dc in p.group_peers():
            t = ((p.y + p.ny - dy) % p.ny) * 2 + (p.c + dc) % 2
            block = self.entering.at[t]
            remote(block, block, self.s_send.at[0], self.s_enter.at[t], p.at()).wait_recv()

    def finish(self):
        for copy in self.started:
            copy.wait_send()

    @staticmethod
    def scratch(nd, nt):
        return [
            pltpu.VMEM((nt, STATE_ROWS, LANES), F32),
            pltpu.VMEM((nt, STATE_ROWS, LANES), F32),
            pltpu.VMEM((nd, STATE_ROWS, LANES), F32),
            pltpu.VMEM((nt, STATE_ROWS, LANES), F32),
        ]

    @staticmethod
    def semaphores(nd, nt):
        return [
            pltpu.SemaphoreType.DMA((2 * (nt - 1) + nd - 1,)),
            pltpu.SemaphoreType.DMA((nt,)),
            pltpu.SemaphoreType.DMA((nd,)),
            pltpu.SemaphoreType.DMA((nt,)),
        ]


def left_lanes(shape):
    return lax.broadcasted_iota(jnp.int32, shape, len(shape) - 1) < HEAD


def split_heads(block, fill):
    left = left_lanes(block.shape)
    other = jnp.full_like(block, fill)
    return jnp.where(left, block, other), jnp.where(left, other, block)


def feature(values):
    return jnp.where(values > 0.0, values + 1.0, jnp.exp(jnp.minimum(values, 0.0)))


def pack_state(product):
    left = left_lanes((HEAD, LANES))
    return jnp.where(left, product[:HEAD], product[HEAD:])


def wide_state(packed):
    left = left_lanes((HEAD, LANES))
    zero = jnp.zeros_like(packed)
    return jnp.concatenate([jnp.where(left, packed, zero), jnp.where(left, zero, packed)], axis=0)


def two_parts(values):
    high = values.astype(BF16)
    return high, (values - high.astype(F32)).astype(BF16)


def same_head():
    row = lax.broadcasted_iota(jnp.int32, (LANES, LANES), 0) < HEAD
    return row == left_lanes((LANES, LANES))


def make_mask(segc, segr, mask, rows):
    total = segc.shape[0]
    for start in range(0, total, rows):
        at = lax.broadcasted_iota(jnp.int32, (rows, total), 0) + start
        key = lax.broadcasted_iota(jnp.int32, (rows, total), 1)
        same = segc[start : start + rows, :] == segr[...]
        mask[start : start + rows, :] = jnp.where((at >= key) & same, 1.0, 0.0).astype(BF16)


def kernel_forward(
    nd, nt_,
    tokens, mine_a, mine_b, segc, segr, firsts, lasts, gain, shift,
    held_a, held_b, normed, fq, fk, vb, mixed, rden, entering,
    mask, num_s, den_s, own, near, far, made, *sems,
):
    p = Place(nd, nt_)
    rows_all = tokens.shape[0]
    ga = Gather(p, mine_a, held_a, *sems[0:4])
    gb = Gather(p, mine_b, held_b, *sems[4:8])
    ex = Exchange(p, firsts, lasts, False, own, near, far, made, entering, sems[8:12])
    p.greet()
    ga.start()
    gb.start()
    held_a[p.t, p.o, p.i] = mine_a[...]
    held_b[p.t, p.o, p.i] = mine_b[...]
    step = 128

    def norm(k, _):
        at = pl.ds(pl.multiple_of(k * step, step), step)
        x = tokens[at, :].astype(F32)
        center = x - jnp.mean(x, axis=-1, keepdims=True)
        spread = jnp.mean(center * center, axis=-1, keepdims=True)
        y = center * lax.rsqrt(spread + EPSILON) * gain[...] + shift[...]
        normed[at, :] = y.astype(BF16)
        return 0

    lax.fori_loop(0, rows_all // step, norm, 0)
    make_mask(segc, segr, mask, 128)
    ga.outer_step()
    ga.plane_step()
    gb.outer_step()
    ga.core_step()
    last = segr[:, rows_all - 1 : rows_all]
    tail = segc[...] == last
    depth = nd * mine_a.shape[0]

    def keys_values(g, _):
        w = held_a[g].reshape(depth, 3 * LANES)
        kv = nn(normed[...], w[:, LANES:])
        keys = feature(kv[:, :LANES]).astype(BF16)
        values = kv[:, LANES:].astype(BF16)
        fk[g] = keys
        vb[g] = values
        kept = jnp.where(tail, keys, jnp.zeros_like(keys))
        own[g, :HEAD, :] = pack_state(tn(kept, values))
        sums = jnp.sum(kept.astype(F32), axis=0, keepdims=True)
        own[g, HEAD:, :] = jnp.broadcast_to(sums, (STATE_ROWS - HEAD, LANES))
        return 0

    lax.fori_loop(0, nt_, keys_values, 0)
    ex.step_near()

    def queries(g, _):
        w = held_a[g].reshape(depth, 3 * LANES)
        fq[g] = feature(nn(normed[...], w[:, :LANES])).astype(BF16)
        return 0

    lax.fori_loop(0, nt_, queries, 0)
    ex.step_far()
    block = min(256, rows_all)

    def inside(g, _):
        values = split_heads(vb[g], 1.0)
        for start in range(0, rows_all, block):
            end = start + block
            now = mask[start:end, :end]
            query = split_heads(fq[g, start:end, :], 0.0)
            keys = fk[g, :end, :]
            parts = []
            for h in range(2):
                scores = nt(query[h], keys).astype(BF16) * now
                parts.append(nn(scores, values[h][:end]))
            left = left_lanes(parts[0].shape)
            num_s[g, start:end, :] = jnp.where(left, parts[0], parts[1])
            den_s[g, start:end, :] = pltpu.roll(
                jnp.where(left, parts[1], parts[0]), HEAD, 1
            )
        return 0

    lax.fori_loop(0, nt_ // 2, inside, 0)
    ex.step_enter()
    lax.fori_loop(nt_ // 2, nt_, inside, 0)
    gb.plane_step()
    ex.arrive()
    carried = segc[...] == segr[:, 0:1]

    def outside(g, _):
        state = entering[g]
        high, low = two_parts(wide_state(state[:HEAD]))
        sums = jnp.broadcast_to(jnp.transpose(state[HEAD:, :])[:, 0:1], (LANES, LANES))
        sum_high, sum_low = two_parts(jnp.where(same_head(), sums, 0.0))
        query = fq[g]
        query = jnp.where(carried, query, jnp.zeros_like(query))
        num = num_s[g] + (nn(query, high) + nn(query, low))
        den = den_s[g] + (nn(query, sum_high) + nn(query, sum_low))
        inverse = 1.0 / den
        rden[g] = inverse
        mixed[g] = num * inverse
        return 0

    lax.fori_loop(0, nt_, outside, 0)
    gb.core_step()
    ga.finish()
    gb.finish()
    ex.finish()


def forward_call(nd, nt_, tokens, mine_a, mine_b, segc, segr, firsts, lasts, gain, shift):
    rows = tokens.shape[0]
    ra, ca = mine_a.shape
    rb, cb = mine_b.shape
    inner = nd // OUTER
    vm = pl.BlockSpec(memory_space=pltpu.VMEM)
    group = (nt_, rows, LANES)
    outs = [
        jax.ShapeDtypeStruct((nt_, OUTER, inner, ra, ca), BF16),
        jax.ShapeDtypeStruct((nt_, OUTER, inner, rb, cb), BF16),
        jax.ShapeDtypeStruct(tokens.shape, BF16),
        jax.ShapeDtypeStruct(group, BF16),
        jax.ShapeDtypeStruct(group, BF16),
        jax.ShapeDtypeStruct(group, BF16),
        jax.ShapeDtypeStruct(group, F32),
        jax.ShapeDtypeStruct(group, F32),
        jax.ShapeDtypeStruct((nt_, STATE_ROWS, LANES), F32),
    ]
    return pl.pallas_call(
        functools.partial(kernel_forward, nd, nt_),
        out_shape=outs,
        in_specs=[vm] * 9,
        out_specs=[vm] * len(outs),
        scratch_shapes=[
            pltpu.VMEM((rows, rows), BF16),
            pltpu.VMEM(group, F32),
            pltpu.VMEM(group, F32),
        ]
        + Exchange.scratch(nd, nt_)
        + Gather.semaphores(nd, nt_)
        + Gather.semaphores(nd, nt_)
        + Exchange.semaphores(nd, nt_),
        compiler_params=pltpu.CompilerParams(
            collective_id=0, has_side_effects=True, vmem_limit_bytes=VMEM_LIMIT
        ),
        name="attention_forward",
    )(tokens, mine_a, mine_b, segc, segr, firsts, lasts, gain, shift)
def pad_lanes(block):
    spare = LANES - block.shape[1]
    return jnp.pad(block, ((0, 0), (0, spare))) if spare > 0 else block


def prepare(nd, nt_, tokens, segment_ids, wq, wk, wv, wo, w1, w2):
    rows = tokens.shape[0]
    t = lax.axis_index("tensor")
    mine_a = jnp.concatenate([pad_lanes(w.astype(BF16)) for w in (wq, wk, wv)], axis=1)
    mine_b = jnp.concatenate(
        [pad_lanes(wo.astype(BF16).T), w1.astype(BF16), w2.astype(BF16).T], axis=1
    )
    by_member = segment_ids.reshape(nt_, rows)
    own = lax.dynamic_slice(segment_ids, (t * rows,), (rows,))
    segc, segr = own.reshape(rows, 1), own.reshape(1, rows)
    firsts = jnp.broadcast_to(by_member[:, :1].astype(F32), (nt_, LANES))
    lasts = jnp.broadcast_to(by_member[:, -1:].astype(F32), (nt_, LANES))
    return mine_a, mine_b, segc, segr, firsts, lasts
def kernel_hidden(
    nd, nt_,
    tokens, mixed, held, cotangent, gain, shift, mixer_bias, outer_bias, inner_bias,
    out, dr, do, part, sums, inner_sums,
    res, unit, inv, h2, h2t, cot, dh2, act, dhid, dbt,
):
    rows_all, width = tokens.shape
    hidden = (held.shape[-1] - LANES) // 2
    step = 128

    def weights(g, start, size):
        return held[g, :, :, :, start : start + size].reshape(width, size)

    def enter(k, _):
        at = pl.ds(pl.multiple_of(k * step, step), step)
        r = tokens[at, :].astype(F32) + mixer_bias[...]
        for g in range(nt_):
            r = r + nt(mixed[g, at, :].astype(BF16), weights(g, 0, LANES))
        center = r - jnp.mean(r, axis=-1, keepdims=True)
        spread = jnp.mean(center * center, axis=-1, keepdims=True)
        scale = lax.rsqrt(spread + EPSILON)
        n = center * scale
        y = n * gain[...] + shift[...]
        res[at, :] = r + outer_bias[...]
        unit[at, :] = n
        inv[at, :] = scale
        h2[at, :] = y.astype(BF16)
        h2t[:, at] = jnp.transpose(y).astype(BF16)
        e = cotangent[at, :].astype(F32)
        cot[:, at] = jnp.transpose(e).astype(BF16)
        dh2[at, :] = jnp.zeros((step, width), F32)
        return 0

    lax.fori_loop(0, rows_all // step, enter, 0)
    block = min(256, rows_all)

    def feed(g, _):
        w1 = weights(g, LANES, hidden)
        w2t = weights(g, LANES + hidden, hidden)
        total = jnp.zeros((1, hidden), F32)
        for start in range(0, rows_all, block):
            end = start + block
            u = nn(h2[start:end, :], w1) + inner_bias[pl.ds(g, 1), :]
            below = 0.5 * (1.0 + lax.erf(u * 0.7071067811865476))
            slope = below + u * (jnp.exp(-0.5 * (u * u)) * 0.3989422804014327)
            a = (u * below).astype(BF16)
            du = (nn(cotangent[start:end, :], w2t) * slope).astype(BF16)
            act[start:end, :] = a
            dhid[start:end, :] = du
            total = total + jnp.sum(du.astype(F32), axis=0, keepdims=True)
            res[start:end, :] += nt(a, w2t)
            dh2[start:end, :] += nt(du, w1)
        inner_sums[pl.ds(g, 1), :] = total
        for o in range(OUTER):
            tall = width // OUTER
            lo, hi = o * tall, (o + 1) * tall
            shape = (held.shape[2], held.shape[3], hidden)
            part[g, o, :, :, LANES : LANES + hidden] = (
                nn(h2t[lo:hi, :], dhid[...]).astype(BF16).reshape(shape)
            )
            part[g, o, :, :, LANES + hidden :] = (
                nn(cot[lo:hi, :], act[...]).astype(BF16).reshape(shape)
            )
        return 0

    lax.fori_loop(0, nt_, feed, 0)
    sums[...] = jnp.zeros_like(sums)

    def leave(k, _):
        at = pl.ds(pl.multiple_of(k * step, step), step)
        out[at, :] = res[at, :].astype(BF16)
        n = unit[at, :]
        grad = dh2[at, :]
        e = cotangent[at, :].astype(F32)
        pushed = grad * gain[...]
        mean = jnp.mean(pushed, axis=-1, keepdims=True)
        along = jnp.mean(pushed * n, axis=-1, keepdims=True)
        back = e + (pushed - mean - n * along) * inv[at, :]
        dr[at, :] = back
        low = back.astype(BF16)
        wide = low.astype(F32)
        dbt[:, at] = jnp.transpose(wide).astype(BF16)
        for g in range(nt_):
            do[g, at, :] = nn(low, weights(g, 0, LANES))
        sums[2:3, :] += jnp.sum(grad * n, axis=0, keepdims=True)
        sums[3:4, :] += jnp.sum(grad, axis=0, keepdims=True)
        sums[4:5, :] += jnp.sum(wide, axis=0, keepdims=True)
        sums[5:6, :] += jnp.sum(e, axis=0, keepdims=True)
        return 0

    lax.fori_loop(0, rows_all // step, leave, 0)
    for g in range(nt_):
        shape = held.shape[1:4] + (LANES,)
        part[g, :, :, :, :LANES] = (
            nn(dbt[...], mixed[g].astype(BF16)).astype(BF16).reshape(shape)
        )


def hidden_call(nd, nt_, tokens, mixed, held, cotangent, gain, shift, mbias, obias, ibias):
    rows, width = tokens.shape
    hidden = (held.shape[-1] - LANES) // 2
    vm = pl.BlockSpec(memory_space=pltpu.VMEM)
    outs = [
        jax.ShapeDtypeStruct((rows, width), BF16),
        jax.ShapeDtypeStruct((rows, width), F32),
        jax.ShapeDtypeStruct(mixed.shape, F32),
        jax.ShapeDtypeStruct(held.shape, BF16),
        jax.ShapeDtypeStruct((8, width), F32),
        jax.ShapeDtypeStruct((nt_, hidden), F32),
    ]
    return pl.pallas_call(
        functools.partial(kernel_hidden, nd, nt_),
        out_shape=outs,
        in_specs=[vm] * 9,
        out_specs=[vm] * len(outs),
        scratch_shapes=[
            pltpu.VMEM((rows, width), F32),
            pltpu.VMEM((rows, width), F32),
            pltpu.VMEM((rows, 1), F32),
            pltpu.VMEM((rows, width), BF16),
            pltpu.VMEM((width, rows), BF16),
            pltpu.VMEM((width, rows), BF16),
            pltpu.VMEM((rows, width), F32),
            pltpu.VMEM((rows, hidden), BF16),
            pltpu.VMEM((rows, hidden), BF16),
            pltpu.VMEM((width, rows), BF16),
        ],
        compiler_params=pltpu.CompilerParams(vmem_limit_bytes=VMEM_LIMIT),
        name="hidden_layer",
    )(tokens, mixed, held, cotangent, gain, shift, mbias, obias, ibias)
class Scatter:
    def __init__(self, place, part, core, plane, own, outer, sems):
        self.p, self.part, self.core = place, part, core
        self.plane, self.own, self.outer = plane, own, outer
        self.send, self.got_core, self.got_plane, self.got_outer = sems
        self.started, self.count = [], 0

    def _go(self, src, dst, recv, peer):
        copy = remote(src, dst, self.send.at[self.count], recv, peer)
        self.count += 1
        copy.start()
        self.started.append(copy)

    def core_send(self, y):
        p = self.p
        self._go(self.part.at[y * 2 + 1 - p.c], self.core.at[y], self.got_core.at[y], p.at(dc=1))

    def core_sum(self, y):
        p = self.p
        block = self.core.at[y]
        remote(block, block, self.send.at[0], self.got_core.at[y], p.at()).wait_recv()

        def add(k, _):
            o, i = k // p.inner, k % p.inner
            mine = self.part[y * 2 + p.c, o, i].astype(F32)
            self.core[y, o, i] = (mine + self.core[y, o, i].astype(F32)).astype(BF16)
            return 0

        lax.fori_loop(0, OUTER * p.inner, add, 0)

    def plane_send(self):
        p = self.p
        for j, (_, di, dy, _) in enumerate(p.plane_peers()):
            i, y = (p.i + di) % p.inner, (p.y + dy) % p.ny
            self._go(
                self.core.at[y, :, i], self.plane.at[j], self.got_plane.at[j], p.at(0, di, dy, 0)
            )

    def plane_sum(self):
        p = self.p
        peers = len(p.plane_peers())
        for j in range(peers):
            block = self.plane.at[j]
            remote(block, block, self.send.at[0], self.got_plane.at[j], p.at()).wait_recv()
        for k in range(OUTER):
            o = (p.o + k) % OUTER
            total = self.core[p.y, o, p.i].astype(F32)
            for j in range(peers):
                total = total + self.plane[j, o].astype(F32)
            self.own[k] = total.astype(BF16)
            if k:
                self._go(
                    self.own.at[k], self.outer.at[k - 1], self.got_outer.at[k - 1], p.at(do=k)
                )

    def outer_sum(self, out):
        p = self.p
        total = self.own[0].astype(F32)
        for k in range(1, OUTER):
            block = self.outer.at[k - 1]
            remote(block, block, self.send.at[0], self.got_outer.at[k - 1], p.at()).wait_recv()
            total = total + self.outer[k - 1].astype(F32)
        out[...] = total

    def finish(self):
        for copy in self.started:
            copy.wait_send()

    @staticmethod
    def scratch(nd, nt_, rows, columns):
        inner, ny = nd // OUTER, nt_ // 2
        peers = inner * ny - 1
        return [
            pltpu.VMEM((ny, OUTER, inner, rows, columns), BF16),
            pltpu.VMEM((peers, OUTER, rows, columns), BF16),
            pltpu.VMEM((OUTER, rows, columns), BF16),
            pltpu.VMEM((OUTER - 1, rows, columns), BF16),
        ]

    @staticmethod
    def semaphores(nd, nt_):
        inner, ny = nd // OUTER, nt_ // 2
        peers = inner * ny - 1
        return [
            pltpu.SemaphoreType.DMA((ny + peers + OUTER - 1,)),
            pltpu.SemaphoreType.DMA((ny,)),
            pltpu.SemaphoreType.DMA((peers,)),
            pltpu.SemaphoreType.DMA((OUTER - 1,)),
        ]


class Total:
    def __init__(self, place, core, plane, outer, sems):
        self.p, self.core, self.plane, self.outer = place, core, plane, outer
        self.send, self.got_core, self.got_plane, self.got_outer = sems
        self.started, self.count = [], 0

    def _go(self, src, dst, recv, peer):
        copy = remote(src, dst, self.send.at[self.count], recv, peer)
        self.count += 1
        copy.start()
        self.started.append(copy)

    def start(self, value):
        self.core[0] = value
        self._go(self.core.at[0], self.core.at[1], self.got_core.at[0], self.p.at(dc=1))

    def plane_step(self):
        p = self.p
        block = self.core.at[1]
        remote(block, block, self.send.at[0], self.got_core.at[0], p.at()).wait_recv()
        here = p.i * p.ny + p.y
        self.plane[here] = self.core[0] + self.core[1]
        for peer in p.plane_peers():
            self._go(
                self.plane.at[here], self.plane.at[here], self.got_plane.at[here], p.at(*peer)
            )

    def outer_step(self):
        p = self.p
        for _, di, dy, _ in p.plane_peers():
            i, y = (p.i + p.inner - di) % p.inner, (p.y + p.ny - dy) % p.ny
            block = self.plane.at[i * p.ny + y]
            sem = self.got_plane.at[i * p.ny + y]
            remote(block, block, self.send.at[0], sem, p.at()).wait_recv()
        total = self.plane[0]
        for k in range(1, p.inner * p.ny):
            total = total + self.plane[k]
        self.outer[p.o] = total
        for peer in p.outer_peers():
            self._go(
                self.outer.at[p.o], self.outer.at[p.o], self.got_outer.at[p.o], p.at(*peer)
            )

    def result(self):
        p = self.p
        for k in range(1, OUTER):
            o = (p.o + OUTER - k) % OUTER
            block = self.outer.at[o]
            remote(block, block, self.send.at[0], self.got_outer.at[o], p.at()).wait_recv()
        total = self.outer[0]
        for k in range(1, OUTER):
            total = total + self.outer[k]
        return total

    def finish(self):
        for copy in self.started:
            copy.wait_send()

    @staticmethod
    def scratch(nd, nt_, shape):
        inner, ny = nd // OUTER, nt_ // 2
        return [
            pltpu.VMEM((2,) + shape, F32),
            pltpu.VMEM((inner * ny,) + shape, F32),
            pltpu.VMEM((OUTER,) + shape, F32),
        ]

    @staticmethod
    def semaphores(nd, nt_):
        inner, ny = nd // OUTER, nt_ // 2
        return [
            pltpu.SemaphoreType.DMA((1 + inner * ny - 1 + OUTER - 1,)),
            pltpu.SemaphoreType.DMA((1,)),
            pltpu.SemaphoreType.DMA((inner * ny,)),
            pltpu.SemaphoreType.DMA((OUTER,)),
        ]


def kernel_backward(
    nd, nt_,
    tokens, held_a, part_b, normed, fq, fk, vb, mixed, rden, do, dr, entering,
    segc, segr, firsts, lasts, gain, sums, inner_sums,
    grad_a, grad_b, grad_tokens, first_total, all_total, inner_total,
    mask, part_a, gn, gd, dk_s, dv_s, dq_s, normed_t, dh1,
    own, near, far, made, leaving,
    *more,
):
    p = Place(nd, nt_)
    rows_all, width = tokens.shape
    sa, sb, more = more[0:4], more[4:8], more[8:]
    t1, t2, t3, more = more[0:3], more[3:6], more[6:9], more[9:]
    ex = Exchange(p, firsts, lasts, True, own, near, far, made, leaving, more[0:4])
    ra = Scatter(p, part_a, *sa, more[4:8])
    rb = Scatter(p, part_b, *sb, more[8:12])
    all_sum = Total(p, *t1, more[12:16])
    inner_sum = Total(p, *t2, more[16:20])
    first_sum = Total(p, *t3, more[20:24])
    p.greet()
    for y in range(p.ny):
        rb.core_send(y)
    all_sum.start(sums[...])
    inner_sum.start(inner_sums[...])
    opening = segc[...] == segr[:, 0:1]

    def first(g, _):
        low = (do[g] * rden[g]).astype(BF16)
        gn[g] = low
        product = low.astype(F32) * mixed[g]
        left = left_lanes(product.shape)
        zero = jnp.zeros_like(product)
        one = jnp.sum(jnp.where(left, product, zero), axis=-1, keepdims=True)
        two = jnp.sum(jnp.where(left, zero, product), axis=-1, keepdims=True)
        slope = -jnp.where(left, one, two)
        gd[g] = slope
        kept = jnp.where(opening, fq[g], jnp.zeros_like(low))
        own[g, :HEAD, :] = pack_state(tn(kept, low))
        total = jnp.sum(kept.astype(F32) * slope, axis=0, keepdims=True)
        own[g, HEAD:, :] = jnp.broadcast_to(total, (STATE_ROWS - HEAD, LANES))
        return 0

    lax.fori_loop(0, nt_, first, 0)
    ex.step_near()
    make_mask(segc, segr, mask, 128)
    for start in range(0, rows_all, 128):
        normed_t[:, start : start + 128] = jnp.transpose(
            normed[start : start + 128, :].astype(F32)
        ).astype(BF16)
    for y in range(p.ny):
        rb.core_sum(y)
    rb.plane_send()
    all_sum.plane_step()
    inner_sum.plane_step()
    ex.step_far()
    block = min(256, rows_all)

    def inside(g, _):
        values, keys = vb[g], fk[g]
        key_heads = split_heads(keys, 0.0)
        state = entering[g]
        high, low = two_parts(wide_state(state[:HEAD]))
        query_t = jnp.transpose(fq[g].astype(F32)).astype(BF16)
        grad_t = jnp.transpose(gn[g].astype(F32)).astype(BF16)
        dk_t = jnp.zeros((LANES, rows_all), F32)
        dv_t = jnp.zeros((LANES, rows_all), F32)
        for start in range(0, rows_all, block):
            end = start + block
            now = mask[start:end, :end]
            query, grad = fq[g, start:end, :], gn[g, start:end, :]
            slope = gd[g, start:end, :]
            query_heads, grad_heads = split_heads(query, 0.0), split_heads(grad, 0.0)
            carried = segc[start:end, :] == segr[:, 0:1]
            dq = jnp.where(
                carried,
                nt(grad, high) + nt(grad, low) + slope * state[HEAD : HEAD + 1, :],
                0.0,
            )
            dk_parts, dv_parts = [], []
            for h in range(2):
                lanes = slice(h * HEAD, h * HEAD + 1)
                rows = slice(h * HEAD, (h + 1) * HEAD)
                weight = nt(query_heads[h], keys[:end]).astype(BF16) * now
                share = (nt(grad_heads[h], values[:end]) + slope[:, lanes]).astype(BF16) * now
                dq = dq + nn(share, key_heads[h][:end])
                dk_parts.append(nn(query_t[rows, start:end], share))
                dv_parts.append(nn(grad_t[rows, start:end], weight))
            dk_now = jnp.concatenate(dk_parts, axis=0)
            dv_now = jnp.concatenate(dv_parts, axis=0)
            if end < rows_all:
                pad = jnp.zeros((LANES, rows_all - end), F32)
                dk_now = jnp.concatenate([dk_now, pad], axis=1)
                dv_now = jnp.concatenate([dv_now, pad], axis=1)
            dk_t, dv_t = dk_t + dk_now, dv_t + dv_now
            dq_s[g, start:end, :] = (
                dq * jnp.minimum(query.astype(F32), 1.0)
            ).astype(BF16)
        dk_s[g] = jnp.transpose(dk_t)
        dv_s[g] = jnp.transpose(dv_t)
        return 0

    lax.fori_loop(0, nt_ // 2, inside, 0)
    ex.step_enter()
    lax.fori_loop(nt_ // 2, nt_, inside, 0)
    rb.plane_sum()
    all_sum.outer_step()
    inner_sum.outer_step()
    ex.arrive()
    closing = segc[...] == segr[:, rows_all - 1 : rows_all]
    dh1[...] = jnp.zeros_like(dh1)

    def outside(g, _):
        state = leaving[g]
        high, low = two_parts(wide_state(state[:HEAD]))
        keys, values = fk[g], vb[g]
        dk = nt(values, high) + nt(values, low) + state[HEAD : HEAD + 1, :]
        dv = nn(keys, high) + nn(keys, low)
        dk = dk_s[g] + jnp.where(closing, dk, 0.0)
        dv = dv_s[g] + jnp.where(closing, dv, 0.0)
        dk = dk * jnp.minimum(keys.astype(F32), 1.0)
        joint = jnp.concatenate([dq_s[g], dk.astype(BF16), dv.astype(BF16)], axis=1)
        w = held_a[g].reshape(width, 3 * LANES)
        part_a[g] = nn(normed_t[...], joint).astype(BF16).reshape(part_a.shape[1:])
        dh1[...] += nt(joint, w)
        return 0

    lax.fori_loop(0, nt_, outside, 0)
    for y in range(p.ny):
        ra.core_send(y)
    first_total[...] = jnp.zeros_like(first_total)
    step = 128

    def leave(k, _):
        at = pl.ds(pl.multiple_of(k * step, step), step)
        x = tokens[at, :].astype(F32)
        center = x - jnp.mean(x, axis=-1, keepdims=True)
        spread = jnp.mean(center * center, axis=-1, keepdims=True)
        scale = lax.rsqrt(spread + EPSILON)
        n = center * scale
        grad = dh1[at, :]
        pushed = grad * gain[...]
        mean = jnp.mean(pushed, axis=-1, keepdims=True)
        along = jnp.mean(pushed * n, axis=-1, keepdims=True)
        back = (pushed - mean - n * along) * scale
        grad_tokens[at, :] = (dr[at, :] + back).astype(BF16)
        first_total[0:1, :] += jnp.sum(grad * n, axis=0, keepdims=True)
        first_total[1:2, :] += jnp.sum(grad, axis=0, keepdims=True)
        return 0

    lax.fori_loop(0, rows_all // step, leave, 0)
    first_sum.start(first_total[...])
    for y in range(p.ny):
        ra.core_sum(y)
    ra.plane_send()
    first_sum.plane_step()
    rb.outer_sum(grad_b)
    all_total[...] = all_sum.result()
    inner_total[...] = inner_sum.result()
    ra.plane_sum()
    first_sum.outer_step()
    ra.outer_sum(grad_a)
    first_total[...] = first_sum.result()
    for each in (ra, rb, all_sum, inner_sum, first_sum, ex):
        each.finish()


def backward_call(nd, nt_, *args):
    tokens, held_a, part_b = args[:3]
    inner_sums = args[-1]
    rows, width = tokens.shape
    ra, ca = held_a.shape[-2:]
    rb, cb = part_b.shape[-2:]
    vm = pl.BlockSpec(memory_space=pltpu.VMEM)
    group = (nt_, rows, LANES)
    outs = [
        jax.ShapeDtypeStruct((ra, ca), F32),
        jax.ShapeDtypeStruct((rb, cb), F32),
        jax.ShapeDtypeStruct((rows, width), BF16),
        jax.ShapeDtypeStruct((8, width), F32),
        jax.ShapeDtypeStruct((8, width), F32),
        jax.ShapeDtypeStruct(inner_sums.shape, F32),
    ]
    return pl.pallas_call(
        functools.partial(kernel_backward, nd, nt_),
        out_shape=outs,
        in_specs=[vm] * len(args),
        out_specs=[vm] * len(outs),
        scratch_shapes=[
            pltpu.VMEM((rows, rows), BF16),
            pltpu.VMEM(held_a.shape, BF16),
            pltpu.VMEM(group, BF16),
            pltpu.VMEM(group, F32),
            pltpu.VMEM(group, F32),
            pltpu.VMEM(group, F32),
            pltpu.VMEM(group, BF16),
            pltpu.VMEM((width, rows), BF16),
            pltpu.VMEM((rows, width), F32),
        ]
        + Exchange.scratch(nd, nt_)
        + [pltpu.VMEM((nt_, STATE_ROWS, LANES), F32)]
        + Scatter.scratch(nd, nt_, ra, ca)
        + Scatter.scratch(nd, nt_, rb, cb)
        + Total.scratch(nd, nt_, (8, width))
        + Total.scratch(nd, nt_, inner_sums.shape)
        + Total.scratch(nd, nt_, (8, width))
        + Exchange.semaphores(nd, nt_)
        + Scatter.semaphores(nd, nt_)
        + Scatter.semaphores(nd, nt_)
        + Total.semaphores(nd, nt_)
        + Total.semaphores(nd, nt_)
        + Total.semaphores(nd, nt_),
        compiler_params=pltpu.CompilerParams(
            collective_id=1, has_side_effects=True, vmem_limit_bytes=VMEM_LIMIT
        ),
        name="attention_backward",
    )(*args)
def local(
    nd, nt_,
    tokens, segment_ids, query_weight, key_weight, value_weight, output_weight,
    inner_weight, outer_weight, inner_bias, first_gain, first_shift,
    second_gain, second_shift, mixer_bias, outer_bias, grad_out,
):
    mine_a, mine_b, segc, segr, firsts, lasts = prepare(
        nd, nt_, tokens, segment_ids, query_weight, key_weight, value_weight,
        output_weight, inner_weight, outer_weight,
    )
    held_a, held_b, normed, fq, fk, vb, mixed, rden, entering = forward_call(
        nd, nt_, tokens, mine_a, mine_b, segc, segr, firsts, lasts,
        first_gain[None], first_shift[None],
    )
    hidden = inner_weight.shape[1]
    layer_out, dr, do, part_b, sums, inner_sums = hidden_call(
        nd, nt_, tokens, mixed, held_b, grad_out, second_gain[None], second_shift[None],
        mixer_bias[None], outer_bias[None], inner_bias.reshape(nt_, hidden),
    )
    grad_a, grad_b, grad_tokens, first_total, all_total, inner_total = backward_call(
        nd, nt_, tokens, held_a, part_b, normed, fq, fk, vb, mixed, rden, do, dr, entering,
        segc, segr, firsts, lasts, first_gain[None], sums, inner_sums,
    )
    head = query_weight.shape[1]
    return (
        layer_out,
        grad_tokens,
        grad_a[:, :head],
        grad_a[:, LANES : LANES + head],
        grad_a[:, 2 * LANES : 2 * LANES + head],
        grad_b[:, :head].T,
        grad_b[:, LANES : LANES + hidden],
        grad_b[:, LANES + hidden :].T,
        inner_total.reshape(inner_bias.shape),
        first_total[0],
        first_total[1],
        all_total[2],
        all_total[3],
        all_total[4],
        all_total[5],
    )


def solution(mesh):
    rows = P(("dp", "tensor"), None)
    one, two, all_of = P("dp", "tensor"), P("tensor", "dp"), P()
    weights = (one, one, one, two, one, two)
    return jax.shard_map(
        functools.partial(local, mesh.shape["dp"], mesh.shape["tensor"]),
        mesh=mesh,
        in_specs=(rows, P("dp")) + weights + (all_of,) * 7 + (rows,),
        out_specs=(rows, rows) + weights + (all_of,) * 7,
        check_vma=False,
    )
```

```python
import functools

import jax
import jax.numpy as jnp
from jax import lax
from jax.experimental import pallas as pl
from jax.experimental.pallas import tpu as pltpu
from jax.sharding import PartitionSpec as P

HEAD = 64
LANES = 128
EPSILON = 1e-05
MESH = pl.DeviceIdType.MESH
F32 = jnp.float32
BF16 = jnp.bfloat16
OUTER = 4
STATE_ROWS = HEAD + 8
VMEM_LIMIT = 56 << 20


def nn(a, b):
    return lax.dot_general(a, b, (((1,), (0,)), ((), ())), preferred_element_type=F32)


def nt(a, b):
    return lax.dot_general(a, b, (((1,), (1,)), ((), ())), preferred_element_type=F32)


def tn(a, b):
    return lax.dot_general(a, b, (((0,), (0,)), ((), ())), preferred_element_type=F32)


class Place:
    def __init__(self, dp_size, tensor_size):
        self.nd, self.nt = dp_size, tensor_size
        self.inner, self.ny = dp_size // OUTER, tensor_size // 2
        self.d, self.t = lax.axis_index("dp"), lax.axis_index("tensor")
        self.o, self.i = self.d // self.inner, self.d % self.inner
        self.y, self.c = self.t // 2, self.t % 2
        self.barrier = pltpu.get_barrier_semaphore()

    def at(self, do=0, di=0, dy=0, dc=0):
        o, i = (self.o + do) % OUTER, (self.i + di) % self.inner
        return self.to(o, i, (self.y + dy) % self.ny, (self.c + dc) % 2)

    def to(self, o, i, y, c):
        return (o * self.inner + i, y * 2 + c)

    def nearest(self, k):
        if k == 0:
            return self.o
        high = self.o // 2
        edge = self.o + high * (3 - 2 * self.o)
        place = k * (1 - edge) + (k // 2) * k * edge
        return place + high * (3 - 2 * place)

    def outer_peers(self):
        return [(k, 0, 0, 0) for k in range(1, OUTER)]

    def plane_peers(self):
        return [
            (0, di, dy, 0) for di in range(self.inner) for dy in range(self.ny) if di or dy
        ]

    def group_peers(self):
        return [(0, 0, dy, dc) for dy in range(self.ny) for dc in range(2) if dy or dc]

    def dp_peers(self):
        return [(do, di, 0, 0) for do in range(OUTER) for di in range(self.inner) if do or di]

    def peers(self):
        found = []
        for peer in (
            self.outer_peers() + self.plane_peers() + self.group_peers() + self.dp_peers()
        ):
            if peer not in found:
                found.append(peer)
        return found

    def greet(self):
        for peer in self.peers():
            pl.semaphore_signal(
                self.barrier, inc=1, device_id=self.at(*peer), device_id_type=MESH
            )

    def meet(self):
        pl.semaphore_wait(self.barrier, len(self.peers()))


def remote(src, dst, send, recv, peer):
    return pltpu.make_async_remote_copy(
        src_ref=src,
        dst_ref=dst,
        send_sem=send,
        recv_sem=recv,
        device_id=peer,
        device_id_type=MESH,
    )


class Sender:
    def __init__(self, place, send):
        self.p, self.send, self.started = place, send, []

    def go(self, src, dst, recv, peer):
        copy = remote(src, dst, self.send.at[len(self.started)], recv, peer)
        copy.start()
        self.started.append(copy)

    def got(self, block, recv):
        remote(block, block, self.send.at[0], recv, self.p.at()).wait_recv()

    def finish(self):
        for copy in self.started:
            copy.wait_send()


class Gather(Sender):
    def __init__(self, place, held, sems):
        super().__init__(place, sems[0])
        self.held = held
        self.got_outer, self.got_i, self.got_y, self.got_d, self.got_core = sems[1:]

    def _block(self, k, i, y):
        p = self.p
        return self.held.at[y * 2 + p.c, p.nearest(k), i]

    def outer_start(self):
        p = self.p
        mine = self._block(0, p.i, p.y)
        for k in range(1, OUTER):
            to = p.to(p.nearest(k), p.i, p.y, p.c)
            self.go(mine, mine, self.got_outer.at[p.o], to)

    def spread(self, k):
        p = self.p
        block = self._block(k, p.i, p.y)
        if k:
            self.got(block, self.got_outer.at[p.nearest(k)])
        for di in range(1, p.inner):
            self.go(block, block, self.got_i.at[di - 1, k], p.at(di=di))
        for dy in range(1, p.ny):
            self.go(block, block, self.got_y.at[dy - 1, k], p.at(dy=dy))
        self.go(block, block, self.got_core.at[p.y], p.at(dc=1))

    def turn(self, k):
        p = self.p
        for di in range(1, p.inner):
            block = self._block(k, (p.i + p.inner - di) % p.inner, p.y)
            self.got(block, self.got_i.at[di - 1, k])
            if k < 2:
                for dy in range(1, p.ny):
                    self.go(block, block, self.got_d.at[di - 1, dy - 1, k], p.at(dy=dy))
            self.go(block, block, self.got_core.at[p.y], p.at(dc=1))
        for dy in range(1, p.ny):
            y = (p.y + p.ny - dy) % p.ny
            block = self._block(k, p.i, y)
            self.got(block, self.got_y.at[dy - 1, k])
            if k >= 2:
                for di in range(1, p.inner):
                    self.go(block, block, self.got_d.at[di - 1, dy - 1, k], p.at(di=di))
            self.go(block, block, self.got_core.at[y], p.at(dc=1))

    def corner(self, k):
        p = self.p
        for di in range(1, p.inner):
            for dy in range(1, p.ny):
                y = (p.y + p.ny - dy) % p.ny
                block = self._block(k, (p.i + p.inner - di) % p.inner, y)
                self.got(block, self.got_d.at[di - 1, dy - 1, k])
                self.go(block, block, self.got_core.at[y], p.at(dc=1))

    def core_done(self):
        p = self.p
        for y in range(p.ny):
            self.got(self.held.at[y * 2 + 1 - p.c], self.got_core.at[y])

    @staticmethod
    def semaphores(nd, nt_):
        di, dy = nd // OUTER - 1, nt_ // 2 - 1
        sends = (OUTER - 1) + OUTER * (di + dy + 1 + di + dy) + 2 * OUTER * di * dy
        return [
            pltpu.SemaphoreType.DMA((sends,)),
            pltpu.SemaphoreType.DMA((OUTER,)),
            pltpu.SemaphoreType.DMA((di, OUTER)),
            pltpu.SemaphoreType.DMA((dy, OUTER)),
            pltpu.SemaphoreType.DMA((di, dy, OUTER)),
            pltpu.SemaphoreType.DMA((nt_ // 2,)),
        ]


class Scatter(Sender):
    def __init__(self, place, bufs, sems):
        super().__init__(place, sems[0])
        (self.give, self.core, self.in_i, self.in_y, self.sum_i, self.sum_y,
         self.then_y, self.then_i, self.own, self.outer) = bufs
        self.got_core, self.got_i, self.got_y, self.got_ty, self.got_ti, self.got_outer = sems[1:]

    def core_send(self, y):
        self.go(self.give.at[y], self.core.at[y], self.got_core.at[y], self.p.at(dc=1))

    def core_wait(self, y):
        self.got(self.core.at[y], self.got_core.at[y])

    def first(self, dy):
        p = self.p
        y = (p.y + dy) % p.ny
        if dy:
            for k in range(2, OUTER):
                o = (p.o + k) % OUTER
                self.go(
                    self.core.at[y, o], self.in_y.at[dy - 1, k - 2],
                    self.got_y.at[dy - 1, k - 2], p.at(dy=dy),
                )
        for k in range(2):
            o = (p.o + k) % OUTER
            for di in range(1, p.inner):
                i = (p.i + di) % p.inner
                self.go(
                    self.core.at[y, o, i], self.in_i.at[di - 1, k, dy],
                    self.got_i.at[di - 1, k, dy], p.at(di=di),
                )

    def second_y(self):
        p = self.p
        for k in range(2, OUTER):
            o = (p.o + k) % OUTER
            for dy in range(1, p.ny):
                self.got(self.in_y.at[dy - 1, k - 2], self.got_y.at[dy - 1, k - 2])
            for di in list(range(1, p.inner)) + [0]:
                i = (p.i + di) % p.inner
                total = self.core[p.y, o, i].astype(F32)
                for dy in range(1, p.ny):
                    total = total + self.in_y[dy - 1, k - 2, i].astype(F32)
                self.sum_y[k - 2, di] = total.astype(BF16)
                if di:
                    self.go(
                        self.sum_y.at[k - 2, di], self.then_i.at[di - 1, k - 2],
                        self.got_ti.at[di - 1, k - 2], p.at(di=di),
                    )

    def second_i(self):
        p = self.p
        for dy in list(range(1, p.ny)) + [0]:
            y = (p.y + dy) % p.ny
            for k in range(2):
                o = (p.o + k) % OUTER
                total = self.core[y, o, p.i].astype(F32)
                for di in range(1, p.inner):
                    self.got(self.in_i.at[di - 1, k, dy], self.got_i.at[di - 1, k, dy])
                    total = total + self.in_i[di - 1, k, dy].astype(F32)
                self.sum_i[k, dy] = total.astype(BF16)
                if dy:
                    self.go(
                        self.sum_i.at[k, dy], self.then_y.at[dy - 1, k],
                        self.got_ty.at[dy - 1, k], p.at(dy=dy),
                    )

    def third(self):
        p = self.p
        for k in (2, 3, 1, 0):
            if k < 2:
                total = self.sum_i[k, 0].astype(F32)
                for dy in range(1, p.ny):
                    self.got(self.then_y.at[dy - 1, k], self.got_ty.at[dy - 1, k])
                    total = total + self.then_y[dy - 1, k].astype(F32)
            else:
                total = self.sum_y[k - 2, 0].astype(F32)
                for di in range(1, p.inner):
                    self.got(self.then_i.at[di - 1, k - 2], self.got_ti.at[di - 1, k - 2])
                    total = total + self.then_i[di - 1, k - 2].astype(F32)
            self.own[k] = total.astype(BF16)
            if k:
                self.go(
                    self.own.at[k], self.outer.at[k - 1], self.got_outer.at[k - 1], p.at(do=k)
                )

    def last(self):
        total = self.own[0].astype(F32)
        for k in range(1, OUTER):
            self.got(self.outer.at[k - 1], self.got_outer.at[k - 1])
            total = total + self.outer[k - 1].astype(F32)
        return total

    @staticmethod
    def scratch(nd, nt_, rows, columns):
        inner, ny = nd // OUTER, nt_ // 2
        leads = [
            (ny, OUTER, inner), (ny, OUTER, inner), (inner - 1, 2, ny), (ny - 1, 2, inner),
            (2, ny), (2, inner), (ny - 1, 2), (inner - 1, 2), (OUTER,), (OUTER - 1,),
        ]
        return [pltpu.VMEM(lead + (rows, columns), BF16) for lead in leads]

    @staticmethod
    def semaphores(nd, nt_):
        inner, ny = nd // OUTER, nt_ // 2
        di, dy = inner - 1, ny - 1
        sends = ny + 2 * dy + 2 * di * ny + 2 * di + 2 * dy + OUTER - 1
        shapes = [(sends,), (ny,), (di, 2, ny), (dy, 2), (dy, 2), (di, 2), (OUTER - 1,)]
        return [pltpu.SemaphoreType.DMA(shape) for shape in shapes]


class Exchange:
    def __init__(self, place, firsts, lasts, back, own, near, far, made, entering, sems):
        self.p, self.back = place, back
        self.own, self.near, self.far = own, near, far
        self.made, self.entering = made, entering
        self.edge, self.inlet = (firsts, lasts) if back else (lasts, firsts)
        self.s_send, self.s_near, self.s_far, self.s_enter = sems
        self.started, self.count = [], 0

    def _go(self, src, dst, recv, peer):
        copy = remote(src, dst, self.s_send.at[self.count], recv, peer)
        self.count += 1
        copy.start()
        self.started.append(copy)

    def step_near(self):
        p = self.p
        for peer in p.group_peers():
            to = p.at(*peer)
            self._go(self.own.at[to[1]], self.near.at[p.t], self.s_near.at[p.t], to)
        self.near[p.t] = self.own[p.t]

    def step_far(self):
        p = self.p
        for _, _, dy, dc in p.group_peers():
            t = ((p.y + p.ny - dy) % p.ny) * 2 + (p.c + dc) % 2
            block = self.near.at[t]
            remote(block, block, self.s_send.at[0], self.s_near.at[t], p.at()).wait_recv()
        border = 0 if self.back else p.nt - 1
        ids = self.edge[border : border + 1, :]
        total = jnp.zeros((STATE_ROWS, LANES), F32)
        for j in range(p.nt):
            total = total + jnp.where(self.edge[j : j + 1, :] == ids, self.near[j], 0.0)
        rows = lax.broadcasted_iota(jnp.int32, (STATE_ROWS, LANES), 0)
        self.far[p.d] = jnp.where(rows > HEAD, jnp.broadcast_to(ids, rows.shape), total)
        for peer in p.dp_peers():
            self._go(self.far.at[p.d], self.far.at[p.d], self.s_far.at[p.d], p.at(*peer))

    def step_enter(self):
        p = self.p
        for do, di, _, _ in p.dp_peers():
            o, i = (p.o + OUTER - do) % OUTER, (p.i + p.inner - di) % p.inner
            d = o * p.inner + i
            block = self.far.at[d]
            remote(block, block, self.s_send.at[0], self.s_far.at[d], p.at()).wait_recv()
        for j in range(p.nt):
            inlet = self.inlet[j : j + 1, :]
            total = jnp.zeros((STATE_ROWS, LANES), F32)
            for d in range(p.nd):
                ids = self.far[d, HEAD + 1 : HEAD + 2, :]
                wanted = jnp.where(d > p.d if self.back else d < p.d, ids, -1.0)
                total = total + jnp.where(wanted == inlet, self.far[d], 0.0)
            for k in range(j + 1, p.nt) if self.back else range(j):
                total = total + jnp.where(self.edge[k : k + 1, :] == inlet, self.near[k], 0.0)
            self.made[j] = total
        for peer in p.group_peers():
            to = p.at(*peer)
            self._go(self.made.at[to[1]], self.entering.at[p.t], self.s_enter.at[p.t], to)
        self.entering[p.t] = self.made[p.t]

    def arrive(self):
        p = self.p
        for _, _, dy, dc in p.group_peers():
            t = ((p.y + p.ny - dy) % p.ny) * 2 + (p.c + dc) % 2
            block = self.entering.at[t]
            remote(block, block, self.s_send.at[0], self.s_enter.at[t], p.at()).wait_recv()

    def finish(self):
        for copy in self.started:
            copy.wait_send()

    @staticmethod
    def scratch(nd, nt):
        return [
            pltpu.VMEM((nt, STATE_ROWS, LANES), F32),
            pltpu.VMEM((nt, STATE_ROWS, LANES), F32),
            pltpu.VMEM((nd, STATE_ROWS, LANES), F32),
            pltpu.VMEM((nt, STATE_ROWS, LANES), F32),
        ]

    @staticmethod
    def semaphores(nd, nt):
        return [
            pltpu.SemaphoreType.DMA((2 * (nt - 1) + nd - 1,)),
            pltpu.SemaphoreType.DMA((nt,)),
            pltpu.SemaphoreType.DMA((nd,)),
            pltpu.SemaphoreType.DMA((nt,)),
        ]


def left_lanes(shape):
    return lax.broadcasted_iota(jnp.int32, shape, len(shape) - 1) < HEAD


def split_heads(block, fill):
    left = left_lanes(block.shape)
    other = jnp.full_like(block, fill)
    return jnp.where(left, block, other), jnp.where(left, other, block)


def feature(values):
    return jnp.where(values > 0.0, values + 1.0, jnp.exp(jnp.minimum(values, 0.0)))


def pack_state(product):
    left = left_lanes((HEAD, LANES))
    return jnp.where(left, product[:HEAD], product[HEAD:])


def wide_state(packed):
    left = left_lanes((HEAD, LANES))
    zero = jnp.zeros_like(packed)
    return jnp.concatenate([jnp.where(left, packed, zero), jnp.where(left, zero, packed)], axis=0)


def two_parts(values):
    high = values.astype(BF16)
    return high, (values - high.astype(F32)).astype(BF16)


def same_head():
    row = lax.broadcasted_iota(jnp.int32, (LANES, LANES), 0) < HEAD
    return row == left_lanes((LANES, LANES))


def make_mask(segc, segr, mask, rows):
    total = segc.shape[0]
    for start in range(0, total, rows):
        at = lax.broadcasted_iota(jnp.int32, (rows, total), 0) + start
        key = lax.broadcasted_iota(jnp.int32, (rows, total), 1)
        same = segc[start : start + rows, :] == segr[...]
        mask[start : start + rows, :] = jnp.where((at >= key) & same, 1.0, 0.0).astype(BF16)


class Total:
    def __init__(self, place, core, plane, outer, sems):
        self.p, self.core, self.plane, self.outer = place, core, plane, outer
        self.send, self.got_core, self.got_plane, self.got_outer = sems
        self.started, self.count = [], 0

    def _go(self, src, dst, recv, peer):
        copy = remote(src, dst, self.send.at[self.count], recv, peer)
        self.count += 1
        copy.start()
        self.started.append(copy)

    def start(self, value):
        self.core[0] = value
        self._go(self.core.at[0], self.core.at[1], self.got_core.at[0], self.p.at(dc=1))

    def plane_step(self):
        p = self.p
        block = self.core.at[1]
        remote(block, block, self.send.at[0], self.got_core.at[0], p.at()).wait_recv()
        here = p.i * p.ny + p.y
        self.plane[here] = self.core[0] + self.core[1]
        for peer in p.plane_peers():
            self._go(
                self.plane.at[here], self.plane.at[here], self.got_plane.at[here], p.at(*peer)
            )

    def outer_step(self):
        p = self.p
        for _, di, dy, _ in p.plane_peers():
            i, y = (p.i + p.inner - di) % p.inner, (p.y + p.ny - dy) % p.ny
            block = self.plane.at[i * p.ny + y]
            sem = self.got_plane.at[i * p.ny + y]
            remote(block, block, self.send.at[0], sem, p.at()).wait_recv()
        total = self.plane[0]
        for k in range(1, p.inner * p.ny):
            total = total + self.plane[k]
        self.outer[p.o] = total
        for peer in p.outer_peers():
            self._go(
                self.outer.at[p.o], self.outer.at[p.o], self.got_outer.at[p.o], p.at(*peer)
            )

    def result(self):
        p = self.p
        for k in range(1, OUTER):
            o = (p.o + OUTER - k) % OUTER
            block = self.outer.at[o]
            remote(block, block, self.send.at[0], self.got_outer.at[o], p.at()).wait_recv()
        total = self.outer[0]
        for k in range(1, OUTER):
            total = total + self.outer[k]
        return total

    def finish(self):
        for copy in self.started:
            copy.wait_send()

    @staticmethod
    def scratch(nd, nt_, shape):
        inner, ny = nd // OUTER, nt_ // 2
        return [
            pltpu.VMEM((2,) + shape, F32),
            pltpu.VMEM((inner * ny,) + shape, F32),
            pltpu.VMEM((OUTER,) + shape, F32),
        ]

    @staticmethod
    def semaphores(nd, nt_):
        inner, ny = nd // OUTER, nt_ // 2
        return [
            pltpu.SemaphoreType.DMA((1 + inner * ny - 1 + OUTER - 1,)),
            pltpu.SemaphoreType.DMA((1,)),
            pltpu.SemaphoreType.DMA((inner * ny,)),
            pltpu.SemaphoreType.DMA((OUTER,)),
        ]


def kernel_whole(
    nd, nt_,
    tokens, segments, wq, wk, wv, wo, w1, w2, inner_bias, gain1, shift1, gain2, shift2,
    mixer_bias, outer_bias, cotangent,
    out, grad_tokens, grad_q, grad_k, grad_v, grad_o, grad_1, grad_2,
    grad_ib, grad_g1, grad_s1, grad_g2, grad_s2, grad_mb, grad_ob,
    *scratch,
):
    it = iter(scratch)

    def take(count):
        return [next(it) for _ in range(count)]

    (held_kv, held_qo, held_2, held_1) = take(4)
    (segc, edges, mask, normed, normed_t, fq, fk, vb, num_s, den_s) = take(10)
    (res, unit, inv, h2, h2t, cot, dh2, act, dhid, dbt) = take(10)
    (do, dr, gn, gd, dk_s, dv_s, dq_s, dh1, sums, first_sums) = take(10)
    own, near, far, made, entering = take(5)
    own_b, near_b, far_b, made_b, leaving = take(5)
    bufs_f, bufs_qo, bufs_kv = take(10), take(10), take(10)
    bufs_t1, bufs_t2 = take(3), take(3)
    p = Place(nd, nt_)
    kv, qo = Gather(p, held_kv, take(6)), Gather(p, held_qo, take(6))
    g2, g1 = Gather(p, held_2, take(6)), Gather(p, held_1, take(6))
    firsts, lasts = edges.at[0], edges.at[1]
    ex = Exchange(p, firsts, lasts, False, own, near, far, made, entering, take(4))
    xb = Exchange(p, firsts, lasts, True, own_b, near_b, far_b, made_b, leaving, take(4))
    sf = Scatter(p, bufs_f, take(7))
    sqo, skv = Scatter(p, bufs_qo, take(7)), Scatter(p, bufs_kv, take(7))
    all_sum, first_sum = Total(p, *bufs_t1, take(4)), Total(p, *bufs_t2, take(4))

    rows_all, width = tokens.shape
    head, hidden = wq.shape[1], w1.shape[1]
    part_rows = wq.shape[0]
    block_shape = (OUTER, p.inner, part_rows)
    step, block = 128, min(256, rows_all)

    p.greet()
    here = (p.t, p.o, p.i)
    if head < LANES:
        blank = jnp.zeros((part_rows, 2 * LANES), BF16)
        held_kv[here] = blank
        held_qo[here] = blank
    held_kv[here + (slice(None), slice(0, head))] = wk[...].astype(BF16)
    held_kv[here + (slice(None), slice(LANES, LANES + head))] = wv[...].astype(BF16)
    p.meet()
    kv.outer_start()
    kv.spread(0)
    held_qo[here + (slice(None), slice(0, head))] = wq[...].astype(BF16)
    held_qo[here + (slice(None), slice(LANES, LANES + head))] = jnp.transpose(wo[...]).astype(BF16)
    held_2[here] = jnp.transpose(w2[...]).astype(BF16)
    held_1[here] = w1[...].astype(BF16)
    qo.outer_start()
    g2.outer_start()
    g1.outer_start()

    segr = segments[:, pl.ds(pl.multiple_of(p.t * rows_all, LANES), rows_all)].astype(F32)
    for start in range(0, rows_all, LANES):
        wide = jnp.broadcast_to(segr[:, start : start + LANES], (8, LANES))
        segc[start : start + LANES, :] = jnp.transpose(wide)[:, 0:1]
    for j in range(nt_):
        for e, at in enumerate((j * rows_all, (j + 1) * rows_all - 1)):
            edge = segments[:, at : at + 1].astype(F32)
            edges[e, j : j + 1, :] = jnp.broadcast_to(edge, (1, LANES))
    first_id, last_id = segr[:, 0:1], segr[:, rows_all - 1 : rows_all]

    def norm(k, _):
        at = pl.ds(pl.multiple_of(k * step, step), step)
        x = tokens[at, :].astype(F32)
        center = x - jnp.mean(x, axis=-1, keepdims=True)
        spread = jnp.mean(center * center, axis=-1, keepdims=True)
        y = center * lax.rsqrt(spread + EPSILON) * gain1[...] + shift1[...]
        normed[at, :] = y.astype(BF16)
        normed_t[:, at] = jnp.transpose(y).astype(BF16)
        cot[:, at] = jnp.transpose(cotangent[at, :].astype(F32)).astype(BF16)
        return 0

    lax.fori_loop(0, rows_all // step, norm, 0)
    for start in range(0, rows_all, 128):
        later = lax.broadcasted_iota(jnp.int32, (128, rows_all), 0) + start
        earlier = lax.broadcasted_iota(jnp.int32, (128, rows_all), 1)
        same = segc[start : start + 128, :] == segr
        mask[start : start + 128, :] = jnp.where((later >= earlier) & same, 1.0, 0.0).astype(BF16)
    for k in range(1, OUTER):
        kv.spread(k)
    for k in range(OUTER):
        kv.turn(k)
    for k in range(OUTER):
        qo.spread(k)
    for k in range(OUTER):
        kv.corner(k)
    kv.core_done()

    def keys_values(g, _):
        w = held_kv[g].reshape(width, 2 * LANES)
        both = nn(normed[...], w)
        keys = feature(both[:, :LANES]).astype(BF16)
        values = both[:, LANES:].astype(BF16)
        fk[g] = keys
        vb[g] = values
        kept = jnp.where(segc[...] == last_id, keys, jnp.zeros_like(keys))
        own[g, :HEAD, :] = pack_state(tn(kept, values))
        total = jnp.sum(kept.astype(F32), axis=0, keepdims=True)
        own[g, HEAD:, :] = jnp.broadcast_to(total, (STATE_ROWS - HEAD, LANES))
        return 0

    lax.fori_loop(0, nt_, keys_values, 0)
    ex.step_near()
    for k in range(OUTER):
        qo.turn(k)
    for k in range(OUTER):
        g2.spread(k)
    for k in range(OUTER):
        qo.corner(k)
    qo.core_done()

    def queries(g, _):
        w = held_qo[g].reshape(width, 2 * LANES)
        fq[g] = feature(nn(normed[...], w[:, :LANES])).astype(BF16)
        return 0

    lax.fori_loop(0, nt_, queries, 0)
    ex.step_far()
    for k in range(OUTER):
        g1.spread(k)

    def inside(g, _):
        values = split_heads(vb[g], 1.0)
        for start in range(0, rows_all, block):
            end = start + block
            now = mask[start:end, :end]
            query = split_heads(fq[g, start:end, :], 0.0)
            keys = fk[g, :end, :]
            parts = []
            for h in range(2):
                scores = nt(query[h], keys).astype(BF16) * now
                parts.append(nn(scores, values[h][:end]))
            left = left_lanes(parts[0].shape)
            num_s[g, start:end, :] = jnp.where(left, parts[0], parts[1])
            den_s[g, start:end, :] = pltpu.roll(
                jnp.where(left, parts[1], parts[0]), HEAD, 1
            )
        return 0

    lax.fori_loop(0, nt_ // 2, inside, 0)
    for k in range(OUTER):
        g2.turn(k)
    ex.step_enter()
    lax.fori_loop(nt_ // 2, nt_, inside, 0)
    for k in range(OUTER):
        g1.turn(k)
    for k in range(OUTER):
        g2.corner(k)
    ex.arrive()

    def outside(g, _):
        state = entering[g]
        high, low = two_parts(wide_state(state[:HEAD]))
        total = jnp.broadcast_to(jnp.transpose(state[HEAD:, :])[:, 0:1], (LANES, LANES))
        sum_high, sum_low = two_parts(jnp.where(same_head(), total, 0.0))
        query = fq[g]
        query = jnp.where(segc[...] == first_id, query, jnp.zeros_like(query))
        num = num_s[g] + (nn(query, high) + nn(query, low))
        den = den_s[g] + (nn(query, sum_high) + nn(query, sum_low))
        inverse = 1.0 / den
        den_s[g] = inverse
        num_s[g] = num * inverse
        return 0

    lax.fori_loop(0, nt_, outside, 0)
    mixed, rden = num_s, den_s
    for k in range(OUTER):
        g1.corner(k)

    def output_weight(g):
        return held_qo[g, :, :, :, LANES:].reshape(width, LANES)

    def enter(k, _):
        at = pl.ds(pl.multiple_of(k * step, step), step)
        r = tokens[at, :].astype(F32) + mixer_bias[...]
        for g in range(nt_):
            r = r + nt(mixed[g, at, :].astype(BF16), output_weight(g))
        center = r - jnp.mean(r, axis=-1, keepdims=True)
        spread = jnp.mean(center * center, axis=-1, keepdims=True)
        scale = lax.rsqrt(spread + EPSILON)
        n = center * scale
        y = n * gain2[...] + shift2[...]
        res[at, :] = r + outer_bias[...]
        unit[at, :] = n
        inv[at, :] = scale
        h2[at, :] = y.astype(BF16)
        h2t[:, at] = jnp.transpose(y).astype(BF16)
        dh2[at, :] = jnp.zeros((step, width), F32)
        return 0

    lax.fori_loop(0, rows_all // step, enter, 0)
    sums[...] = jnp.zeros_like(sums)
    g2.core_done()
    g1.core_done()
    tall = width // OUTER

    def feed(g):
        wi = held_1[g].reshape(width, hidden)
        wt = held_2[g].reshape(width, hidden)
        total = jnp.zeros((1, hidden), F32)
        bias = inner_bias[:, pl.ds(pl.multiple_of(g * hidden, LANES), hidden)]
        for start in range(0, rows_all, block):
            end = start + block
            u = nn(h2[start:end, :], wi) + bias
            below = 0.5 * (1.0 + lax.erf(u * 0.7071067811865476))
            slope = below + u * (jnp.exp(-0.5 * (u * u)) * 0.3989422804014327)
            a = (u * below).astype(BF16)
            du = (nn(cotangent[start:end, :], wt) * slope).astype(BF16)
            act[start:end, :] = a
            dhid[start:end, :] = du
            total = total + jnp.sum(du.astype(F32), axis=0, keepdims=True)
            res[start:end, :] += nt(a, wt)
            dh2[start:end, :] += nt(du, wi)
        sums[pl.ds(8 + g, 1), 0:hidden] = total

    shape = (p.inner, part_rows, hidden)

    def feed_grads(y, mine):
        for o in range(OUTER):
            for s, (left, right) in enumerate(((h2t, dhid), (cot, act))):
                lanes = slice(s * hidden, (s + 1) * hidden)
                value = nn(left[o * tall : (o + 1) * tall, :], right[...]).reshape(shape)
                if mine:
                    value = value + sf.core[y, o, :, :, lanes].astype(F32)
                    sf.core[y, o, :, :, lanes] = value.astype(BF16)
                else:
                    sf.give[y, o, :, :, lanes] = value.astype(BF16)

    for dy in list(range(1, p.ny)) + [0]:
        y = (p.y + dy) % p.ny
        feed(y * 2 + 1 - p.c)
        feed_grads(y, False)
        sf.core_send(y)
        feed(y * 2 + p.c)
        sf.core_wait(y)
        feed_grads(y, True)
        sf.first(dy)

    def leave(k, _):
        at = pl.ds(pl.multiple_of(k * step, step), step)
        out[at, :] = res[at, :].astype(BF16)
        n = unit[at, :]
        grad = dh2[at, :]
        e = cotangent[at, :].astype(F32)
        pushed = grad * gain2[...]
        mean = jnp.mean(pushed, axis=-1, keepdims=True)
        along = jnp.mean(pushed * n, axis=-1, keepdims=True)
        back = e + (pushed - mean - n * along) * inv[at, :]
        dr[at, :] = back
        low = back.astype(BF16)
        wide = low.astype(F32)
        dbt[:, at] = jnp.transpose(wide).astype(BF16)
        for g in range(nt_):
            do[g, at, :] = nn(low, output_weight(g))
        sums[2:3, :] += jnp.sum(grad * n, axis=0, keepdims=True)
        sums[3:4, :] += jnp.sum(grad, axis=0, keepdims=True)
        sums[4:5, :] += jnp.sum(wide, axis=0, keepdims=True)
        sums[5:6, :] += jnp.sum(e, axis=0, keepdims=True)
        return 0

    lax.fori_loop(0, rows_all // step, leave, 0)

    def first(g, _):
        low = (do[g] * rden[g]).astype(BF16)
        gn[g] = low
        product = low.astype(F32) * mixed[g]
        left = left_lanes(product.shape)
        zero = jnp.zeros_like(product)
        one = jnp.sum(jnp.where(left, product, zero), axis=-1, keepdims=True)
        two = jnp.sum(jnp.where(left, zero, product), axis=-1, keepdims=True)
        slope = -jnp.where(left, one, two)
        gd[g] = slope
        kept = jnp.where(segc[...] == first_id, fq[g], jnp.zeros_like(low))
        own_b[g, :HEAD, :] = pack_state(tn(kept, low))
        total = jnp.sum(kept.astype(F32) * slope, axis=0, keepdims=True)
        own_b[g, HEAD:, :] = jnp.broadcast_to(total, (STATE_ROWS - HEAD, LANES))
        return 0

    lax.fori_loop(0, nt_, first, 0)
    xb.step_near()
    all_sum.start(sums[...])

    def inside_back(g, _):
        values, keys = vb[g], fk[g]
        key_heads = split_heads(keys, 0.0)
        state = entering[g]
        high, low = two_parts(wide_state(state[:HEAD]))
        query_t = jnp.transpose(fq[g].astype(F32)).astype(BF16)
        grad_t = jnp.transpose(gn[g].astype(F32)).astype(BF16)
        dk_t = jnp.zeros((LANES, rows_all), F32)
        dv_t = jnp.zeros((LANES, rows_all), F32)
        for start in range(0, rows_all, block):
            end = start + block
            now = mask[start:end, :end]
            query, grad = fq[g, start:end, :], gn[g, start:end, :]
            slope = gd[g, start:end, :]
            query_heads, grad_heads = split_heads(query, 0.0), split_heads(grad, 0.0)
            dq = jnp.where(
                segc[start:end, :] == first_id,
                nt(grad, high) + nt(grad, low) + slope * state[HEAD : HEAD + 1, :],
                0.0,
            )
            dk_parts, dv_parts = [], []
            for h in range(2):
                lanes = slice(h * HEAD, h * HEAD + 1)
                part = slice(h * HEAD, (h + 1) * HEAD)
                weight = nt(query_heads[h], keys[:end]).astype(BF16) * now
                share = (nt(grad_heads[h], values[:end]) + slope[:, lanes]).astype(BF16) * now
                dq = dq + nn(share, key_heads[h][:end])
                dk_parts.append(nn(query_t[part, start:end], share))
                dv_parts.append(nn(grad_t[part, start:end], weight))
            dk_now = jnp.concatenate(dk_parts, axis=0)
            dv_now = jnp.concatenate(dv_parts, axis=0)
            if end < rows_all:
                pad = jnp.zeros((LANES, rows_all - end), F32)
                dk_now = jnp.concatenate([dk_now, pad], axis=1)
                dv_now = jnp.concatenate([dv_now, pad], axis=1)
            dk_t, dv_t = dk_t + dk_now, dv_t + dv_now
            dq_s[g, start:end, :] = (dq * jnp.minimum(query.astype(F32), 1.0)).astype(BF16)
        dk_s[g] = jnp.transpose(dk_t)
        dv_s[g] = jnp.transpose(dv_t)
        return 0

    lax.fori_loop(0, nt_ // 2, inside_back, 0)
    xb.step_far()
    all_sum.plane_step()
    sf.second_y()
    lax.fori_loop(nt_ // 2, nt_, inside_back, 0)
    xb.step_enter()
    all_sum.outer_step()
    sf.second_i()

    def attention_grads(scatter, dc, joint):
        for dy in list(range(1, p.ny)) + [0]:
            y = (p.y + dy) % p.ny
            g = y * 2 + (p.c + dc) % 2
            values = joint(g)
            if not dc:
                scatter.core_wait(y)
            for s, (left, right) in enumerate(values):
                lanes = slice(s * LANES, (s + 1) * LANES)
                value = nn(left, right).reshape(block_shape + (LANES,))
                if dc:
                    scatter.give[y, :, :, :, lanes] = value.astype(BF16)
                else:
                    value = value + scatter.core[y, :, :, :, lanes].astype(F32)
                    scatter.core[y, :, :, :, lanes] = value.astype(BF16)
            if dc:
                scatter.core_send(y)
            else:
                scatter.first(dy)

    def query_output(g):
        return ((normed_t[...], dq_s[g]), (dbt[...], mixed[g].astype(BF16)))

    attention_grads(sqo, 1, query_output)
    attention_grads(sqo, 0, query_output)
    sf.third()

    def query_back(g, _):
        dh1[...] += nt(dq_s[g], held_qo[g, :, :, :, :LANES].reshape(width, LANES))
        return 0

    dh1[...] = jnp.zeros_like(dh1)
    lax.fori_loop(0, nt_, query_back, 0)
    sqo.second_y()
    sqo.second_i()
    xb.arrive()

    def key_value(g):
        state = leaving[g]
        high, low = two_parts(wide_state(state[:HEAD]))
        keys, values = fk[g], vb[g]
        dk = nt(values, high) + nt(values, low) + state[HEAD : HEAD + 1, :]
        dv = nn(keys, high) + nn(keys, low)
        closing = segc[...] == last_id
        dk = dk_s[g] + jnp.where(closing, dk, 0.0)
        dv = dv_s[g] + jnp.where(closing, dv, 0.0)
        dk = (dk * jnp.minimum(keys.astype(F32), 1.0)).astype(BF16)
        dv = dv.astype(BF16)
        joint = jnp.concatenate([dk, dv], axis=1)
        dh1[...] += nt(joint, held_kv[g].reshape(width, 2 * LANES))
        return ((normed_t[...], dk), (normed_t[...], dv))

    attention_grads(skv, 1, key_value)
    attention_grads(skv, 0, key_value)
    sqo.third()
    first_sums[...] = jnp.zeros_like(first_sums)

    def finish(k, _):
        at = pl.ds(pl.multiple_of(k * step, step), step)
        x = tokens[at, :].astype(F32)
        center = x - jnp.mean(x, axis=-1, keepdims=True)
        spread = jnp.mean(center * center, axis=-1, keepdims=True)
        scale = lax.rsqrt(spread + EPSILON)
        n = center * scale
        grad = dh1[at, :]
        pushed = grad * gain1[...]
        mean = jnp.mean(pushed, axis=-1, keepdims=True)
        along = jnp.mean(pushed * n, axis=-1, keepdims=True)
        back = (pushed - mean - n * along) * scale
        grad_tokens[at, :] = (dr[at, :] + back).astype(BF16)
        first_sums[0:1, :] += jnp.sum(grad * n, axis=0, keepdims=True)
        first_sums[1:2, :] += jnp.sum(grad, axis=0, keepdims=True)
        return 0

    lax.fori_loop(0, rows_all // step, finish, 0)
    first_sum.start(first_sums[...])
    skv.second_y()
    first_sum.plane_step()
    skv.second_i()
    total = sf.last()
    grad_1[...] = total[:, :hidden]
    grad_2[...] = jnp.transpose(total[:, hidden:])
    skv.third()
    first_sum.outer_step()
    total = sqo.last()
    grad_q[...] = total[:, :head]
    grad_o[...] = jnp.transpose(total[:, LANES:])[:head, :]
    total = all_sum.result()
    grad_g2[...] = total[2:3, :]
    grad_s2[...] = total[3:4, :]
    grad_mb[...] = total[4:5, :]
    grad_ob[...] = total[5:6, :]
    for g in range(nt_):
        grad_ib[:, g * hidden : (g + 1) * hidden] = total[8 + g : 9 + g, :hidden]
    total = skv.last()
    grad_k[...] = total[:, :head]
    grad_v[...] = total[:, LANES : LANES + head]
    total = first_sum.result()
    grad_g1[...] = total[0:1, :]
    grad_s1[...] = total[1:2, :]
    for each in (kv, qo, g2, g1, ex, xb, sf, sqo, skv, all_sum, first_sum):
        each.finish()


def local(nd, nt_, *args):
    (tokens, segments, wq, wk, wv, wo, w1, w2, inner_bias, *vectors, cotangent) = args
    rows, width = tokens.shape
    inner = nd // OUTER
    part_rows, hidden = w1.shape
    vm = pl.BlockSpec(memory_space=pltpu.VMEM)
    group = (nt_, rows, LANES)
    row = jax.ShapeDtypeStruct((1, width), F32)
    outs = [
        jax.ShapeDtypeStruct(tokens.shape, BF16),
        jax.ShapeDtypeStruct(tokens.shape, BF16),
        *[jax.ShapeDtypeStruct(w.shape, F32) for w in (wq, wk, wv, wo, w1, w2)],
        jax.ShapeDtypeStruct((1, nt_ * hidden), F32),
        *[row] * 6,
    ]
    held = (nt_, OUTER, inner, part_rows)
    state = pltpu.VMEM((nt_, STATE_ROWS, LANES), F32)
    square = (rows, width)
    scratch = [
        pltpu.VMEM(held + (2 * LANES,), BF16),
        pltpu.VMEM(held + (2 * LANES,), BF16),
        pltpu.VMEM(held + (hidden,), BF16),
        pltpu.VMEM(held + (hidden,), BF16),
        pltpu.VMEM((rows, 1), F32),
        pltpu.VMEM((2, nt_, LANES), F32),
        pltpu.VMEM((rows, rows), BF16),
        pltpu.VMEM(square, BF16),
        pltpu.VMEM((width, rows), BF16),
        pltpu.VMEM(group, BF16),
        pltpu.VMEM(group, BF16),
        pltpu.VMEM(group, BF16),
        pltpu.VMEM(group, F32),
        pltpu.VMEM(group, F32),
        pltpu.VMEM(square, F32),
        pltpu.VMEM(square, F32),
        pltpu.VMEM((rows, 1), F32),
        pltpu.VMEM(square, BF16),
        pltpu.VMEM((width, rows), BF16),
        pltpu.VMEM((width, rows), BF16),
        pltpu.VMEM(square, F32),
        pltpu.VMEM((rows, hidden), BF16),
        pltpu.VMEM((rows, hidden), BF16),
        pltpu.VMEM((width, rows), BF16),
        pltpu.VMEM(group, F32),
        pltpu.VMEM(square, F32),
        pltpu.VMEM(group, BF16),
        pltpu.VMEM(group, F32),
        pltpu.VMEM(group, F32),
        pltpu.VMEM(group, F32),
        pltpu.VMEM(group, BF16),
        pltpu.VMEM(square, F32),
        pltpu.VMEM((8 + max(8, nt_), width), F32),
        pltpu.VMEM((8, width), F32),
    ]
    for _ in range(2):
        scratch += Exchange.scratch(nd, nt_) + [state]
    scratch += Scatter.scratch(nd, nt_, part_rows, 2 * hidden)
    scratch += Scatter.scratch(nd, nt_, part_rows, 2 * LANES)
    scratch += Scatter.scratch(nd, nt_, part_rows, 2 * LANES)
    scratch += Total.scratch(nd, nt_, (8 + max(8, nt_), width))
    scratch += Total.scratch(nd, nt_, (8, width))
    for _ in range(4):
        scratch += Gather.semaphores(nd, nt_)
    for _ in range(2):
        scratch += Exchange.semaphores(nd, nt_)
    for _ in range(3):
        scratch += Scatter.semaphores(nd, nt_)
    for _ in range(2):
        scratch += Total.semaphores(nd, nt_)
    operands = (
        tokens, segments[None], wq, wk, wv, wo, w1, w2, inner_bias[None],
        *[v[None] for v in vectors], cotangent,
    )
    results = pl.pallas_call(
        functools.partial(kernel_whole, nd, nt_),
        out_shape=outs,
        in_specs=[vm] * len(operands),
        out_specs=[vm] * len(outs),
        scratch_shapes=scratch,
        compiler_params=pltpu.CompilerParams(
            collective_id=0, has_side_effects=True, vmem_limit_bytes=VMEM_LIMIT
        ),
        name="whole_layer",
    )(*operands)
    return tuple(results[:8]) + tuple(v.reshape(-1) for v in results[8:])


def solution(mesh):
    rows = P(("dp", "tensor"), None)
    one, two, all_of = P("dp", "tensor"), P("tensor", "dp"), P()
    weights = (one, one, one, two, one, two)
    return jax.shard_map(
        functools.partial(local, mesh.shape["dp"], mesh.shape["tensor"]),
        mesh=mesh,
        in_specs=(rows, P("dp")) + weights + (all_of,) * 7 + (rows,),
        out_specs=(rows, rows) + weights + (all_of,) * 7,
        check_vma=False,
    )
```

```python
import functools

import jax
import jax.numpy as jnp
from jax import lax
from jax.experimental import pallas as pl
from jax.experimental.pallas import tpu as pltpu
from jax.sharding import PartitionSpec as P

HEAD = 64
LANES = 128
EPSILON = 1e-05
MESH = pl.DeviceIdType.MESH
F32 = jnp.float32
BF16 = jnp.bfloat16
OUTER = 4
EVEN_WAYS = ((0, 1), (2, 3))
WIDE_WAYS = ((0, 1, 3), (2,))
VMEM_LIMIT = 56 << 20


def nn(a, b):
    return lax.dot_general(a, b, (((1,), (0,)), ((), ())), preferred_element_type=F32)


def nt(a, b):
    return lax.dot_general(a, b, (((1,), (1,)), ((), ())), preferred_element_type=F32)


def tn(a, b):
    return lax.dot_general(a, b, (((0,), (0,)), ((), ())), preferred_element_type=F32)


class Place:
    def __init__(self, dp_size, tensor_size):
        self.nd, self.nt = dp_size, tensor_size
        self.inner, self.ny = dp_size // OUTER, tensor_size // 2
        self.d, self.t = lax.axis_index("dp"), lax.axis_index("tensor")
        self.o, self.i = self.d // self.inner, self.d % self.inner
        self.y, self.c = self.t // 2, self.t % 2
        self.barrier = pltpu.get_barrier_semaphore()

    def at(self, do=0, di=0, dy=0, dc=0):
        o, i = (self.o + do) % OUTER, (self.i + di) % self.inner
        return self.to(o, i, (self.y + dy) % self.ny, (self.c + dc) % 2)

    def to(self, o, i, y, c):
        return (o * self.inner + i, y * 2 + c)

    def nearest(self, k):
        if k == 0:
            return self.o
        high = self.o // 2
        edge = self.o + high * (3 - 2 * self.o)
        place = k * (1 - edge) + (k // 2) * k * edge
        return place + high * (3 - 2 * place)

    def outer_peers(self):
        return [(k, 0, 0, 0) for k in range(1, OUTER)]

    def plane_peers(self):
        return [
            (0, di, dy, 0) for di in range(self.inner) for dy in range(self.ny) if di or dy
        ]

    def peers(self):
        return self.outer_peers() + [
            (0, di, dy, dc)
            for di in range(self.inner)
            for dy in range(self.ny)
            for dc in range(2)
            if di or dy or dc
        ]

    def greet(self):
        for peer in self.peers():
            pl.semaphore_signal(
                self.barrier, inc=1, device_id=self.at(*peer), device_id_type=MESH
            )

    def meet(self):
        pl.semaphore_wait(self.barrier, len(self.peers()))


def remote(src, dst, send, recv, peer):
    return pltpu.make_async_remote_copy(
        src_ref=src,
        dst_ref=dst,
        send_sem=send,
        recv_sem=recv,
        device_id=peer,
        device_id_type=MESH,
    )


class Sender:
    def __init__(self, place, send):
        self.p, self.send, self.started = place, send, []

    def go(self, src, dst, recv, peer):
        copy = remote(src, dst, self.send.at[len(self.started)], recv, peer)
        copy.start()
        self.started.append(copy)

    def got(self, block, recv):
        remote(block, block, self.send.at[0], recv, self.p.at()).wait_recv()

    def finish(self):
        for copy in self.started:
            copy.wait_send()


class Gather(Sender):
    def __init__(self, place, held, sems):
        super().__init__(place, sems[0])
        self.held = held
        self.got_outer, self.got_i, self.got_y, self.got_d, self.got_core = sems[1:]

    def _block(self, k, i, y):
        p = self.p
        return self.held.at[y * 2 + p.c, p.nearest(k), i]

    def outer_start(self):
        p = self.p
        mine = self._block(0, p.i, p.y)
        for k in range(1, OUTER):
            to = p.to(p.nearest(k), p.i, p.y, p.c)
            self.go(mine, mine, self.got_outer.at[p.o], to)

    def spread(self, k):
        p = self.p
        block = self._block(k, p.i, p.y)
        if k:
            self.got(block, self.got_outer.at[p.nearest(k)])
        for di in range(1, p.inner):
            self.go(block, block, self.got_i.at[di - 1, k], p.at(di=di))
        for dy in range(1, p.ny):
            self.go(block, block, self.got_y.at[dy - 1, k], p.at(dy=dy))
        self.go(block, block, self.got_core.at[p.y], p.at(dc=1))

    def turn(self, k):
        p = self.p
        for di in range(1, p.inner):
            block = self._block(k, (p.i + p.inner - di) % p.inner, p.y)
            self.got(block, self.got_i.at[di - 1, k])
            if k < 2:
                for dy in range(1, p.ny):
                    self.go(block, block, self.got_d.at[di - 1, dy - 1, k], p.at(dy=dy))
            self.go(block, block, self.got_core.at[p.y], p.at(dc=1))
        for dy in range(1, p.ny):
            y = (p.y + p.ny - dy) % p.ny
            block = self._block(k, p.i, y)
            self.got(block, self.got_y.at[dy - 1, k])
            if k >= 2:
                for di in range(1, p.inner):
                    self.go(block, block, self.got_d.at[di - 1, dy - 1, k], p.at(di=di))
            self.go(block, block, self.got_core.at[y], p.at(dc=1))

    def corner(self, k):
        p = self.p
        for di in range(1, p.inner):
            for dy in range(1, p.ny):
                y = (p.y + p.ny - dy) % p.ny
                block = self._block(k, (p.i + p.inner - di) % p.inner, y)
                self.got(block, self.got_d.at[di - 1, dy - 1, k])
                self.go(block, block, self.got_core.at[y], p.at(dc=1))

    def core_done(self, dy):
        p = self.p
        y = (p.y + dy) % p.ny
        self.got(self.held.at[y * 2 + 1 - p.c], self.got_core.at[y])

    @staticmethod
    def semaphores(nd, nt_):
        di, dy = nd // OUTER - 1, nt_ // 2 - 1
        sends = (OUTER - 1) + OUTER * (di + dy + 1 + di + dy) + 2 * OUTER * di * dy
        return [
            pltpu.SemaphoreType.DMA((sends,)),
            pltpu.SemaphoreType.DMA((OUTER,)),
            pltpu.SemaphoreType.DMA((di, OUTER)),
            pltpu.SemaphoreType.DMA((dy, OUTER)),
            pltpu.SemaphoreType.DMA((di, dy, OUTER)),
            pltpu.SemaphoreType.DMA((nt_ // 2,)),
        ]


class Scatter(Sender):
    def __init__(self, place, by_i, by_y, bufs, sems):
        super().__init__(place, sems[0])
        self.by_i, self.by_y = by_i, by_y
        (self.give, self.core, self.in_i, self.in_y, self.sum_i, self.sum_y,
         self.then_y, self.then_i, self.own, self.outer) = bufs
        self.got_core, self.got_i, self.got_y, self.got_ty, self.got_ti, self.got_outer = sems[1:]

    def core_send(self, y):
        self.go(self.give.at[y], self.core.at[y], self.got_core.at[y], self.p.at(dc=1))

    def core_wait(self, y):
        self.got(self.core.at[y], self.got_core.at[y])

    def first_i(self, dy, k):
        p, at = self.p, self.by_i.index(k)
        y, o = (p.y + dy) % p.ny, (p.o + k) % OUTER
        for di in range(1, p.inner):
            self.go(
                self.core.at[y, o, (p.i + di) % p.inner], self.in_i.at[di - 1, at, dy],
                self.got_i.at[di - 1, at, dy], p.at(di=di),
            )

    def first_y(self, dy, k, di):
        p, at = self.p, self.by_y.index(k)
        y, o, i = (p.y + dy) % p.ny, (p.o + k) % OUTER, (p.i + di) % p.inner
        self.go(
            self.core.at[y, o, i], self.in_y.at[dy - 1, at, di],
            self.got_y.at[dy - 1, at, di], p.at(dy=dy),
        )

    def first(self, dy):
        for k in self.by_y:
            for di in range(self.p.inner) if dy else ():
                self.first_y(dy, k, di)
        for k in self.by_i:
            self.first_i(dy, k)

    def second_y(self, k):
        p, at = self.p, self.by_y.index(k)
        o = (p.o + k) % OUTER
        for di in list(range(1, p.inner)) + [0]:
            total = self.core[p.y, o, (p.i + di) % p.inner].astype(F32)
            for dy in range(1, p.ny):
                block = self.in_y.at[dy - 1, at, di]
                self.got(block, self.got_y.at[dy - 1, at, di])
                total = total + block[...].astype(F32)
            self.sum_y[at, di] = total.astype(BF16)
            if di:
                self.go(
                    self.sum_y.at[at, di], self.then_i.at[di - 1, at],
                    self.got_ti.at[di - 1, at], p.at(di=di),
                )

    def second_i(self, k, dy):
        p, at = self.p, self.by_i.index(k)
        total = self.core[(p.y + dy) % p.ny, (p.o + k) % OUTER, p.i].astype(F32)
        for di in range(1, p.inner):
            block = self.in_i.at[di - 1, at, dy]
            self.got(block, self.got_i.at[di - 1, at, dy])
            total = total + block[...].astype(F32)
        self.sum_i[at, dy] = total.astype(BF16)
        if dy:
            self.go(
                self.sum_i.at[at, dy], self.then_y.at[dy - 1, at],
                self.got_ty.at[dy - 1, at], p.at(dy=dy),
            )

    def second(self):
        for k in self.by_y:
            self.second_y(k)
        for dy in list(range(1, self.p.ny)) + [0]:
            for k in self.by_i:
                self.second_i(k, dy)

    def third(self, k):
        p = self.p
        if k in self.by_i:
            at, count, place, sems = self.by_i.index(k), p.ny, self.then_y, self.got_ty
            total = self.sum_i[at, 0].astype(F32)
        else:
            at, count, place, sems = self.by_y.index(k), p.inner, self.then_i, self.got_ti
            total = self.sum_y[at, 0].astype(F32)
        for j in range(count - 1):
            self.got(place.at[j, at], sems.at[j, at])
            total = total + place[j, at].astype(F32)
        self.own[k] = total.astype(BF16)
        if k:
            self.go(self.own.at[k], self.outer.at[k - 1], self.got_outer.at[k - 1], p.at(do=k))

    def last(self):
        total = self.own[0].astype(F32)
        for k in range(1, OUTER):
            self.got(self.outer.at[k - 1], self.got_outer.at[k - 1])
            total = total + self.outer[k - 1].astype(F32)
        return total

    @staticmethod
    def scratch(nd, nt_, by_i, by_y, rows, columns):
        inner, ny = nd // OUTER, nt_ // 2
        ki, ky = len(by_i), len(by_y)
        leads = [
            (ny, OUTER, inner), (ny, OUTER, inner), (inner - 1, ki, ny), (ny - 1, ky, inner),
            (ki, ny), (ky, inner), (ny - 1, ki), (inner - 1, ky), (OUTER,), (OUTER - 1,),
        ]
        return [pltpu.VMEM(lead + (rows, columns), BF16) for lead in leads]

    @staticmethod
    def semaphores(nd, nt_, by_i, by_y):
        inner, ny = nd // OUTER, nt_ // 2
        di, dy, ki, ky = inner - 1, ny - 1, len(by_i), len(by_y)
        sends = ny + ky * dy * inner + ki * di * ny + ky * di + ki * dy + OUTER - 1
        shapes = [
            (sends,), (ny,), (di, ki, ny), (dy, ky, inner), (dy, ki), (di, ky), (OUTER - 1,),
        ]
        return [pltpu.SemaphoreType.DMA(shape) for shape in shapes]


class Exchange(Sender):
    def __init__(self, place, back, bufs, sems):
        super().__init__(place, sems[0])
        self.back = back
        self.own, self.near, self.far, self.made, self.entering = bufs
        self.s_near, self.s_far, self.s_enter = sems[1:]
        self.rows = HEAD // place.inner
        self.members = place.inner * place.nt
        self.me = place.i * place.nt + place.t

    def put(self, g, packed, total, edge, inlet):
        p = self.p
        row = lax.broadcasted_iota(jnp.int32, (8, LANES), 0)
        foot = jnp.where(row == 0, total, jnp.where(row == 1, edge, inlet))
        for sub in range(p.inner):
            self.own[g * p.inner + sub, : self.rows, :] = packed[
                sub * self.rows : (sub + 1) * self.rows
            ]
            self.own[g * p.inner + sub, self.rows :, :] = foot

    def state(self, g):
        p = self.p
        at = pl.ds(g * p.inner, p.inner)
        packed = self.entering[at, : self.rows, :].reshape(HEAD, LANES)
        return packed, self.entering[g * p.inner, self.rows :, :]

    def _peers(self):
        p = self.p
        return [
            (di, dy, dc)
            for di in range(p.inner) for dy in range(p.ny) for dc in range(2) if di or dy or dc
        ]

    def _member(self, di, dy, dc):
        p = self.p
        i, y = (p.i + p.inner - di) % p.inner, (p.y + p.ny - dy) % p.ny
        return i * p.nt + y * 2 + (p.c + dc) % 2

    def _edge(self, block):
        return block[self.rows + 1 : self.rows + 2, :]

    def _inlet(self, block):
        return block[self.rows + 2 : self.rows + 3, :]

    def _hand(self, blocks, place, sems):
        p = self.p
        for di, dy, dc in self._peers():
            to = p.at(0, di, dy, dc)
            member = (to[0] % p.inner) * p.nt + to[1]
            self.go(blocks.at[member], place.at[self.me], sems.at[self.me], to)
        place[self.me] = blocks[self.me]

    def step_near(self):
        self._hand(self.own, self.near, self.s_near)

    def step_far(self):
        p = self.p
        for peer in self._peers():
            m = self._member(*peer)
            self.got(self.near.at[m], self.s_near.at[m])
        border = self.near[0 if self.back else self.members - 1]
        total = jnp.zeros_like(border)
        for j in range(self.members):
            block = self.near[j]
            total = total + jnp.where(self._edge(block) == self._edge(border), block, 0.0)
        row = lax.broadcasted_iota(jnp.int32, total.shape, 0)
        self.far[p.o] = jnp.where(row > self.rows, border, total)
        for k in range(1, OUTER):
            o = p.nearest(k)
            self.go(self.far.at[p.o], self.far.at[p.o], self.s_far.at[p.o], p.to(o, p.i, p.y, p.c))

    def step_enter(self):
        p = self.p
        for k in range(1, OUTER):
            o = p.nearest(k)
            self.got(self.far.at[o], self.s_far.at[o])
        order = list(range(self.members))
        if self.back:
            order.reverse()
        inlet = self._inlet(self.near[order[0]])
        incoming = jnp.zeros(self.near.shape[1:], F32)
        for o in range(OUTER):
            block = self.far[o]
            ids = jnp.where(o > p.o if self.back else o < p.o, self._edge(block), -1.0)
            incoming = incoming + jnp.where(ids == inlet, block, 0.0)
        for place, j in enumerate(order):
            block = self.near[j]
            if place:
                inlet = self._inlet(block)
                incoming = jnp.where(edge == inlet, running, 0.0)
            self.made[j] = incoming
            edge = self._edge(block)
            running = block + jnp.where(edge == inlet, incoming, 0.0)
        self._hand(self.made, self.entering, self.s_enter)

    def arrive(self):
        for peer in self._peers():
            m = self._member(*peer)
            self.got(self.entering.at[m], self.s_enter.at[m])

    @staticmethod
    def scratch(nd, nt_):
        inner = nd // OUTER
        shape = (HEAD // inner + 8, LANES)
        counts = [inner * nt_, inner * nt_, OUTER, inner * nt_, inner * nt_]
        return [pltpu.VMEM((count,) + shape, F32) for count in counts]

    @staticmethod
    def semaphores(nd, nt_):
        members = nd // OUTER * nt_
        counts = [2 * (members - 1) + OUTER - 1, members, OUTER, members]
        return [pltpu.SemaphoreType.DMA((count,)) for count in counts]


def left_lanes(shape):
    return lax.broadcasted_iota(jnp.int32, shape, len(shape) - 1) < HEAD


def split_heads(block, fill):
    left = left_lanes(block.shape)
    other = jnp.full_like(block, fill)
    return jnp.where(left, block, other), jnp.where(left, other, block)


def feature(values):
    return jnp.where(values > 0.0, values + 1.0, jnp.exp(jnp.minimum(values, 0.0)))


def pack_state(product):
    left = left_lanes((HEAD, LANES))
    return jnp.where(left, product[:HEAD], product[HEAD:])


def wide_state(packed):
    left = left_lanes((HEAD, LANES))
    zero = jnp.zeros_like(packed)
    return jnp.concatenate([jnp.where(left, packed, zero), jnp.where(left, zero, packed)], axis=0)


def two_parts(values):
    high = values.astype(BF16)
    return high, (values - high.astype(F32)).astype(BF16)


def same_head():
    row = lax.broadcasted_iota(jnp.int32, (LANES, LANES), 0) < HEAD
    return row == left_lanes((LANES, LANES))


class Total(Sender):
    def __init__(self, place, bufs, sems):
        super().__init__(place, sems[0])
        self.mine, self.core, self.plane, self.outer, self.whole = bufs
        self.got_core, self.got_plane, self.got_outer, self.got_whole = sems[1:]

    def start(self, value):
        p = self.p
        self.mine[...] = value.reshape(self.mine.shape)
        self.go(self.mine.at[1 - p.c], self.core, self.got_core.at[0], p.at(dc=1))

    def plane_step(self):
        p = self.p
        self.got(self.core, self.got_core.at[0])
        here = p.i * p.ny + p.y
        self.plane[here] = self.mine[p.c] + self.core[...]
        for peer in p.plane_peers():
            self.go(
                self.plane.at[here], self.plane.at[here], self.got_plane.at[here], p.at(*peer)
            )

    def outer_step(self):
        p = self.p
        for _, di, dy, _ in p.plane_peers():
            place = (p.i + p.inner - di) % p.inner * p.ny + (p.y + p.ny - dy) % p.ny
            self.got(self.plane.at[place], self.got_plane.at[place])
        total = self.plane[0]
        for k in range(1, p.inner * p.ny):
            total = total + self.plane[k]
        self.outer[p.o] = total
        for k in range(1, OUTER):
            to = p.to(p.nearest(k), p.i, p.y, p.c)
            self.go(self.outer.at[p.o], self.outer.at[p.o], self.got_outer.at[p.o], to)

    def core_step(self):
        p = self.p
        for k in range(1, OUTER):
            o = p.nearest(k)
            self.got(self.outer.at[o], self.got_outer.at[o])
        total = self.outer[0]
        for k in range(1, OUTER):
            total = total + self.outer[k]
        self.whole[p.c] = total
        self.go(self.whole.at[p.c], self.whole.at[p.c], self.got_whole.at[p.c], p.at(dc=1))

    def result(self):
        other = 1 - self.p.c
        self.got(self.whole.at[other], self.got_whole.at[other])
        return self.whole[...].reshape(-1, self.whole.shape[-1])

    @staticmethod
    def scratch(nd, nt_, rows, columns):
        leads = [(2,), (), (nd // OUTER * (nt_ // 2),), (OUTER,), (2,)]
        return [pltpu.VMEM(lead + (rows // 2, columns), F32) for lead in leads]

    @staticmethod
    def semaphores(nd, nt_):
        plane = nd // OUTER * (nt_ // 2)
        counts = [plane + OUTER, 1, plane, OUTER, 2]
        return [pltpu.SemaphoreType.DMA((count,)) for count in counts]


def kernel_whole(
    nd, nt_,
    tokens_in, segments, wq_in, wk_in, wv_in, wo_in, w1_in, w2_in,
    inner_bias, gain1, shift1, gain2, shift2, mixer_bias, outer_bias, cotangent_in,
    out_to, tokens_to, grad_q, grad_k, grad_v, grad_o, grad_1, grad_2,
    grad_ib, grad_g1, grad_s1, grad_g2, grad_s2, grad_mb, grad_ob,
    *scratch,
):
    it = iter(scratch)

    def take(count):
        return [next(it) for _ in range(count)]

    (held_kv, held_qo, held_2, held_1) = take(4)
    (tokens, wq, wk, wv, wo, w1, w2, cotangent, out, grad_tokens) = take(10)
    (segc, mask, normed, normed_t, fq, fk, vb, num_s, den_s) = take(9)
    (res, unit, inv, h2, h2t, cot, dh2, act, dhid, dbt) = take(10)
    (do, dr, gn, gd, dk_s, dv_s, dq_s, dkv_s, dh1, sums, first_sums) = take(11)
    bufs_x, bufs_xb = take(5), take(5)
    bufs_f, bufs_qo, bufs_kv = take(10), take(10), take(10)
    bufs_t1, bufs_t2 = take(5), take(5)
    p = Place(nd, nt_)
    kv, qo = Gather(p, held_kv, take(6)), Gather(p, held_qo, take(6))
    g2, g1 = Gather(p, held_2, take(6)), Gather(p, held_1, take(6))
    ex = Exchange(p, False, bufs_x, take(4))
    xb = Exchange(p, True, bufs_xb, take(4))
    sf = Scatter(p, *WIDE_WAYS, bufs_f, take(7))
    sqo = Scatter(p, *EVEN_WAYS, bufs_qo, take(7))
    skv = Scatter(p, *EVEN_WAYS, bufs_kv, take(7))
    all_sum, first_sum = Total(p, bufs_t1, take(5)), Total(p, bufs_t2, take(5))

    rows_all, width = tokens.shape
    head, hidden = wq.shape[1], w1.shape[1]
    part_rows = wq.shape[0]
    block_shape = (OUTER, p.inner, part_rows)
    step, block = 128, min(256, rows_all)

    (in_sems, out_sems) = take(2)
    p.greet()
    loads = [
        pltpu.make_async_copy(src, dst, in_sems.at[n])
        for n, (src, dst) in enumerate((
            (wk_in, wk), (wv_in, wv), (tokens_in, tokens), (wq_in, wq), (wo_in, wo),
            (w2_in, w2), (w1_in, w1), (cotangent_in, cotangent),
        ))
    ]
    for load in loads:
        load.start()
    here = (p.t, p.o, p.i)
    if head < LANES:
        blank = jnp.zeros((part_rows, 2 * LANES), BF16)
        held_kv[here] = blank
        held_qo[here] = blank
    loads[0].wait()
    loads[1].wait()
    held_kv[here + (slice(None), slice(0, head))] = wk[...].astype(BF16)
    held_kv[here + (slice(None), slice(LANES, LANES + head))] = wv[...].astype(BF16)
    for load in loads[3:7]:
        load.wait()
    held_qo[here + (slice(None), slice(0, head))] = wq[...].astype(BF16)
    held_qo[here + (slice(None), slice(LANES, LANES + head))] = wo[...].astype(BF16)
    held_2[here] = w2[...].astype(BF16)
    held_1[here] = w1[...].astype(BF16)
    loads[2].wait()
    segr = segments[:, pl.ds(pl.multiple_of(p.t * rows_all, LANES), rows_all)].astype(F32)
    for start in range(0, rows_all, LANES):
        wide = jnp.broadcast_to(segr[:, start : start + LANES], (8, LANES))
        segc[start : start + LANES, :] = jnp.transpose(wide)[:, 0:1]
    first_id, last_id = segr[:, 0:1], segr[:, rows_all - 1 : rows_all]

    def norm(k, _):
        at = pl.ds(pl.multiple_of(k * step, step), step)
        x = tokens[at, :].astype(F32)
        center = x - jnp.mean(x, axis=-1, keepdims=True)
        spread = jnp.mean(center * center, axis=-1, keepdims=True)
        y = center * lax.rsqrt(spread + EPSILON) * gain1[...] + shift1[...]
        normed[at, :] = y.astype(BF16)
        normed_t[:, at] = jnp.transpose(y).astype(BF16)
        return 0

    lax.fori_loop(0, rows_all // step, norm, 0)
    for start in range(0, rows_all, 128):
        later = lax.broadcasted_iota(jnp.int32, (128, rows_all), 0) + start
        earlier = lax.broadcasted_iota(jnp.int32, (128, rows_all), 1)
        same = segc[start : start + 128, :] == segr
        mask[start : start + 128, :] = jnp.where((later >= earlier) & same, 1.0, 0.0).astype(BF16)
    p.meet()
    kv.outer_start()
    kv.spread(0)
    qo.outer_start()
    qo.spread(0)
    g2.outer_start()
    g2.spread(0)
    g1.outer_start()
    for k in range(1, OUTER):
        kv.spread(k)
    g1.spread(0)
    for k in range(OUTER):
        kv.turn(k)
    for k in range(1, OUTER):
        qo.spread(k)
    for k in range(OUTER):
        kv.corner(k)
    for dy in range(p.ny):
        kv.core_done(dy)

    def keys_values(g, _):
        w = held_kv[g].reshape(width, 2 * LANES)
        both = nn(normed[...], w)
        keys = feature(both[:, :LANES]).astype(BF16)
        values = both[:, LANES:].astype(BF16)
        fk[g] = keys
        vb[g] = values
        kept = jnp.where(segc[...] == last_id, keys, jnp.zeros_like(keys))
        total = jnp.sum(kept.astype(F32), axis=0, keepdims=True)
        ex.put(g, pack_state(tn(kept, values)), total, last_id, first_id)
        return 0

    lax.fori_loop(0, nt_, keys_values, 0)
    ex.step_near()
    for k in range(OUTER):
        qo.turn(k)
    for k in range(1, OUTER):
        g2.spread(k)
    loads[7].wait()
    for start in range(0, rows_all, step):
        turned = jnp.transpose(cotangent[start : start + step, :].astype(F32))
        cot[:, start : start + step] = turned.astype(BF16)
    ex.step_far()
    g1.spread(1)
    for k in range(OUTER):
        qo.corner(k)
    for dy in range(p.ny):
        qo.core_done(dy)

    def queries(g, _):
        w = held_qo[g].reshape(width, 2 * LANES)
        fq[g] = feature(nn(normed[...], w[:, :LANES])).astype(BF16)
        return 0

    lax.fori_loop(0, nt_, queries, 0)

    def inside(g, _):
        values = split_heads(vb[g], 1.0)
        for start in range(0, rows_all, block):
            end = start + block
            now = mask[start:end, :end]
            query = split_heads(fq[g, start:end, :], 0.0)
            keys = fk[g, :end, :]
            parts = []
            for h in range(2):
                scores = nt(query[h], keys).astype(BF16) * now
                parts.append(nn(scores, values[h][:end]))
            left = left_lanes(parts[0].shape)
            num_s[g, start:end, :] = jnp.where(left, parts[0], parts[1])
            den_s[g, start:end, :] = pltpu.roll(
                jnp.where(left, parts[1], parts[0]), HEAD, 1
            )
        return 0

    lax.fori_loop(0, nt_ // 2, inside, 0)
    ex.step_enter()
    for k in range(2, OUTER):
        g1.spread(k)
    for k in range(OUTER):
        g2.turn(k)
    lax.fori_loop(nt_ // 2, nt_, inside, 0)
    for k in range(2):
        g1.turn(k)
    ex.arrive()

    def outside(g, _):
        packed, foot = ex.state(g)
        high, low = two_parts(wide_state(packed))
        total = jnp.broadcast_to(jnp.transpose(foot)[:, 0:1], (LANES, LANES))
        sum_high, sum_low = two_parts(jnp.where(same_head(), total, 0.0))
        query = fq[g]
        query = jnp.where(segc[...] == first_id, query, jnp.zeros_like(query))
        num = num_s[g] + (nn(query, high) + nn(query, low))
        den = den_s[g] + (nn(query, sum_high) + nn(query, sum_low))
        inverse = 1.0 / den
        den_s[g] = inverse
        num_s[g] = num * inverse
        return 0

    lax.fori_loop(0, nt_, outside, 0)
    mixed, rden = num_s, den_s
    for k in range(2, OUTER):
        g1.turn(k)

    def output_weight(g):
        return held_qo[g, :, :, :, LANES:].reshape(width, LANES)

    def enter(k, _):
        at = pl.ds(pl.multiple_of(k * step, step), step)
        r = tokens[at, :].astype(F32) + mixer_bias[...]
        for g in range(nt_):
            r = r + nt(mixed[g, at, :].astype(BF16), output_weight(g))
        center = r - jnp.mean(r, axis=-1, keepdims=True)
        spread = jnp.mean(center * center, axis=-1, keepdims=True)
        scale = lax.rsqrt(spread + EPSILON)
        n = center * scale
        y = n * gain2[...] + shift2[...]
        res[at, :] = r + outer_bias[...]
        unit[at, :] = n
        inv[at, :] = scale
        h2[at, :] = y.astype(BF16)
        h2t[:, at] = jnp.transpose(y).astype(BF16)
        dh2[at, :] = jnp.zeros((step, width), F32)
        return 0

    lax.fori_loop(0, rows_all // step, enter, 0)
    sums[...] = jnp.zeros_like(sums)
    g2.core_done(0)
    g1.core_done(0)
    tall = width // OUTER

    def feed(g):
        wi = held_1[g].reshape(width, hidden)
        wt = held_2[g].reshape(width, hidden)
        total = jnp.zeros((1, hidden), F32)
        bias = inner_bias[:, pl.ds(pl.multiple_of(g * hidden, LANES), hidden)]
        for start in range(0, rows_all, block):
            end = start + block
            u = nn(h2[start:end, :], wi) + bias
            below = 0.5 * (1.0 + lax.erf(u * 0.7071067811865476))
            slope = below + u * (jnp.exp(-0.5 * (u * u)) * 0.3989422804014327)
            a = (u * below).astype(BF16)
            du = (nn(cotangent[start:end, :], wt) * slope).astype(BF16)
            act[start:end, :] = a
            dhid[start:end, :] = du
            total = total + jnp.sum(du.astype(F32), axis=0, keepdims=True)
            res[start:end, :] += nt(a, wt)
            dh2[start:end, :] += nt(du, wi)
        sums[pl.ds(8 + g, 1), 0:hidden] = total

    shape = (p.inner, part_rows, hidden)

    def feed_grads(y, mine):
        for o in range(OUTER):
            for s, (left, right) in enumerate(((h2t, dhid), (cot, act))):
                lanes = slice(s * hidden, (s + 1) * hidden)
                value = nn(left[o * tall : (o + 1) * tall, :], right[...]).reshape(shape)
                if mine:
                    value = value + sf.core[y, o, :, :, lanes].astype(F32)
                    sf.core[y, o, :, :, lanes] = value.astype(BF16)
                else:
                    sf.give[y, o, :, :, lanes] = value.astype(BF16)

    for dy in range(p.ny):
        y = (p.y + dy) % p.ny
        if dy:
            g2.core_done(dy)
            g1.core_done(dy)
        feed(y * 2 + 1 - p.c)
        feed_grads(y, False)
        sf.core_send(y)
        if not dy:
            for k in range(OUTER):
                g2.corner(k)
                g1.corner(k)
        feed(y * 2 + p.c)
        sf.core_wait(y)
        feed_grads(y, True)
        if dy:
            sf.first_y(dy, 2, 0)
        else:
            for k in sf.by_i:
                sf.first_i(0, k)

    def leave(k, _):
        at = pl.ds(pl.multiple_of(k * step, step), step)
        out[at, :] = res[at, :].astype(BF16)
        n = unit[at, :]
        grad = dh2[at, :]
        e = cotangent[at, :].astype(F32)
        pushed = grad * gain2[...]
        mean = jnp.mean(pushed, axis=-1, keepdims=True)
        along = jnp.mean(pushed * n, axis=-1, keepdims=True)
        back = e + (pushed - mean - n * along) * inv[at, :]
        dr[at, :] = back
        low = back.astype(BF16)
        wide = low.astype(F32)
        dbt[:, at] = jnp.transpose(wide).astype(BF16)
        for g in range(nt_):
            do[g, at, :] = nn(low, output_weight(g))
        sums[2:3, :] += jnp.sum(grad * n, axis=0, keepdims=True)
        sums[3:4, :] += jnp.sum(grad, axis=0, keepdims=True)
        sums[4:5, :] += jnp.sum(wide, axis=0, keepdims=True)
        sums[5:6, :] += jnp.sum(e, axis=0, keepdims=True)
        return 0

    lax.fori_loop(0, rows_all // step, leave, 0)
    store_out = pltpu.make_async_copy(out, out_to, out_sems.at[0])
    store_out.start()

    def first(g, _):
        low = (do[g] * rden[g]).astype(BF16)
        gn[g] = low
        product = low.astype(F32) * mixed[g]
        left = left_lanes(product.shape)
        zero = jnp.zeros_like(product)
        one = jnp.sum(jnp.where(left, product, zero), axis=-1, keepdims=True)
        two = jnp.sum(jnp.where(left, zero, product), axis=-1, keepdims=True)
        slope = -jnp.where(left, one, two)
        gd[g] = slope
        kept = jnp.where(segc[...] == first_id, fq[g], jnp.zeros_like(low))
        total = jnp.sum(kept.astype(F32) * slope, axis=0, keepdims=True)
        xb.put(g, pack_state(tn(kept, low)), total, first_id, last_id)
        return 0

    lax.fori_loop(0, nt_, first, 0)
    xb.step_near()
    for dy in range(1, p.ny):
        for di in range(1, p.inner):
            sf.first_y(dy, 2, di)
        for k in sf.by_i:
            sf.first_i(dy, k)
    all_sum.start(sums[...])

    def inside_back(g, _):
        values, keys = vb[g], fk[g]
        key_heads = split_heads(keys, 0.0)
        packed, foot = ex.state(g)
        high, low = two_parts(wide_state(packed))
        query_t = jnp.transpose(fq[g].astype(F32)).astype(BF16)
        grad_t = jnp.transpose(gn[g].astype(F32)).astype(BF16)
        dk_t = jnp.zeros((LANES, rows_all), F32)
        dv_t = jnp.zeros((LANES, rows_all), F32)
        for start in range(0, rows_all, block):
            end = start + block
            now = mask[start:end, :end]
            query, grad = fq[g, start:end, :], gn[g, start:end, :]
            slope = gd[g, start:end, :]
            query_heads, grad_heads = split_heads(query, 0.0), split_heads(grad, 0.0)
            dq = jnp.where(
                segc[start:end, :] == first_id,
                nt(grad, high) + nt(grad, low) + slope * foot[0:1, :],
                0.0,
            )
            dk_parts, dv_parts = [], []
            for h in range(2):
                lanes = slice(h * HEAD, h * HEAD + 1)
                part = slice(h * HEAD, (h + 1) * HEAD)
                weight = nt(query_heads[h], keys[:end]).astype(BF16) * now
                share = (nt(grad_heads[h], values[:end]) + slope[:, lanes]).astype(BF16) * now
                dq = dq + nn(share, key_heads[h][:end])
                dk_parts.append(nn(query_t[part, start:end], share))
                dv_parts.append(nn(grad_t[part, start:end], weight))
            dk_now = jnp.concatenate(dk_parts, axis=0)
            dv_now = jnp.concatenate(dv_parts, axis=0)
            if end < rows_all:
                pad = jnp.zeros((LANES, rows_all - end), F32)
                dk_now = jnp.concatenate([dk_now, pad], axis=1)
                dv_now = jnp.concatenate([dv_now, pad], axis=1)
            dk_t, dv_t = dk_t + dk_now, dv_t + dv_now
            dq_s[g, start:end, :] = (dq * jnp.minimum(query.astype(F32), 1.0)).astype(BF16)
        dk_s[g] = jnp.transpose(dk_t)
        dv_s[g] = jnp.transpose(dv_t)
        return 0

    lax.fori_loop(0, nt_ // 2, inside_back, 0)
    xb.step_far()
    all_sum.plane_step()
    for k in sf.by_i:
        sf.second_i(k, 0)
    lax.fori_loop(nt_ // 2, nt_, inside_back, 0)
    for dy in range(1, p.ny):
        sf.second_i(0, dy)
    xb.step_enter()
    sf.second_y(2)
    for dy in range(1, p.ny):
        sf.second_i(1, dy)

    def attention_grads(scatter, dc, joint):
        for dy in list(range(1, p.ny)) + [0]:
            y = (p.y + dy) % p.ny
            g = y * 2 + (p.c + dc) % 2
            values = joint(g)
            if not dc:
                scatter.core_wait(y)
            for s, (left, right) in enumerate(values):
                lanes = slice(s * LANES, (s + 1) * LANES)
                value = nn(left, right).reshape(block_shape + (LANES,))
                if dc:
                    scatter.give[y, :, :, :, lanes] = value.astype(BF16)
                else:
                    value = value + scatter.core[y, :, :, :, lanes].astype(F32)
                    scatter.core[y, :, :, :, lanes] = value.astype(BF16)
            if dc:
                scatter.core_send(y)
            else:
                scatter.first(dy)

    def query_output(g):
        return ((normed_t[...], dq_s[g]), (dbt[...], mixed[g].astype(BF16)))

    attention_grads(sqo, 1, query_output)
    attention_grads(sqo, 0, query_output)
    all_sum.outer_step()

    def query_back(g, _):
        dh1[...] += nt(dq_s[g], held_qo[g, :, :, :, :LANES].reshape(width, LANES))
        return 0

    dh1[...] = jnp.zeros_like(dh1)
    lax.fori_loop(0, nt_, query_back, 0)
    for dy in range(1, p.ny):
        sf.second_i(3, dy)
    xb.arrive()

    def key_value(g):
        packed, foot = xb.state(g)
        high, low = two_parts(wide_state(packed))
        keys, values = fk[g], vb[g]
        dk = nt(values, high) + nt(values, low) + foot[0:1, :]
        dv = nn(keys, high) + nn(keys, low)
        closing = segc[...] == last_id
        dk = dk_s[g] + jnp.where(closing, dk, 0.0)
        dv = dv_s[g] + jnp.where(closing, dv, 0.0)
        dk = (dk * jnp.minimum(keys.astype(F32), 1.0)).astype(BF16)
        dv = dv.astype(BF16)
        dkv_s[g, :, :LANES] = dk
        dkv_s[g, :, LANES:] = dv
        return ((normed_t[...], dk), (normed_t[...], dv))

    attention_grads(skv, 1, key_value)
    sf.third(2)
    sf.third(1)
    attention_grads(skv, 0, key_value)
    sf.third(3)

    def key_value_back(g, _):
        dh1[...] += nt(dkv_s[g], held_kv[g].reshape(width, 2 * LANES))
        return 0

    lax.fori_loop(0, nt_, key_value_back, 0)
    first_sums[...] = jnp.zeros_like(first_sums)

    def finish(k, _):
        at = pl.ds(pl.multiple_of(k * step, step), step)
        x = tokens[at, :].astype(F32)
        center = x - jnp.mean(x, axis=-1, keepdims=True)
        spread = jnp.mean(center * center, axis=-1, keepdims=True)
        scale = lax.rsqrt(spread + EPSILON)
        n = center * scale
        grad = dh1[at, :]
        pushed = grad * gain1[...]
        mean = jnp.mean(pushed, axis=-1, keepdims=True)
        along = jnp.mean(pushed * n, axis=-1, keepdims=True)
        back = (pushed - mean - n * along) * scale
        grad_tokens[at, :] = (dr[at, :] + back).astype(BF16)
        first_sums[0:1, :] += jnp.sum(grad * n, axis=0, keepdims=True)
        first_sums[8:9, :] += jnp.sum(grad, axis=0, keepdims=True)
        return 0

    lax.fori_loop(0, rows_all // step, finish, 0)
    store_tokens = pltpu.make_async_copy(grad_tokens, tokens_to, out_sems.at[1])
    store_tokens.start()
    first_sum.start(first_sums[...])
    sqo.second()
    first_sum.plane_step()
    skv.second()
    for k in (2, 3, 1):
        sqo.third(k)
    for k in (2, 3, 1):
        skv.third(k)
    first_sum.outer_step()
    for scatter in (sf, sqo, skv):
        scatter.third(0)
    all_sum.core_step()
    total = sf.last()
    grad_1[...] = total[:, :hidden]
    grad_2[...] = total[:, hidden:]
    total = sqo.last()
    grad_q[...] = total[:, :head]
    grad_o[...] = total[:, LANES : LANES + head]
    first_sum.core_step()
    total = all_sum.result()
    grad_g2[...] = total[2:3, :]
    grad_s2[...] = total[3:4, :]
    grad_mb[...] = total[4:5, :]
    grad_ob[...] = total[5:6, :]
    for g in range(nt_):
        grad_ib[:, g * hidden : (g + 1) * hidden] = total[8 + g : 9 + g, :hidden]
    total = skv.last()
    grad_k[...] = total[:, :head]
    grad_v[...] = total[:, LANES : LANES + head]
    total = first_sum.result()
    grad_g1[...] = total[0:1, :]
    grad_s1[...] = total[8:9, :]
    store_out.wait()
    store_tokens.wait()
    for each in (kv, qo, g2, g1, ex, xb, sf, sqo, skv, all_sum, first_sum):
        each.finish()


def kernel_outputs(count, *refs):
    given, made, held = (refs[k * count : (k + 1) * count] for k in range(3))
    loaded, stored = refs[3 * count :]
    loads = [pltpu.make_async_copy(given[k], held[k], loaded.at[k]) for k in range(count)]
    stores = [pltpu.make_async_copy(held[k], made[k], stored.at[k]) for k in range(count)]
    for load in loads:
        load.start()
    for load, store in zip(loads, stores):
        load.wait()
        store.start()
    for store in stores:
        store.wait()


def local(nd, nt_, *args):
    (tokens, segments, wq, wk, wv, wo, w1, w2, inner_bias, *vectors, cotangent) = args
    rows, width = tokens.shape
    inner = nd // OUTER
    part_rows, hidden = w1.shape
    vm, hbm = (pl.BlockSpec(memory_space=space) for space in (pltpu.VMEM, pl.ANY))
    group = (nt_, rows, LANES)
    total_rows = 8 + max(8, nt_)
    head = wq.shape[1]
    row = jax.ShapeDtypeStruct((1, width), F32)
    narrow = jax.ShapeDtypeStruct((part_rows, head), F32)
    wide = jax.ShapeDtypeStruct((part_rows, hidden), F32)
    outs = [
        jax.ShapeDtypeStruct(tokens.shape, BF16),
        jax.ShapeDtypeStruct(tokens.shape, BF16),
        narrow, narrow, narrow, narrow, wide, wide,
        jax.ShapeDtypeStruct((1, nt_ * hidden), F32),
        *[row] * 6,
    ]
    held = (nt_, OUTER, inner, part_rows)
    square = (rows, width)
    scratch = [
        pltpu.VMEM(held + (2 * LANES,), BF16),
        pltpu.VMEM(held + (2 * LANES,), BF16),
        pltpu.VMEM(held + (hidden,), BF16),
        pltpu.VMEM(held + (hidden,), BF16),
        pltpu.VMEM(square, BF16),
        *[pltpu.VMEM(w.shape, F32) for w in (wq, wk, wv, wo.T, w1, w2.T)],
        pltpu.VMEM(square, BF16),
        pltpu.VMEM(square, BF16),
        pltpu.VMEM(square, BF16),
        pltpu.VMEM((rows, 1), F32),
        pltpu.VMEM((rows, rows), BF16),
        pltpu.VMEM(square, BF16),
        pltpu.VMEM((width, rows), BF16),
        pltpu.VMEM(group, BF16),
        pltpu.VMEM(group, BF16),
        pltpu.VMEM(group, BF16),
        pltpu.VMEM(group, F32),
        pltpu.VMEM(group, F32),
        pltpu.VMEM(square, F32),
        pltpu.VMEM(square, F32),
        pltpu.VMEM((rows, 1), F32),
        pltpu.VMEM(square, BF16),
        pltpu.VMEM((width, rows), BF16),
        pltpu.VMEM((width, rows), BF16),
        pltpu.VMEM(square, F32),
        pltpu.VMEM((rows, hidden), BF16),
        pltpu.VMEM((rows, hidden), BF16),
        pltpu.VMEM((width, rows), BF16),
        pltpu.VMEM(group, F32),
        pltpu.VMEM(square, F32),
        pltpu.VMEM(group, BF16),
        pltpu.VMEM(group, F32),
        pltpu.VMEM(group, F32),
        pltpu.VMEM(group, F32),
        pltpu.VMEM(group, BF16),
        pltpu.VMEM((nt_, rows, 2 * LANES), BF16),
        pltpu.VMEM(square, F32),
        pltpu.VMEM((total_rows, width), F32),
        pltpu.VMEM((16, width), F32),
    ]
    for _ in range(2):
        scratch += Exchange.scratch(nd, nt_)
    scratch += Scatter.scratch(nd, nt_, *WIDE_WAYS, part_rows, 2 * hidden)
    scratch += Scatter.scratch(nd, nt_, *EVEN_WAYS, part_rows, 2 * LANES)
    scratch += Scatter.scratch(nd, nt_, *EVEN_WAYS, part_rows, 2 * LANES)
    scratch += Total.scratch(nd, nt_, total_rows, width)
    scratch += Total.scratch(nd, nt_, 16, width)
    for _ in range(4):
        scratch += Gather.semaphores(nd, nt_)
    for _ in range(2):
        scratch += Exchange.semaphores(nd, nt_)
    for ways in (WIDE_WAYS, EVEN_WAYS, EVEN_WAYS):
        scratch += Scatter.semaphores(nd, nt_, *ways)
    for _ in range(2):
        scratch += Total.semaphores(nd, nt_)
    scratch += [pltpu.SemaphoreType.DMA((8,)), pltpu.SemaphoreType.DMA((2,))]
    operands = (
        tokens, segments[None], wq, wk, wv, wo.T, w1, w2.T, inner_bias[None],
        *[v[None] for v in vectors], cotangent,
    )
    results = pl.pallas_call(
        functools.partial(kernel_whole, nd, nt_),
        out_shape=outs,
        in_specs=[hbm, vm] + [hbm] * 6 + [vm] * 7 + [hbm],
        out_specs=[hbm, hbm] + [vm] * (len(outs) - 2),
        scratch_shapes=scratch,
        compiler_params=pltpu.CompilerParams(
            collective_id=0, has_side_effects=True, vmem_limit_bytes=VMEM_LIMIT
        ),
        name="whole_layer",
    )(*operands)
    final = pl.pallas_call(
        functools.partial(kernel_outputs, len(outs)),
        out_shape=outs,
        in_specs=[hbm] * len(outs),
        out_specs=[hbm] * len(outs),
        scratch_shapes=[pltpu.VMEM(o.shape, o.dtype) for o in outs]
        + [pltpu.SemaphoreType.DMA((len(outs),))] * 2,
        name="outputs",
    )(*results)
    return (
        *final[:5], final[5].T, final[6], final[7].T, *[v.reshape(-1) for v in final[8:]],
    )


def solution(mesh):
    rows = P(("dp", "tensor"), None)
    one, two, all_of = P("dp", "tensor"), P("tensor", "dp"), P()
    weights = (one, one, one, two, one, two)
    return jax.shard_map(
        functools.partial(local, mesh.shape["dp"], mesh.shape["tensor"]),
        mesh=mesh,
        in_specs=(rows, P("dp")) + weights + (all_of,) * 7 + (rows,),
        out_specs=(rows, rows) + weights + (all_of,) * 7,
        check_vma=False,
    )
```

```python
import functools

import jax
import jax.numpy as jnp
from jax import lax
from jax.experimental import pallas as pl
from jax.experimental.pallas import tpu as pltpu
from jax.sharding import PartitionSpec as P

HEAD = 64
LANES = 128
EPSILON = 1e-05
MESH = pl.DeviceIdType.MESH
F32 = jnp.float32
BF16 = jnp.bfloat16
OUTER = 4
KV_STRAIGHT = True
EVEN_WAYS = ((0, 1), (2, 3))
WIDE_WAYS = ((2, 0, 1), (3,))
VMEM_LIMIT = 56 << 20


def nn(a, b):
    return lax.dot_general(a, b, (((1,), (0,)), ((), ())), preferred_element_type=F32)


def nt(a, b):
    return lax.dot_general(a, b, (((1,), (1,)), ((), ())), preferred_element_type=F32)


def tn(a, b):
    return lax.dot_general(a, b, (((0,), (0,)), ((), ())), preferred_element_type=F32)


class Place:
    def __init__(self, dp_size, tensor_size):
        self.nd, self.nt = dp_size, tensor_size
        self.inner, self.ny = dp_size // OUTER, tensor_size // 2
        self.d, self.t = lax.axis_index("dp"), lax.axis_index("tensor")
        self.o, self.i = self.d // self.inner, self.d % self.inner
        self.y, self.c = self.t // 2, self.t % 2
        self.barrier = pltpu.get_barrier_semaphore()

    def at(self, do=0, di=0, dy=0, dc=0):
        o, i = (self.o + do) % OUTER, (self.i + di) % self.inner
        return self.to(o, i, (self.y + dy) % self.ny, (self.c + dc) % 2)

    def to(self, o, i, y, c):
        return (o * self.inner + i, y * 2 + c)

    def nearest(self, k):
        if k == 0:
            return self.o
        high = self.o // 2
        edge = self.o + high * (3 - 2 * self.o)
        place = k * (1 - edge) + (k // 2) * k * edge
        return place + high * (3 - 2 * place)

    def outer_peers(self):
        return [(k, 0, 0, 0) for k in range(1, OUTER)]

    def plane_peers(self):
        return [
            (0, di, dy, 0) for di in range(self.inner) for dy in range(self.ny) if di or dy
        ]

    def peers(self):
        return self.outer_peers() + [
            (0, di, dy, dc)
            for di in range(self.inner)
            for dy in range(self.ny)
            for dc in range(2)
            if di or dy or dc
        ]

    def greet(self):
        for peer in self.peers():
            pl.semaphore_signal(
                self.barrier, inc=1, device_id=self.at(*peer), device_id_type=MESH
            )

    def meet(self):
        pl.semaphore_wait(self.barrier, len(self.peers()))


def remote(src, dst, send, recv, peer):
    return pltpu.make_async_remote_copy(
        src_ref=src,
        dst_ref=dst,
        send_sem=send,
        recv_sem=recv,
        device_id=peer,
        device_id_type=MESH,
    )


class Sender:
    def __init__(self, place, send):
        self.p, self.send, self.started = place, send, []

    def go(self, src, dst, recv, peer):
        copy = remote(src, dst, self.send.at[len(self.started)], recv, peer)
        copy.start()
        self.started.append(copy)

    def got(self, block, recv):
        remote(block, block, self.send.at[0], recv, self.p.at()).wait_recv()

    def finish(self):
        for copy in self.started:
            copy.wait_send()


class Gather(Sender):
    def __init__(self, place, held, sems, straight=False):
        super().__init__(place, sems[0])
        self.held, self.straight = held, straight
        self.got_outer, self.got_i, self.got_y, self.got_d, self.got_core = sems[1:]

    def _block(self, k, i, y):
        p = self.p
        return self.held.at[y * 2 + p.c, p.nearest(k), i]

    def outer_start(self):
        p = self.p
        mine = self._block(0, p.i, p.y)
        for k in range(1, OUTER):
            to = p.to(p.nearest(k), p.i, p.y, p.c)
            self.go(mine, mine, self.got_outer.at[p.o], to)

    def spread(self, k):
        p = self.p
        block = self._block(k, p.i, p.y)
        if k:
            self.got(block, self.got_outer.at[p.nearest(k)])
        for di in range(1, p.inner):
            self.go(block, block, self.got_i.at[di - 1, k], p.at(di=di))
        for dy in range(1, p.ny):
            self.go(block, block, self.got_y.at[dy - 1, k], p.at(dy=dy))
            for di in range(1, p.inner) if self.straight else ():
                self.go(block, block, self.got_d.at[di - 1, dy - 1, k], p.at(di=di, dy=dy))
        self.go(block, block, self.got_core.at[p.y], p.at(dc=1))

    def turn(self, k):
        p = self.p
        for di in range(1, p.inner):
            block = self._block(k, (p.i + p.inner - di) % p.inner, p.y)
            self.got(block, self.got_i.at[di - 1, k])
            if k < 2 and not self.straight:
                for dy in range(1, p.ny):
                    self.go(block, block, self.got_d.at[di - 1, dy - 1, k], p.at(dy=dy))
            self.go(block, block, self.got_core.at[p.y], p.at(dc=1))
        for dy in range(1, p.ny):
            y = (p.y + p.ny - dy) % p.ny
            block = self._block(k, p.i, y)
            self.got(block, self.got_y.at[dy - 1, k])
            if k >= 2 and not self.straight:
                for di in range(1, p.inner):
                    self.go(block, block, self.got_d.at[di - 1, dy - 1, k], p.at(di=di))
            self.go(block, block, self.got_core.at[y], p.at(dc=1))

    def corner(self, k):
        p = self.p
        for di in range(1, p.inner):
            for dy in range(1, p.ny):
                y = (p.y + p.ny - dy) % p.ny
                block = self._block(k, (p.i + p.inner - di) % p.inner, y)
                self.got(block, self.got_d.at[di - 1, dy - 1, k])
                self.go(block, block, self.got_core.at[y], p.at(dc=1))

    def core_done(self, dy):
        p = self.p
        y = (p.y + dy) % p.ny
        self.got(self.held.at[y * 2 + 1 - p.c], self.got_core.at[y])

    @staticmethod
    def semaphores(nd, nt_):
        di, dy = nd // OUTER - 1, nt_ // 2 - 1
        sends = (OUTER - 1) + OUTER * (di + dy + 1 + di + dy) + 2 * OUTER * di * dy
        return [
            pltpu.SemaphoreType.DMA((sends,)),
            pltpu.SemaphoreType.DMA((OUTER,)),
            pltpu.SemaphoreType.DMA((di, OUTER)),
            pltpu.SemaphoreType.DMA((dy, OUTER)),
            pltpu.SemaphoreType.DMA((di, dy, OUTER)),
            pltpu.SemaphoreType.DMA((nt_ // 2,)),
        ]


class Scatter(Sender):
    def __init__(self, place, by_i, by_y, bufs, sems):
        super().__init__(place, sems[0])
        self.by_i, self.by_y = by_i, by_y
        (self.give, self.core, self.in_i, self.in_y, self.sum_i, self.sum_y,
         self.then_y, self.then_i, self.own, self.outer) = bufs
        self.got_core, self.got_i, self.got_y, self.got_ty, self.got_ti, self.got_outer = sems[1:]

    def core_send(self, y):
        self.go(self.give.at[y], self.core.at[y], self.got_core.at[y], self.p.at(dc=1))

    def core_wait(self, y):
        self.got(self.core.at[y], self.got_core.at[y])

    def first_i(self, dy, k):
        p, at = self.p, self.by_i.index(k)
        y, o = (p.y + dy) % p.ny, (p.o + k) % OUTER
        for di in range(1, p.inner):
            self.go(
                self.core.at[y, o, (p.i + di) % p.inner], self.in_i.at[di - 1, at, dy],
                self.got_i.at[di - 1, at, dy], p.at(di=di),
            )

    def first_y(self, dy, k, di):
        p, at = self.p, self.by_y.index(k)
        y, o, i = (p.y + dy) % p.ny, (p.o + k) % OUTER, (p.i + di) % p.inner
        self.go(
            self.core.at[y, o, i], self.in_y.at[dy - 1, at, di],
            self.got_y.at[dy - 1, at, di], p.at(dy=dy),
        )

    def first(self, dy):
        for k in self.by_y:
            for di in range(self.p.inner) if dy else ():
                self.first_y(dy, k, di)
        for k in self.by_i:
            self.first_i(dy, k)

    def second_y(self, k):
        p, at = self.p, self.by_y.index(k)
        o = (p.o + k) % OUTER
        for di in list(range(1, p.inner)) + [0]:
            total = self.core[p.y, o, (p.i + di) % p.inner].astype(F32)
            for dy in range(1, p.ny):
                block = self.in_y.at[dy - 1, at, di]
                self.got(block, self.got_y.at[dy - 1, at, di])
                total = total + block[...].astype(F32)
            self.sum_y[at, di] = total.astype(BF16)
            if di:
                self.go(
                    self.sum_y.at[at, di], self.then_i.at[di - 1, at],
                    self.got_ti.at[di - 1, at], p.at(di=di),
                )

    def second_i(self, k, dy):
        p, at = self.p, self.by_i.index(k)
        total = self.core[(p.y + dy) % p.ny, (p.o + k) % OUTER, p.i].astype(F32)
        for di in range(1, p.inner):
            block = self.in_i.at[di - 1, at, dy]
            self.got(block, self.got_i.at[di - 1, at, dy])
            total = total + block[...].astype(F32)
        self.sum_i[at, dy] = total.astype(BF16)
        if dy:
            self.go(
                self.sum_i.at[at, dy], self.then_y.at[dy - 1, at],
                self.got_ty.at[dy - 1, at], p.at(dy=dy),
            )

    def second(self):
        for k in self.by_y:
            self.second_y(k)
        for dy in list(range(1, self.p.ny)) + [0]:
            for k in self.by_i:
                self.second_i(k, dy)

    def third(self, k):
        p = self.p
        if k in self.by_i:
            at, count, place, sems = self.by_i.index(k), p.ny, self.then_y, self.got_ty
            total = self.sum_i[at, 0].astype(F32)
        else:
            at, count, place, sems = self.by_y.index(k), p.inner, self.then_i, self.got_ti
            total = self.sum_y[at, 0].astype(F32)
        for j in range(count - 1):
            self.got(place.at[j, at], sems.at[j, at])
            total = total + place[j, at].astype(F32)
        self.own[k] = total.astype(BF16)
        if k:
            self.go(self.own.at[k], self.outer.at[k - 1], self.got_outer.at[k - 1], p.at(do=k))

    def last(self):
        total = self.own[0].astype(F32)
        for k in range(1, OUTER):
            self.got(self.outer.at[k - 1], self.got_outer.at[k - 1])
            total = total + self.outer[k - 1].astype(F32)
        return total

    @staticmethod
    def scratch(nd, nt_, by_i, by_y, rows, columns):
        inner, ny = nd // OUTER, nt_ // 2
        ki, ky = len(by_i), len(by_y)
        leads = [
            (ny, OUTER, inner), (ny, OUTER, inner), (inner - 1, ki, ny), (ny - 1, ky, inner),
            (ki, ny), (ky, inner), (ny - 1, ki), (inner - 1, ky), (OUTER,), (OUTER - 1,),
        ]
        return [pltpu.VMEM(lead + (rows, columns), BF16) for lead in leads]

    @staticmethod
    def semaphores(nd, nt_, by_i, by_y):
        inner, ny = nd // OUTER, nt_ // 2
        di, dy, ki, ky = inner - 1, ny - 1, len(by_i), len(by_y)
        sends = ny + ky * dy * inner + ki * di * ny + ky * di + ki * dy + OUTER - 1
        shapes = [
            (sends,), (ny,), (di, ki, ny), (dy, ky, inner), (dy, ki), (di, ky), (OUTER - 1,),
        ]
        return [pltpu.SemaphoreType.DMA(shape) for shape in shapes]


class Exchange(Sender):
    def __init__(self, place, back, bufs, sems):
        super().__init__(place, sems[0])
        self.back = back
        self.own, self.near, self.far, self.made, self.entering = bufs
        self.s_near, self.s_far, self.s_enter = sems[1:]
        self.rows = HEAD // place.inner
        self.members = place.inner * place.nt
        self.me = place.i * place.nt + place.t

    def put(self, g, packed, total, edge, inlet):
        p = self.p
        row = lax.broadcasted_iota(jnp.int32, (8, LANES), 0)
        foot = jnp.where(row == 0, total, jnp.where(row == 1, edge, inlet))
        for sub in range(p.inner):
            self.own[g * p.inner + sub, : self.rows, :] = packed[
                sub * self.rows : (sub + 1) * self.rows
            ]
            self.own[g * p.inner + sub, self.rows :, :] = foot

    def state(self, g):
        p = self.p
        at = pl.ds(g * p.inner, p.inner)
        packed = self.entering[at, : self.rows, :].reshape(HEAD, LANES)
        return packed, self.entering[g * p.inner, self.rows :, :]

    def _peers(self):
        p = self.p
        return [
            (di, dy, dc)
            for di in range(p.inner) for dy in range(p.ny) for dc in range(2) if di or dy or dc
        ]

    def _member(self, di, dy, dc):
        p = self.p
        i, y = (p.i + p.inner - di) % p.inner, (p.y + p.ny - dy) % p.ny
        return i * p.nt + y * 2 + (p.c + dc) % 2

    def _edge(self, block):
        return block[self.rows + 1 : self.rows + 2, :]

    def _inlet(self, block):
        return block[self.rows + 2 : self.rows + 3, :]

    def _hand(self, blocks, place, sems):
        p = self.p
        for di, dy, dc in self._peers():
            to = p.at(0, di, dy, dc)
            member = (to[0] % p.inner) * p.nt + to[1]
            self.go(blocks.at[member], place.at[self.me], sems.at[self.me], to)
        place[self.me] = blocks[self.me]

    def step_near(self):
        self._hand(self.own, self.near, self.s_near)

    def step_far(self):
        p = self.p
        for peer in self._peers():
            m = self._member(*peer)
            self.got(self.near.at[m], self.s_near.at[m])
        border = self.near[0 if self.back else self.members - 1]
        total = jnp.zeros_like(border)
        for j in range(self.members):
            block = self.near[j]
            total = total + jnp.where(self._edge(block) == self._edge(border), block, 0.0)
        row = lax.broadcasted_iota(jnp.int32, total.shape, 0)
        self.far[p.o] = jnp.where(row > self.rows, border, total)
        for k in range(1, OUTER):
            o = p.nearest(k)
            self.go(self.far.at[p.o], self.far.at[p.o], self.s_far.at[p.o], p.to(o, p.i, p.y, p.c))

    def step_enter(self):
        p = self.p
        for k in range(1, OUTER):
            o = p.nearest(k)
            self.got(self.far.at[o], self.s_far.at[o])
        order = list(range(self.members))
        if self.back:
            order.reverse()
        inlet = self._inlet(self.near[order[0]])
        incoming = jnp.zeros(self.near.shape[1:], F32)
        for o in range(OUTER):
            block = self.far[o]
            ids = jnp.where(o > p.o if self.back else o < p.o, self._edge(block), -1.0)
            incoming = incoming + jnp.where(ids == inlet, block, 0.0)
        for place, j in enumerate(order):
            block = self.near[j]
            if place:
                inlet = self._inlet(block)
                incoming = jnp.where(edge == inlet, running, 0.0)
            self.made[j] = incoming
            edge = self._edge(block)
            running = block + jnp.where(edge == inlet, incoming, 0.0)
        self._hand(self.made, self.entering, self.s_enter)

    def arrive(self):
        for peer in self._peers():
            m = self._member(*peer)
            self.got(self.entering.at[m], self.s_enter.at[m])

    @staticmethod
    def scratch(nd, nt_):
        inner = nd // OUTER
        shape = (HEAD // inner + 8, LANES)
        counts = [inner * nt_, inner * nt_, OUTER, inner * nt_, inner * nt_]
        return [pltpu.VMEM((count,) + shape, F32) for count in counts]

    @staticmethod
    def semaphores(nd, nt_):
        members = nd // OUTER * nt_
        counts = [2 * (members - 1) + OUTER - 1, members, OUTER, members]
        return [pltpu.SemaphoreType.DMA((count,)) for count in counts]


def left_lanes(shape):
    return lax.broadcasted_iota(jnp.int32, shape, len(shape) - 1) < HEAD


def split_heads(block, fill):
    left = left_lanes(block.shape)
    other = jnp.full_like(block, fill)
    return jnp.where(left, block, other), jnp.where(left, other, block)


def feature(values):
    return jnp.where(values > 0.0, values + 1.0, jnp.exp(jnp.minimum(values, 0.0)))


def pack_state(product):
    left = left_lanes((HEAD, LANES))
    return jnp.where(left, product[:HEAD], product[HEAD:])


def wide_state(packed):
    left = left_lanes((HEAD, LANES))
    zero = jnp.zeros_like(packed)
    return jnp.concatenate([jnp.where(left, packed, zero), jnp.where(left, zero, packed)], axis=0)


def two_parts(values):
    high = values.astype(BF16)
    return high, (values - high.astype(F32)).astype(BF16)


def same_head():
    row = lax.broadcasted_iota(jnp.int32, (LANES, LANES), 0) < HEAD
    return row == left_lanes((LANES, LANES))


class Total(Sender):
    def __init__(self, place, bufs, sems):
        super().__init__(place, sems[0])
        self.mine, self.core, self.plane, self.outer, self.whole = bufs
        self.got_core, self.got_plane, self.got_outer, self.got_whole = sems[1:]

    def start(self, value):
        p = self.p
        self.mine[...] = value.reshape(self.mine.shape)
        self.go(self.mine.at[1 - p.c], self.core, self.got_core.at[0], p.at(dc=1))

    def plane_step(self):
        p = self.p
        self.got(self.core, self.got_core.at[0])
        here = p.i * p.ny + p.y
        self.plane[here] = self.mine[p.c] + self.core[...]
        for peer in p.plane_peers():
            self.go(
                self.plane.at[here], self.plane.at[here], self.got_plane.at[here], p.at(*peer)
            )

    def outer_step(self):
        p = self.p
        for _, di, dy, _ in p.plane_peers():
            place = (p.i + p.inner - di) % p.inner * p.ny + (p.y + p.ny - dy) % p.ny
            self.got(self.plane.at[place], self.got_plane.at[place])
        total = self.plane[0]
        for k in range(1, p.inner * p.ny):
            total = total + self.plane[k]
        self.outer[p.o] = total
        for k in range(1, OUTER):
            to = p.to(p.nearest(k), p.i, p.y, p.c)
            self.go(self.outer.at[p.o], self.outer.at[p.o], self.got_outer.at[p.o], to)

    def core_step(self):
        p = self.p
        for k in range(1, OUTER):
            o = p.nearest(k)
            self.got(self.outer.at[o], self.got_outer.at[o])
        total = self.outer[0]
        for k in range(1, OUTER):
            total = total + self.outer[k]
        self.whole[p.c] = total
        self.go(self.whole.at[p.c], self.whole.at[p.c], self.got_whole.at[p.c], p.at(dc=1))

    def result(self):
        other = 1 - self.p.c
        self.got(self.whole.at[other], self.got_whole.at[other])
        return self.whole[...].reshape(-1, self.whole.shape[-1])

    @staticmethod
    def scratch(nd, nt_, rows, columns):
        leads = [(2,), (), (nd // OUTER * (nt_ // 2),), (OUTER,), (2,)]
        return [pltpu.VMEM(lead + (rows // 2, columns), F32) for lead in leads]

    @staticmethod
    def semaphores(nd, nt_):
        plane = nd // OUTER * (nt_ // 2)
        counts = [plane + OUTER, 1, plane, OUTER, 2]
        return [pltpu.SemaphoreType.DMA((count,)) for count in counts]


def kernel_whole(
    nd, nt_,
    *refs,
):
    given, results, scratch = refs[:16], refs[16:31], refs[31:]
    it = iter(scratch)

    def take(count):
        return [next(it) for _ in range(count)]

    (held_kv, held_qo, held_2, held_1) = take(4)
    operands, made = take(16), take(15)
    (tokens, segments, wq, wk, wv, wo, w1, w2, inner_bias,
     gain1, shift1, gain2, shift2, mixer_bias, outer_bias, cotangent) = operands
    (out, grad_tokens, grad_q, grad_k, grad_v, grad_o, grad_1, grad_2,
     grad_ib, grad_g1, grad_s1, grad_g2, grad_s2, grad_mb, grad_ob) = made
    (segc, mask, normed, normed_t, fq, fk, vb, num_s, den_s) = take(9)
    (res, unit, inv, h2, h2t, cot, dh2, act, dhid, dbt) = take(10)
    (do, dr, gn, gd, dk_s, dv_s, dq_s, dkv_s, dh1, sums, first_sums) = take(11)
    bufs_x, bufs_xb = take(5), take(5)
    bufs_f, bufs_qo, bufs_kv = take(10), take(10), take(10)
    bufs_t1, bufs_t2 = take(5), take(5)
    p = Place(nd, nt_)
    kv, qo = Gather(p, held_kv, take(6), KV_STRAIGHT), Gather(p, held_qo, take(6))
    g2, g1 = Gather(p, held_2, take(6)), Gather(p, held_1, take(6))
    ex = Exchange(p, False, bufs_x, take(4))
    xb = Exchange(p, True, bufs_xb, take(4))
    sf = Scatter(p, *WIDE_WAYS, bufs_f, take(7))
    sqo = Scatter(p, *EVEN_WAYS, bufs_qo, take(7))
    skv = Scatter(p, *EVEN_WAYS, bufs_kv, take(7))
    all_sum, first_sum = Total(p, bufs_t1, take(5)), Total(p, bufs_t2, take(5))

    rows_all, width = tokens.shape
    head, hidden = wq.shape[1], w1.shape[1]
    part_rows = wq.shape[0]
    block_shape = (OUTER, p.inner, part_rows)
    step, block = 128, min(256, rows_all)

    (in_sems, out_sems) = take(2)
    p.greet()
    loads = [
        pltpu.make_async_copy(given[n], operands[n], in_sems.at[n]) for n in range(len(given))
    ]
    stores = [
        pltpu.make_async_copy(made[n], results[n], out_sems.at[n]) for n in range(len(made))
    ]
    early = (3, 4)
    for n in early + tuple(n for n in range(len(given)) if n not in early):
        loads[n].start()
    here = (p.t, p.o, p.i)
    if head < LANES:
        blank = jnp.zeros((part_rows, 2 * LANES), BF16)
        held_kv[here] = blank
        held_qo[here] = blank
    for n in early:
        loads[n].wait()
    held_kv[here + (slice(None), slice(0, head))] = wk[...].astype(BF16)
    held_kv[here + (slice(None), slice(LANES, LANES + head))] = wv[...].astype(BF16)
    p.meet()
    kv.outer_start()
    kv.spread(0)
    for n in range(len(loads) - 1):
        if n not in early:
            loads[n].wait()
    held_qo[here + (slice(None), slice(0, head))] = wq[...].astype(BF16)
    held_qo[here + (slice(None), slice(LANES, LANES + head))] = wo[...].astype(BF16)
    held_2[here] = w2[...].astype(BF16)
    held_1[here] = w1[...].astype(BF16)
    segr = segments[:, pl.ds(pl.multiple_of(p.t * rows_all, LANES), rows_all)].astype(F32)
    for start in range(0, rows_all, LANES):
        wide = jnp.broadcast_to(segr[:, start : start + LANES], (8, LANES))
        segc[start : start + LANES, :] = jnp.transpose(wide)[:, 0:1]
    first_id, last_id = segr[:, 0:1], segr[:, rows_all - 1 : rows_all]

    def norm(k, _):
        at = pl.ds(pl.multiple_of(k * step, step), step)
        x = tokens[at, :].astype(F32)
        center = x - jnp.mean(x, axis=-1, keepdims=True)
        spread = jnp.mean(center * center, axis=-1, keepdims=True)
        y = center * lax.rsqrt(spread + EPSILON) * gain1[...] + shift1[...]
        normed[at, :] = y.astype(BF16)
        normed_t[:, at] = jnp.transpose(y).astype(BF16)
        return 0

    lax.fori_loop(0, rows_all // step, norm, 0)
    for start in range(0, rows_all, 128):
        later = lax.broadcasted_iota(jnp.int32, (128, rows_all), 0) + start
        earlier = lax.broadcasted_iota(jnp.int32, (128, rows_all), 1)
        same = segc[start : start + 128, :] == segr
        mask[start : start + 128, :] = jnp.where((later >= earlier) & same, 1.0, 0.0).astype(BF16)
    for k in range(1, OUTER):
        kv.spread(k)
    qo.outer_start()
    qo.spread(0)
    g2.outer_start()
    for k in range(OUTER):
        kv.turn(k)
    for k in range(1, OUTER):
        qo.spread(k)
    g1.outer_start()
    for k in range(OUTER):
        kv.corner(k)
    g2.spread(0)
    g1.spread(0)
    for dy in range(p.ny):
        kv.core_done(dy)

    def keys_values(g, _):
        w = held_kv[g].reshape(width, 2 * LANES)
        both = nn(normed[...], w)
        keys = feature(both[:, :LANES]).astype(BF16)
        values = both[:, LANES:].astype(BF16)
        fk[g] = keys
        vb[g] = values
        kept = jnp.where(segc[...] == last_id, keys, jnp.zeros_like(keys))
        total = jnp.sum(kept.astype(F32), axis=0, keepdims=True)
        ex.put(g, pack_state(tn(kept, values)), total, last_id, first_id)
        return 0

    lax.fori_loop(0, nt_, keys_values, 0)
    ex.step_near()
    for k in range(OUTER):
        qo.turn(k)
    for k in range(1, OUTER):
        g2.spread(k)
    loads[-1].wait()
    for start in range(0, rows_all, step):
        turned = jnp.transpose(cotangent[start : start + step, :].astype(F32))
        cot[:, start : start + step] = turned.astype(BF16)
    ex.step_far()
    g1.spread(1)
    for k in range(OUTER):
        qo.corner(k)
    for dy in range(p.ny):
        qo.core_done(dy)

    def queries(g, _):
        w = held_qo[g].reshape(width, 2 * LANES)
        fq[g] = feature(nn(normed[...], w[:, :LANES])).astype(BF16)
        return 0

    lax.fori_loop(0, nt_, queries, 0)

    def inside(g, _):
        values = split_heads(vb[g], 1.0)
        for start in range(0, rows_all, block):
            end = start + block
            now = mask[start:end, :end]
            query = split_heads(fq[g, start:end, :], 0.0)
            keys = fk[g, :end, :]
            parts = []
            for h in range(2):
                scores = nt(query[h], keys).astype(BF16) * now
                parts.append(nn(scores, values[h][:end]))
            left = left_lanes(parts[0].shape)
            num_s[g, start:end, :] = jnp.where(left, parts[0], parts[1])
            den_s[g, start:end, :] = pltpu.roll(
                jnp.where(left, parts[1], parts[0]), HEAD, 1
            )
        return 0

    lax.fori_loop(0, nt_ // 2, inside, 0)
    ex.step_enter()
    for k in range(2, OUTER):
        g1.spread(k)
    for k in range(OUTER):
        g2.turn(k)
    lax.fori_loop(nt_ // 2, nt_, inside, 0)
    for k in range(2):
        g1.turn(k)
    ex.arrive()

    def outside(g, _):
        packed, foot = ex.state(g)
        high, low = two_parts(wide_state(packed))
        total = jnp.broadcast_to(jnp.transpose(foot)[:, 0:1], (LANES, LANES))
        sum_high, sum_low = two_parts(jnp.where(same_head(), total, 0.0))
        query = fq[g]
        query = jnp.where(segc[...] == first_id, query, jnp.zeros_like(query))
        num = num_s[g] + (nn(query, high) + nn(query, low))
        den = den_s[g] + (nn(query, sum_high) + nn(query, sum_low))
        inverse = 1.0 / den
        den_s[g] = inverse
        num_s[g] = num * inverse
        return 0

    lax.fori_loop(0, nt_, outside, 0)
    mixed, rden = num_s, den_s
    for k in range(2, OUTER):
        g1.turn(k)

    def output_weight(g):
        return held_qo[g, :, :, :, LANES:].reshape(width, LANES)

    def enter(k, _):
        at = pl.ds(pl.multiple_of(k * step, step), step)
        r = tokens[at, :].astype(F32) + mixer_bias[...]
        for g in range(nt_):
            r = r + nt(mixed[g, at, :].astype(BF16), output_weight(g))
        center = r - jnp.mean(r, axis=-1, keepdims=True)
        spread = jnp.mean(center * center, axis=-1, keepdims=True)
        scale = lax.rsqrt(spread + EPSILON)
        n = center * scale
        y = n * gain2[...] + shift2[...]
        res[at, :] = r + outer_bias[...]
        unit[at, :] = n
        inv[at, :] = scale
        h2[at, :] = y.astype(BF16)
        h2t[:, at] = jnp.transpose(y).astype(BF16)
        dh2[at, :] = jnp.zeros((step, width), F32)
        return 0

    lax.fori_loop(0, rows_all // step, enter, 0)
    sums[...] = jnp.zeros_like(sums)
    g2.core_done(0)
    g1.core_done(0)
    tall = width // OUTER

    def feed(g):
        wi = held_1[g].reshape(width, hidden)
        wt = held_2[g].reshape(width, hidden)
        total = jnp.zeros((1, hidden), F32)
        bias = inner_bias[:, pl.ds(pl.multiple_of(g * hidden, LANES), hidden)]
        for start in range(0, rows_all, block):
            end = start + block
            u = nn(h2[start:end, :], wi) + bias
            below = 0.5 * (1.0 + lax.erf(u * 0.7071067811865476))
            slope = below + u * (jnp.exp(-0.5 * (u * u)) * 0.3989422804014327)
            a = (u * below).astype(BF16)
            du = (nn(cotangent[start:end, :], wt) * slope).astype(BF16)
            act[start:end, :] = a
            dhid[start:end, :] = du
            total = total + jnp.sum(du.astype(F32), axis=0, keepdims=True)
            res[start:end, :] += nt(a, wt)
            dh2[start:end, :] += nt(du, wi)
        sums[pl.ds(8 + g, 1), 0:hidden] = total

    shape = (p.inner, part_rows, hidden)

    def feed_grads(y, mine):
        for o in range(OUTER):
            for s, (left, right) in enumerate(((h2t, dhid), (cot, act))):
                lanes = slice(s * hidden, (s + 1) * hidden)
                value = nn(left[o * tall : (o + 1) * tall, :], right[...]).reshape(shape)
                if mine:
                    value = value + sf.core[y, o, :, :, lanes].astype(F32)
                    sf.core[y, o, :, :, lanes] = value.astype(BF16)
                else:
                    sf.give[y, o, :, :, lanes] = value.astype(BF16)

    for dy in range(p.ny):
        y = (p.y + dy) % p.ny
        if dy:
            g2.core_done(dy)
            g1.core_done(dy)
        feed(y * 2 + 1 - p.c)
        feed_grads(y, False)
        sf.core_send(y)
        if not dy:
            for k in range(OUTER):
                g2.corner(k)
                g1.corner(k)
        feed(y * 2 + p.c)
        sf.core_wait(y)
        feed_grads(y, True)
        sf.first_i(dy, 2)
        if dy:
            sf.first_y(dy, 3, 0)
        else:
            sf.first_i(0, 0)

    def leave(k, _):
        at = pl.ds(pl.multiple_of(k * step, step), step)
        out[at, :] = res[at, :].astype(BF16)
        n = unit[at, :]
        grad = dh2[at, :]
        e = cotangent[at, :].astype(F32)
        pushed = grad * gain2[...]
        mean = jnp.mean(pushed, axis=-1, keepdims=True)
        along = jnp.mean(pushed * n, axis=-1, keepdims=True)
        back = e + (pushed - mean - n * along) * inv[at, :]
        dr[at, :] = back
        low = back.astype(BF16)
        wide = low.astype(F32)
        dbt[:, at] = jnp.transpose(wide).astype(BF16)
        for g in range(nt_):
            do[g, at, :] = nn(low, output_weight(g))
        sums[2:3, :] += jnp.sum(grad * n, axis=0, keepdims=True)
        sums[3:4, :] += jnp.sum(grad, axis=0, keepdims=True)
        sums[4:5, :] += jnp.sum(wide, axis=0, keepdims=True)
        sums[5:6, :] += jnp.sum(e, axis=0, keepdims=True)
        return 0

    lax.fori_loop(0, rows_all // step, leave, 0)
    stores[0].start()

    def first(g, _):
        low = (do[g] * rden[g]).astype(BF16)
        gn[g] = low
        product = low.astype(F32) * mixed[g]
        left = left_lanes(product.shape)
        zero = jnp.zeros_like(product)
        one = jnp.sum(jnp.where(left, product, zero), axis=-1, keepdims=True)
        two = jnp.sum(jnp.where(left, zero, product), axis=-1, keepdims=True)
        slope = -jnp.where(left, one, two)
        gd[g] = slope
        kept = jnp.where(segc[...] == first_id, fq[g], jnp.zeros_like(low))
        total = jnp.sum(kept.astype(F32) * slope, axis=0, keepdims=True)
        xb.put(g, pack_state(tn(kept, low)), total, first_id, last_id)
        return 0

    lax.fori_loop(0, nt_, first, 0)
    xb.step_near()
    for dy in range(1, p.ny):
        for k in range(2):
            sf.first_i(dy, k)
    all_sum.start(sums[...])

    def inside_back(g, _):
        values, keys = vb[g], fk[g]
        key_heads = split_heads(keys, 0.0)
        packed, foot = ex.state(g)
        high, low = two_parts(wide_state(packed))
        query_t = jnp.transpose(fq[g].astype(F32)).astype(BF16)
        grad_t = jnp.transpose(gn[g].astype(F32)).astype(BF16)
        dk_t = jnp.zeros((LANES, rows_all), F32)
        dv_t = jnp.zeros((LANES, rows_all), F32)
        for start in range(0, rows_all, block):
            end = start + block
            now = mask[start:end, :end]
            query, grad = fq[g, start:end, :], gn[g, start:end, :]
            slope = gd[g, start:end, :]
            query_heads, grad_heads = split_heads(query, 0.0), split_heads(grad, 0.0)
            dq = jnp.where(
                segc[start:end, :] == first_id,
                nt(grad, high) + nt(grad, low) + slope * foot[0:1, :],
                0.0,
            )
            dk_parts, dv_parts = [], []
            for h in range(2):
                lanes = slice(h * HEAD, h * HEAD + 1)
                part = slice(h * HEAD, (h + 1) * HEAD)
                weight = nt(query_heads[h], keys[:end]).astype(BF16) * now
                share = (nt(grad_heads[h], values[:end]) + slope[:, lanes]).astype(BF16) * now
                dq = dq + nn(share, key_heads[h][:end])
                dk_parts.append(nn(query_t[part, start:end], share))
                dv_parts.append(nn(grad_t[part, start:end], weight))
            dk_now = jnp.concatenate(dk_parts, axis=0)
            dv_now = jnp.concatenate(dv_parts, axis=0)
            if end < rows_all:
                pad = jnp.zeros((LANES, rows_all - end), F32)
                dk_now = jnp.concatenate([dk_now, pad], axis=1)
                dv_now = jnp.concatenate([dv_now, pad], axis=1)
            dk_t, dv_t = dk_t + dk_now, dv_t + dv_now
            dq_s[g, start:end, :] = (dq * jnp.minimum(query.astype(F32), 1.0)).astype(BF16)
        dk_s[g] = jnp.transpose(dk_t)
        dv_s[g] = jnp.transpose(dv_t)
        return 0

    quarter = nt_ // 4
    lax.fori_loop(0, quarter, inside_back, 0)
    for dy in range(1, p.ny):
        sf.second_i(2, dy)
        for di in range(1, p.inner):
            sf.first_y(dy, 3, di)
    lax.fori_loop(quarter, 2 * quarter, inside_back, 0)
    xb.step_far()
    all_sum.plane_step()
    sf.second_i(2, 0)
    lax.fori_loop(2 * quarter, nt_, inside_back, 0)
    xb.step_enter()
    sf.third(2)
    for dy in range(1, p.ny):
        sf.second_i(0, dy)
    sf.first_i(0, 1)

    def attention_grads(scatter, dc, joint):
        for dy in list(range(1, p.ny)) + [0]:
            y = (p.y + dy) % p.ny
            g = y * 2 + (p.c + dc) % 2
            values = joint(g)
            if not dc:
                scatter.core_wait(y)
            for s, (left, right) in enumerate(values):
                lanes = slice(s * LANES, (s + 1) * LANES)
                value = nn(left, right).reshape(block_shape + (LANES,))
                if dc:
                    scatter.give[y, :, :, :, lanes] = value.astype(BF16)
                else:
                    value = value + scatter.core[y, :, :, :, lanes].astype(F32)
                    scatter.core[y, :, :, :, lanes] = value.astype(BF16)
            if dc:
                scatter.core_send(y)
            else:
                scatter.first(dy)

    def query_output(g):
        return ((normed_t[...], dq_s[g]), (dbt[...], mixed[g].astype(BF16)))

    attention_grads(sqo, 1, query_output)
    for dy in range(1, p.ny):
        sf.second_i(1, dy)
    sf.second_y(3)
    attention_grads(sqo, 0, query_output)
    sf.second_i(0, 0)
    all_sum.outer_step()

    def query_back(g, _):
        dh1[...] += nt(dq_s[g], held_qo[g, :, :, :, :LANES].reshape(width, LANES))
        return 0

    dh1[...] = jnp.zeros_like(dh1)
    lax.fori_loop(0, nt_, query_back, 0)
    sf.second_i(1, 0)
    xb.arrive()

    def key_value(g):
        packed, foot = xb.state(g)
        high, low = two_parts(wide_state(packed))
        keys, values = fk[g], vb[g]
        dk = nt(values, high) + nt(values, low) + foot[0:1, :]
        dv = nn(keys, high) + nn(keys, low)
        closing = segc[...] == last_id
        dk = dk_s[g] + jnp.where(closing, dk, 0.0)
        dv = dv_s[g] + jnp.where(closing, dv, 0.0)
        dk = (dk * jnp.minimum(keys.astype(F32), 1.0)).astype(BF16)
        dv = dv.astype(BF16)
        dkv_s[g, :, :LANES] = dk
        dkv_s[g, :, LANES:] = dv
        return ((normed_t[...], dk), (normed_t[...], dv))

    attention_grads(skv, 1, key_value)
    sf.third(1)
    attention_grads(skv, 0, key_value)
    sf.third(3)

    def key_value_back(g, _):
        dh1[...] += nt(dkv_s[g], held_kv[g].reshape(width, 2 * LANES))
        return 0

    lax.fori_loop(0, nt_, key_value_back, 0)
    first_sums[...] = jnp.zeros_like(first_sums)

    def finish(k, _):
        at = pl.ds(pl.multiple_of(k * step, step), step)
        x = tokens[at, :].astype(F32)
        center = x - jnp.mean(x, axis=-1, keepdims=True)
        spread = jnp.mean(center * center, axis=-1, keepdims=True)
        scale = lax.rsqrt(spread + EPSILON)
        n = center * scale
        grad = dh1[at, :]
        pushed = grad * gain1[...]
        mean = jnp.mean(pushed, axis=-1, keepdims=True)
        along = jnp.mean(pushed * n, axis=-1, keepdims=True)
        back = (pushed - mean - n * along) * scale
        grad_tokens[at, :] = (dr[at, :] + back).astype(BF16)
        first_sums[0:1, :] += jnp.sum(grad * n, axis=0, keepdims=True)
        first_sums[8:9, :] += jnp.sum(grad, axis=0, keepdims=True)
        return 0

    lax.fori_loop(0, rows_all // step, finish, 0)
    stores[1].start()
    first_sum.start(first_sums[...])
    sqo.second()
    first_sum.plane_step()
    skv.second()
    for k in (2, 3, 1):
        sqo.third(k)
    first_sum.outer_step()
    for k in (2, 3, 1):
        skv.third(k)
    for scatter in (sf, sqo, skv):
        scatter.third(0)
    all_sum.core_step()
    total = sf.last()
    grad_1[...] = total[:, :hidden]
    grad_2[...] = total[:, hidden:]
    total = sqo.last()
    grad_q[...] = total[:, :head]
    grad_o[...] = total[:, LANES : LANES + head]
    first_sum.core_step()
    total = all_sum.result()
    grad_g2[...] = total[2:3, :]
    grad_s2[...] = total[3:4, :]
    grad_mb[...] = total[4:5, :]
    grad_ob[...] = total[5:6, :]
    for g in range(nt_):
        grad_ib[:, g * hidden : (g + 1) * hidden] = total[8 + g : 9 + g, :hidden]
    total = skv.last()
    grad_k[...] = total[:, :head]
    grad_v[...] = total[:, LANES : LANES + head]
    total = first_sum.result()
    grad_g1[...] = total[0:1, :]
    grad_s1[...] = total[8:9, :]
    for store in stores[2:]:
        store.start()
    for store in stores:
        store.wait()
    for each in (kv, qo, g2, g1, ex, xb, sf, sqo, skv, all_sum, first_sum):
        each.finish()


def kernel_outputs(count, *refs):
    given, made, held = (refs[k * count : (k + 1) * count] for k in range(3))
    loaded, stored = refs[3 * count :]
    loads = [pltpu.make_async_copy(given[k], held[k], loaded.at[k]) for k in range(count)]
    stores = [pltpu.make_async_copy(held[k], made[k], stored.at[k]) for k in range(count)]
    for load in loads:
        load.start()
    for load, store in zip(loads, stores):
        load.wait()
        store.start()
    for store in stores:
        store.wait()


def local(nd, nt_, *args):
    (tokens, segments, wq, wk, wv, wo, w1, w2, inner_bias, *vectors, cotangent) = args
    rows, width = tokens.shape
    inner = nd // OUTER
    part_rows, hidden = w1.shape
    hbm = pl.BlockSpec(memory_space=pl.ANY)
    group = (nt_, rows, LANES)
    total_rows = 8 + max(8, nt_)
    head = wq.shape[1]
    row = jax.ShapeDtypeStruct((1, width), F32)
    narrow = jax.ShapeDtypeStruct((part_rows, head), F32)
    wide = jax.ShapeDtypeStruct((part_rows, hidden), F32)
    outs = [
        jax.ShapeDtypeStruct(tokens.shape, BF16),
        jax.ShapeDtypeStruct(tokens.shape, BF16),
        narrow, narrow, narrow, narrow, wide, wide,
        jax.ShapeDtypeStruct((1, nt_ * hidden), F32),
        *[row] * 6,
    ]
    operands = (
        tokens, segments[None], wq, wk, wv, wo.T, w1, w2.T, inner_bias[None],
        *[v[None] for v in vectors], cotangent,
    )
    held = (nt_, OUTER, inner, part_rows)
    square = (rows, width)
    scratch = [
        pltpu.VMEM(held + (2 * LANES,), BF16),
        pltpu.VMEM(held + (2 * LANES,), BF16),
        pltpu.VMEM(held + (hidden,), BF16),
        pltpu.VMEM(held + (hidden,), BF16),
        *[pltpu.VMEM(v.shape, v.dtype) for v in operands],
        *[pltpu.VMEM(v.shape, v.dtype) for v in outs],
        pltpu.VMEM((rows, 1), F32),
        pltpu.VMEM((rows, rows), BF16),
        pltpu.VMEM(square, BF16),
        pltpu.VMEM((width, rows), BF16),
        pltpu.VMEM(group, BF16),
        pltpu.VMEM(group, BF16),
        pltpu.VMEM(group, BF16),
        pltpu.VMEM(group, F32),
        pltpu.VMEM(group, F32),
        pltpu.VMEM(square, F32),
        pltpu.VMEM(square, F32),
        pltpu.VMEM((rows, 1), F32),
        pltpu.VMEM(square, BF16),
        pltpu.VMEM((width, rows), BF16),
        pltpu.VMEM((width, rows), BF16),
        pltpu.VMEM(square, F32),
        pltpu.VMEM((rows, hidden), BF16),
        pltpu.VMEM((rows, hidden), BF16),
        pltpu.VMEM((width, rows), BF16),
        pltpu.VMEM(group, F32),
        pltpu.VMEM(square, F32),
        pltpu.VMEM(group, BF16),
        pltpu.VMEM(group, F32),
        pltpu.VMEM(group, F32),
        pltpu.VMEM(group, F32),
        pltpu.VMEM(group, BF16),
        pltpu.VMEM((nt_, rows, 2 * LANES), BF16),
        pltpu.VMEM(square, F32),
        pltpu.VMEM((total_rows, width), F32),
        pltpu.VMEM((16, width), F32),
    ]
    for _ in range(2):
        scratch += Exchange.scratch(nd, nt_)
    scratch += Scatter.scratch(nd, nt_, *WIDE_WAYS, part_rows, 2 * hidden)
    scratch += Scatter.scratch(nd, nt_, *EVEN_WAYS, part_rows, 2 * LANES)
    scratch += Scatter.scratch(nd, nt_, *EVEN_WAYS, part_rows, 2 * LANES)
    scratch += Total.scratch(nd, nt_, total_rows, width)
    scratch += Total.scratch(nd, nt_, 16, width)
    for _ in range(4):
        scratch += Gather.semaphores(nd, nt_)
    for _ in range(2):
        scratch += Exchange.semaphores(nd, nt_)
    for ways in (WIDE_WAYS, EVEN_WAYS, EVEN_WAYS):
        scratch += Scatter.semaphores(nd, nt_, *ways)
    for _ in range(2):
        scratch += Total.semaphores(nd, nt_)
    scratch += [pltpu.SemaphoreType.DMA((len(v),)) for v in (operands, outs)]
    results = pl.pallas_call(
        functools.partial(kernel_whole, nd, nt_),
        out_shape=outs,
        in_specs=[hbm] * len(operands),
        out_specs=[hbm] * len(outs),
        scratch_shapes=scratch,
        compiler_params=pltpu.CompilerParams(
            collective_id=0, has_side_effects=True, vmem_limit_bytes=VMEM_LIMIT
        ),
        name="whole_layer",
    )(*operands)
    final = pl.pallas_call(
        functools.partial(kernel_outputs, len(outs)),
        out_shape=outs,
        in_specs=[hbm] * len(outs),
        out_specs=[hbm] * len(outs),
        scratch_shapes=[pltpu.VMEM(o.shape, o.dtype) for o in outs]
        + [pltpu.SemaphoreType.DMA((len(outs),))] * 2,
        name="outputs",
    )(*results)
    return (
        *final[:5], final[5].T, final[6], final[7].T, *[v.reshape(-1) for v in final[8:]],
    )


def solution(mesh):
    rows = P(("dp", "tensor"), None)
    one, two, all_of = P("dp", "tensor"), P("tensor", "dp"), P()
    weights = (one, one, one, two, one, two)
    return jax.shard_map(
        functools.partial(local, mesh.shape["dp"], mesh.shape["tensor"]),
        mesh=mesh,
        in_specs=(rows, P("dp")) + weights + (all_of,) * 7 + (rows,),
        out_specs=(rows, rows) + weights + (all_of,) * 7,
        check_vma=False,
    )
```

```python
import functools

import jax
import jax.numpy as jnp
from jax import lax
from jax.experimental import pallas as pl
from jax.experimental.pallas import tpu as pltpu
from jax.sharding import PartitionSpec as P

HEAD = 64
LANES = 128
EPSILON = 1e-05
MESH = pl.DeviceIdType.MESH
F32 = jnp.float32
BF16 = jnp.bfloat16
OUTER = 4
KV_STRAIGHT = True
EVEN_WAYS = ((0, 1), (2, 3))
WIDE_WAYS = ((2, 0, 1), (3,))
VMEM_LIMIT = 56 << 20


def nn(a, b):
    return lax.dot_general(a, b, (((1,), (0,)), ((), ())), preferred_element_type=F32)


def nt(a, b):
    return lax.dot_general(a, b, (((1,), (1,)), ((), ())), preferred_element_type=F32)


def tn(a, b):
    return lax.dot_general(a, b, (((0,), (0,)), ((), ())), preferred_element_type=F32)


class Place:
    def __init__(self, dp_size, tensor_size):
        self.nd, self.nt = dp_size, tensor_size
        self.inner, self.ny = dp_size // OUTER, tensor_size // 2
        self.d, self.t = lax.axis_index("dp"), lax.axis_index("tensor")
        self.o, self.i = self.d // self.inner, self.d % self.inner
        self.y, self.c = self.t // 2, self.t % 2
        self.barrier = pltpu.get_barrier_semaphore()

    def at(self, do=0, di=0, dy=0, dc=0):
        o, i = (self.o + do) % OUTER, (self.i + di) % self.inner
        return self.to(o, i, (self.y + dy) % self.ny, (self.c + dc) % 2)

    def to(self, o, i, y, c):
        return (o * self.inner + i, y * 2 + c)

    def nearest(self, k):
        if k == 0:
            return self.o
        high = self.o // 2
        edge = self.o + high * (3 - 2 * self.o)
        place = k * (1 - edge) + (k // 2) * k * edge
        return place + high * (3 - 2 * place)

    def outer_peers(self):
        return [(k, 0, 0, 0) for k in range(1, OUTER)]

    def plane_peers(self):
        return [
            (0, di, dy, 0) for di in range(self.inner) for dy in range(self.ny) if di or dy
        ]

    def peers(self):
        return self.outer_peers() + [
            (0, di, dy, dc)
            for di in range(self.inner)
            for dy in range(self.ny)
            for dc in range(2)
            if di or dy or dc
        ]

    def greet(self):
        for peer in self.peers():
            pl.semaphore_signal(
                self.barrier, inc=1, device_id=self.at(*peer), device_id_type=MESH
            )

    def meet(self):
        pl.semaphore_wait(self.barrier, len(self.peers()))


def remote(src, dst, send, recv, peer):
    return pltpu.make_async_remote_copy(
        src_ref=src,
        dst_ref=dst,
        send_sem=send,
        recv_sem=recv,
        device_id=peer,
        device_id_type=MESH,
    )


class Sender:
    def __init__(self, place, send):
        self.p, self.send, self.started = place, send, []

    def go(self, src, dst, recv, peer):
        copy = remote(src, dst, self.send.at[len(self.started)], recv, peer)
        copy.start()
        self.started.append(copy)

    def got(self, block, recv):
        remote(block, block, self.send.at[0], recv, self.p.at()).wait_recv()

    def finish(self):
        for copy in self.started:
            copy.wait_send()


class Gather(Sender):
    def __init__(self, place, held, sems, straight=False):
        super().__init__(place, sems[0])
        self.held, self.straight = held, straight
        self.got_outer, self.got_i, self.got_y, self.got_d, self.got_core = sems[1:]

    def _block(self, k, i, y):
        p = self.p
        return self.held.at[y * 2 + p.c, p.nearest(k), i]

    def outer_start(self):
        p = self.p
        mine = self._block(0, p.i, p.y)
        for k in range(1, OUTER):
            to = p.to(p.nearest(k), p.i, p.y, p.c)
            self.go(mine, mine, self.got_outer.at[p.o], to)

    def spread(self, k):
        p = self.p
        block = self._block(k, p.i, p.y)
        if k:
            self.got(block, self.got_outer.at[p.nearest(k)])
        for di in range(1, p.inner):
            self.go(block, block, self.got_i.at[di - 1, k], p.at(di=di))
        for dy in range(1, p.ny):
            self.go(block, block, self.got_y.at[dy - 1, k], p.at(dy=dy))
            for di in range(1, p.inner) if self.straight else ():
                self.go(block, block, self.got_d.at[di - 1, dy - 1, k], p.at(di=di, dy=dy))
        self.go(block, block, self.got_core.at[p.y], p.at(dc=1))

    def turn(self, k):
        p = self.p
        for di in range(1, p.inner):
            block = self._block(k, (p.i + p.inner - di) % p.inner, p.y)
            self.got(block, self.got_i.at[di - 1, k])
            if k < 2 and not self.straight:
                for dy in range(1, p.ny):
                    self.go(block, block, self.got_d.at[di - 1, dy - 1, k], p.at(dy=dy))
            self.go(block, block, self.got_core.at[p.y], p.at(dc=1))
        for dy in range(1, p.ny):
            y = (p.y + p.ny - dy) % p.ny
            block = self._block(k, p.i, y)
            self.got(block, self.got_y.at[dy - 1, k])
            if k >= 2 and not self.straight:
                for di in range(1, p.inner):
                    self.go(block, block, self.got_d.at[di - 1, dy - 1, k], p.at(di=di))
            self.go(block, block, self.got_core.at[y], p.at(dc=1))

    def corner(self, k):
        p = self.p
        for di in range(1, p.inner):
            for dy in range(1, p.ny):
                y = (p.y + p.ny - dy) % p.ny
                block = self._block(k, (p.i + p.inner - di) % p.inner, y)
                self.got(block, self.got_d.at[di - 1, dy - 1, k])
                self.go(block, block, self.got_core.at[y], p.at(dc=1))

    def core_done(self, dy):
        p = self.p
        y = (p.y + dy) % p.ny
        self.got(self.held.at[y * 2 + 1 - p.c], self.got_core.at[y])

    @staticmethod
    def semaphores(nd, nt_):
        di, dy = nd // OUTER - 1, nt_ // 2 - 1
        sends = (OUTER - 1) + OUTER * (di + dy + 1 + di + dy) + 2 * OUTER * di * dy
        return [
            pltpu.SemaphoreType.DMA((sends,)),
            pltpu.SemaphoreType.DMA((OUTER,)),
            pltpu.SemaphoreType.DMA((di, OUTER)),
            pltpu.SemaphoreType.DMA((dy, OUTER)),
            pltpu.SemaphoreType.DMA((di, dy, OUTER)),
            pltpu.SemaphoreType.DMA((nt_ // 2,)),
        ]


class Scatter(Sender):
    def __init__(self, place, by_i, by_y, bufs, sems):
        super().__init__(place, sems[0])
        self.by_i, self.by_y = by_i, by_y
        (self.give, self.core, self.in_i, self.in_y, self.sum_i, self.sum_y,
         self.then_y, self.then_i, self.own, self.outer) = bufs
        self.got_core, self.got_i, self.got_y, self.got_ty, self.got_ti, self.got_outer = sems[1:]

    def core_send(self, y):
        self.go(self.give.at[y], self.core.at[y], self.got_core.at[y], self.p.at(dc=1))

    def core_wait(self, y):
        self.got(self.core.at[y], self.got_core.at[y])

    def first_i(self, dy, k):
        p, at = self.p, self.by_i.index(k)
        y, o = (p.y + dy) % p.ny, (p.o + k) % OUTER
        for di in range(1, p.inner):
            self.go(
                self.core.at[y, o, (p.i + di) % p.inner], self.in_i.at[di - 1, at, dy],
                self.got_i.at[di - 1, at, dy], p.at(di=di),
            )

    def first_y(self, dy, k, di):
        p, at = self.p, self.by_y.index(k)
        y, o, i = (p.y + dy) % p.ny, (p.o + k) % OUTER, (p.i + di) % p.inner
        self.go(
            self.core.at[y, o, i], self.in_y.at[dy - 1, at, di],
            self.got_y.at[dy - 1, at, di], p.at(dy=dy),
        )

    def first(self, dy):
        for k in self.by_y:
            for di in range(self.p.inner) if dy else ():
                self.first_y(dy, k, di)
        for k in self.by_i:
            self.first_i(dy, k)

    def second_y(self, k):
        p, at = self.p, self.by_y.index(k)
        o = (p.o + k) % OUTER
        for di in list(range(1, p.inner)) + [0]:
            total = self.core[p.y, o, (p.i + di) % p.inner].astype(F32)
            for dy in range(1, p.ny):
                block = self.in_y.at[dy - 1, at, di]
                self.got(block, self.got_y.at[dy - 1, at, di])
                total = total + block[...].astype(F32)
            self.sum_y[at, di] = total.astype(BF16)
            if di:
                self.go(
                    self.sum_y.at[at, di], self.then_i.at[di - 1, at],
                    self.got_ti.at[di - 1, at], p.at(di=di),
                )

    def second_i(self, k, dy):
        p, at = self.p, self.by_i.index(k)
        total = self.core[(p.y + dy) % p.ny, (p.o + k) % OUTER, p.i].astype(F32)
        for di in range(1, p.inner):
            block = self.in_i.at[di - 1, at, dy]
            self.got(block, self.got_i.at[di - 1, at, dy])
            total = total + block[...].astype(F32)
        self.sum_i[at, dy] = total.astype(BF16)
        if dy:
            self.go(
                self.sum_i.at[at, dy], self.then_y.at[dy - 1, at],
                self.got_ty.at[dy - 1, at], p.at(dy=dy),
            )

    def second(self):
        for k in self.by_y:
            self.second_y(k)
        for dy in list(range(1, self.p.ny)) + [0]:
            for k in self.by_i:
                self.second_i(k, dy)

    def third(self, k):
        p = self.p
        if k in self.by_i:
            at, count, place, sems = self.by_i.index(k), p.ny, self.then_y, self.got_ty
            total = self.sum_i[at, 0].astype(F32)
        else:
            at, count, place, sems = self.by_y.index(k), p.inner, self.then_i, self.got_ti
            total = self.sum_y[at, 0].astype(F32)
        for j in range(count - 1):
            self.got(place.at[j, at], sems.at[j, at])
            total = total + place[j, at].astype(F32)
        self.own[k] = total.astype(BF16)
        if k:
            self.go(self.own.at[k], self.outer.at[k - 1], self.got_outer.at[k - 1], p.at(do=k))

    def last(self):
        total = self.own[0].astype(F32)
        for k in range(1, OUTER):
            self.got(self.outer.at[k - 1], self.got_outer.at[k - 1])
            total = total + self.outer[k - 1].astype(F32)
        return total

    @staticmethod
    def scratch(nd, nt_, by_i, by_y, rows, columns):
        inner, ny = nd // OUTER, nt_ // 2
        ki, ky = len(by_i), len(by_y)
        leads = [
            (ny, OUTER, inner), (ny, OUTER, inner), (inner - 1, ki, ny), (ny - 1, ky, inner),
            (ki, ny), (ky, inner), (ny - 1, ki), (inner - 1, ky), (OUTER,), (OUTER - 1,),
        ]
        return [pltpu.VMEM(lead + (rows, columns), BF16) for lead in leads]

    @staticmethod
    def semaphores(nd, nt_, by_i, by_y):
        inner, ny = nd // OUTER, nt_ // 2
        di, dy, ki, ky = inner - 1, ny - 1, len(by_i), len(by_y)
        sends = ny + ky * dy * inner + ki * di * ny + ky * di + ki * dy + OUTER - 1
        shapes = [
            (sends,), (ny,), (di, ki, ny), (dy, ky, inner), (dy, ki), (di, ky), (OUTER - 1,),
        ]
        return [pltpu.SemaphoreType.DMA(shape) for shape in shapes]


class Exchange(Sender):
    def __init__(self, place, back, bufs, sems):
        super().__init__(place, sems[0])
        self.back = back
        self.own, self.near, self.far, self.made, self.entering = bufs
        self.s_near, self.s_far, self.s_enter = sems[1:]
        self.rows = HEAD // place.inner
        self.members = place.inner * place.nt
        self.me = place.i * place.nt + place.t

    def put(self, g, packed, total, edge, inlet):
        p = self.p
        row = lax.broadcasted_iota(jnp.int32, (8, LANES), 0)
        foot = jnp.where(row == 0, total, jnp.where(row == 1, edge, inlet))
        for sub in range(p.inner):
            self.own[g * p.inner + sub, : self.rows, :] = packed[
                sub * self.rows : (sub + 1) * self.rows
            ]
            self.own[g * p.inner + sub, self.rows :, :] = foot

    def state(self, g):
        p = self.p
        at = pl.ds(g * p.inner, p.inner)
        packed = self.entering[at, : self.rows, :].reshape(HEAD, LANES)
        return packed, self.entering[g * p.inner, self.rows :, :]

    def _peers(self):
        p = self.p
        return [
            (di, dy, dc)
            for di in range(p.inner) for dy in range(p.ny) for dc in range(2) if di or dy or dc
        ]

    def _member(self, di, dy, dc):
        p = self.p
        i, y = (p.i + p.inner - di) % p.inner, (p.y + p.ny - dy) % p.ny
        return i * p.nt + y * 2 + (p.c + dc) % 2

    def _edge(self, block):
        return block[self.rows + 1 : self.rows + 2, :]

    def _inlet(self, block):
        return block[self.rows + 2 : self.rows + 3, :]

    def _hand(self, blocks, place, sems):
        p = self.p
        for di, dy, dc in self._peers():
            to = p.at(0, di, dy, dc)
            member = (to[0] % p.inner) * p.nt + to[1]
            self.go(blocks.at[member], place.at[self.me], sems.at[self.me], to)
        place[self.me] = blocks[self.me]

    def step_near(self):
        self._hand(self.own, self.near, self.s_near)

    def step_far(self):
        p = self.p
        for peer in self._peers():
            m = self._member(*peer)
            self.got(self.near.at[m], self.s_near.at[m])
        border = self.near[0 if self.back else self.members - 1]
        total = jnp.zeros_like(border)
        for j in range(self.members):
            block = self.near[j]
            total = total + jnp.where(self._edge(block) == self._edge(border), block, 0.0)
        row = lax.broadcasted_iota(jnp.int32, total.shape, 0)
        self.far[p.o] = jnp.where(row > self.rows, border, total)
        for k in range(1, OUTER):
            o = p.nearest(k)
            self.go(self.far.at[p.o], self.far.at[p.o], self.s_far.at[p.o], p.to(o, p.i, p.y, p.c))

    def step_enter(self):
        p = self.p
        for k in range(1, OUTER):
            o = p.nearest(k)
            self.got(self.far.at[o], self.s_far.at[o])
        order = list(range(self.members))
        if self.back:
            order.reverse()
        inlet = self._inlet(self.near[order[0]])
        incoming = jnp.zeros(self.near.shape[1:], F32)
        for o in range(OUTER):
            block = self.far[o]
            ids = jnp.where(o > p.o if self.back else o < p.o, self._edge(block), -1.0)
            incoming = incoming + jnp.where(ids == inlet, block, 0.0)
        for place, j in enumerate(order):
            block = self.near[j]
            if place:
                inlet = self._inlet(block)
                incoming = jnp.where(edge == inlet, running, 0.0)
            self.made[j] = incoming
            edge = self._edge(block)
            running = block + jnp.where(edge == inlet, incoming, 0.0)
        self._hand(self.made, self.entering, self.s_enter)

    def arrive(self):
        for peer in self._peers():
            m = self._member(*peer)
            self.got(self.entering.at[m], self.s_enter.at[m])

    @staticmethod
    def scratch(nd, nt_):
        inner = nd // OUTER
        shape = (HEAD // inner + 8, LANES)
        counts = [inner * nt_, inner * nt_, OUTER, inner * nt_, inner * nt_]
        return [pltpu.VMEM((count,) + shape, F32) for count in counts]

    @staticmethod
    def semaphores(nd, nt_):
        members = nd // OUTER * nt_
        counts = [2 * (members - 1) + OUTER - 1, members, OUTER, members]
        return [pltpu.SemaphoreType.DMA((count,)) for count in counts]


def left_lanes(shape):
    return lax.broadcasted_iota(jnp.int32, shape, len(shape) - 1) < HEAD


def split_heads(block, fill):
    left = left_lanes(block.shape)
    other = jnp.full_like(block, fill)
    return jnp.where(left, block, other), jnp.where(left, other, block)


def feature(values):
    return jnp.where(values > 0.0, values + 1.0, jnp.exp(jnp.minimum(values, 0.0)))


def pack_state(product):
    left = left_lanes((HEAD, LANES))
    return jnp.where(left, product[:HEAD], product[HEAD:])


def wide_state(packed):
    left = left_lanes((HEAD, LANES))
    zero = jnp.zeros_like(packed)
    return jnp.concatenate([jnp.where(left, packed, zero), jnp.where(left, zero, packed)], axis=0)


def two_parts(values):
    high = values.astype(BF16)
    return high, (values - high.astype(F32)).astype(BF16)


def twice(values):
    return jnp.concatenate([values, values], axis=1)


def same_head():
    row = lax.broadcasted_iota(jnp.int32, (LANES, LANES), 0) < HEAD
    return row == left_lanes((LANES, LANES))


class Total(Sender):
    def __init__(self, place, bufs, sems):
        super().__init__(place, sems[0])
        self.mine, self.core, self.plane, self.outer, self.whole = bufs
        self.got_core, self.got_plane, self.got_outer, self.got_whole = sems[1:]

    def start(self, value):
        p = self.p
        self.mine[...] = value.reshape(self.mine.shape)
        self.go(self.mine.at[1 - p.c], self.core, self.got_core.at[0], p.at(dc=1))

    def plane_step(self):
        p = self.p
        self.got(self.core, self.got_core.at[0])
        here = p.i * p.ny + p.y
        self.plane[here] = self.mine[p.c] + self.core[...]
        for peer in p.plane_peers():
            self.go(
                self.plane.at[here], self.plane.at[here], self.got_plane.at[here], p.at(*peer)
            )

    def outer_step(self):
        p = self.p
        for _, di, dy, _ in p.plane_peers():
            place = (p.i + p.inner - di) % p.inner * p.ny + (p.y + p.ny - dy) % p.ny
            self.got(self.plane.at[place], self.got_plane.at[place])
        total = self.plane[0]
        for k in range(1, p.inner * p.ny):
            total = total + self.plane[k]
        self.outer[p.o] = total
        for k in range(1, OUTER):
            to = p.to(p.nearest(k), p.i, p.y, p.c)
            self.go(self.outer.at[p.o], self.outer.at[p.o], self.got_outer.at[p.o], to)

    def core_step(self):
        p = self.p
        for k in range(1, OUTER):
            o = p.nearest(k)
            self.got(self.outer.at[o], self.got_outer.at[o])
        total = self.outer[0]
        for k in range(1, OUTER):
            total = total + self.outer[k]
        self.whole[p.c] = total
        self.go(self.whole.at[p.c], self.whole.at[p.c], self.got_whole.at[p.c], p.at(dc=1))

    def result(self):
        other = 1 - self.p.c
        self.got(self.whole.at[other], self.got_whole.at[other])
        return self.whole[...].reshape(-1, self.whole.shape[-1])

    @staticmethod
    def scratch(nd, nt_, rows, columns):
        leads = [(2,), (), (nd // OUTER * (nt_ // 2),), (OUTER,), (2,)]
        return [pltpu.VMEM(lead + (rows // 2, columns), F32) for lead in leads]

    @staticmethod
    def semaphores(nd, nt_):
        plane = nd // OUTER * (nt_ // 2)
        counts = [plane + OUTER, 1, plane, OUTER, 2]
        return [pltpu.SemaphoreType.DMA((count,)) for count in counts]


def kernel_whole(
    nd, nt_,
    *refs,
):
    given, results, scratch = refs[:16], refs[16:31], refs[31:]
    it = iter(scratch)

    def take(count):
        return [next(it) for _ in range(count)]

    (held_kv, held_qo, held_2, held_1) = take(4)
    operands, made = take(16), take(15)
    (tokens, segments, wq, wk, wv, wo, w1, w2, inner_bias,
     gain1, shift1, gain2, shift2, mixer_bias, outer_bias, cotangent) = operands
    (out, grad_tokens, grad_q, grad_k, grad_v, grad_o, grad_1, grad_2,
     grad_ib, grad_g1, grad_s1, grad_g2, grad_s2, grad_mb, grad_ob) = made
    (segc, mask, normed, normed_t, fq, fk, vb, num_s, den_s) = take(9)
    (res, unit, inv, h2, h2t, cot, dh2, act, dhid, dbt) = take(10)
    (do, dr, gn, gd, dk_s, dv_s, dq_s, dkv_s, dh1, sums, first_sums) = take(11)
    bufs_x, bufs_xb = take(5), take(5)
    bufs_f, bufs_qo, bufs_kv = take(10), take(10), take(10)
    bufs_t1, bufs_t2 = take(5), take(5)
    p = Place(nd, nt_)
    kv, qo = Gather(p, held_kv, take(6), KV_STRAIGHT), Gather(p, held_qo, take(6))
    g2, g1 = Gather(p, held_2, take(6)), Gather(p, held_1, take(6))
    ex = Exchange(p, False, bufs_x, take(4))
    xb = Exchange(p, True, bufs_xb, take(4))
    sf = Scatter(p, *WIDE_WAYS, bufs_f, take(7))
    sqo = Scatter(p, *EVEN_WAYS, bufs_qo, take(7))
    skv = Scatter(p, *EVEN_WAYS, bufs_kv, take(7))
    all_sum, first_sum = Total(p, bufs_t1, take(5)), Total(p, bufs_t2, take(5))

    rows_all, width = tokens.shape
    head, hidden = wq.shape[1], w1.shape[1]
    part_rows = wq.shape[0]
    block_shape = (OUTER, p.inner, part_rows)
    step, block = 128, min(256, rows_all)

    (in_sems, out_sems) = take(2)
    p.greet()
    loads = [
        pltpu.make_async_copy(given[n], operands[n], in_sems.at[n]) for n in range(len(given))
    ]
    stores = [
        pltpu.make_async_copy(made[n], results[n], out_sems.at[n]) for n in range(len(made))
    ]
    early = (3, 4)
    for n in early + tuple(n for n in range(len(given)) if n not in early):
        loads[n].start()
    here = (p.t, p.o, p.i)
    if head < LANES:
        blank = jnp.zeros((part_rows, 2 * LANES), BF16)
        held_kv[here] = blank
        held_qo[here] = blank
    for n in early:
        loads[n].wait()
    held_kv[here + (slice(None), slice(0, head))] = wk[...].astype(BF16)
    held_kv[here + (slice(None), slice(LANES, LANES + head))] = wv[...].astype(BF16)
    p.meet()
    kv.outer_start()
    kv.spread(0)
    for n in range(len(loads) - 1):
        if n not in early:
            loads[n].wait()
    held_qo[here + (slice(None), slice(0, head))] = wq[...].astype(BF16)
    held_qo[here + (slice(None), slice(LANES, LANES + head))] = wo[...].astype(BF16)
    held_2[here] = w2[...].astype(BF16)
    held_1[here] = w1[...].astype(BF16)
    segr = segments[:, pl.ds(pl.multiple_of(p.t * rows_all, LANES), rows_all)].astype(F32)
    for start in range(0, rows_all, LANES):
        wide = jnp.broadcast_to(segr[:, start : start + LANES], (8, LANES))
        segc[start : start + LANES, :] = jnp.transpose(wide)[:, 0:1]
    first_id, last_id = segr[:, 0:1], segr[:, rows_all - 1 : rows_all]

    def norm(k, _):
        at = pl.ds(pl.multiple_of(k * step, step), step)
        x = tokens[at, :].astype(F32)
        center = x - jnp.mean(x, axis=-1, keepdims=True)
        spread = jnp.mean(center * center, axis=-1, keepdims=True)
        y = center * lax.rsqrt(spread + EPSILON) * gain1[...] + shift1[...]
        normed[at, :] = y.astype(BF16)
        normed_t[:, at] = jnp.transpose(y).astype(BF16)
        return 0

    lax.fori_loop(0, rows_all // step, norm, 0)
    for start in range(0, rows_all, 128):
        later = lax.broadcasted_iota(jnp.int32, (128, rows_all), 0) + start
        earlier = lax.broadcasted_iota(jnp.int32, (128, rows_all), 1)
        same = segc[start : start + 128, :] == segr
        mask[start : start + 128, :] = jnp.where((later >= earlier) & same, 1.0, 0.0).astype(BF16)
    for k in range(1, OUTER):
        kv.spread(k)
    qo.outer_start()
    qo.spread(0)
    g2.outer_start()
    def keys_values(g):
        w = held_kv[g].reshape(width, 2 * LANES)
        both = nn(normed[...], w)
        keys = feature(both[:, :LANES]).astype(BF16)
        values = both[:, LANES:].astype(BF16)
        fk[g] = keys
        vb[g] = values
        kept = jnp.where(segc[...] == last_id, keys, jnp.zeros_like(keys))
        total = jnp.sum(kept.astype(F32), axis=0, keepdims=True)
        ex.put(g, pack_state(tn(kept, values)), total, last_id, first_id)

    def columns(dy, dc):
        return (p.y + dy) % p.ny * 2 + (p.c + dc) % 2

    for k in range(OUTER):
        kv.turn(k)
    for k in range(1, OUTER):
        qo.spread(k)
    g1.outer_start()
    keys_values(columns(0, 0))
    for k in range(OUTER):
        kv.corner(k)
    g2.spread(0)
    g1.spread(0)
    for dy in range(1, p.ny):
        keys_values(columns(dy, 0))
    for dy in range(p.ny):
        kv.core_done(dy)
        keys_values(columns(dy, 1))

    def queries(g):
        w = held_qo[g].reshape(width, 2 * LANES)
        fq[g] = feature(nn(normed[...], w[:, :LANES])).astype(BF16)

    ex.step_near()
    for k in range(OUTER):
        qo.turn(k)
    queries(columns(0, 0))
    for k in range(1, OUTER):
        g2.spread(k)
    loads[-1].wait()
    for start in range(0, rows_all, step):
        turned = jnp.transpose(cotangent[start : start + step, :].astype(F32))
        cot[:, start : start + step] = turned.astype(BF16)
    ex.step_far()
    g1.spread(1)
    for k in range(OUTER):
        qo.corner(k)
    for dy in range(1, p.ny):
        queries(columns(dy, 0))
    for dy in range(p.ny):
        qo.core_done(dy)
        queries(columns(dy, 1))


    def inside(g, _):
        values = split_heads(vb[g], 1.0)
        for start in range(0, rows_all, block):
            end = start + block
            now = mask[start:end, :end]
            query = split_heads(fq[g, start:end, :], 0.0)
            keys = fk[g, :end, :]
            parts = []
            for h in range(2):
                scores = nt(query[h], keys).astype(BF16) * now
                parts.append(nn(scores, values[h][:end]))
            left = left_lanes(parts[0].shape)
            num_s[g, start:end, :] = jnp.where(left, parts[0], parts[1])
            den_s[g, start:end, :] = pltpu.roll(
                jnp.where(left, parts[1], parts[0]), HEAD, 1
            )
        return 0

    lax.fori_loop(0, nt_ // 2, inside, 0)
    ex.step_enter()
    for k in range(2, OUTER):
        g1.spread(k)
    for k in range(OUTER):
        g2.turn(k)
    lax.fori_loop(nt_ // 2, nt_, inside, 0)
    for k in range(2):
        g1.turn(k)
    ex.arrive()

    def outside(g, _):
        packed, foot = ex.state(g)
        total = jnp.broadcast_to(jnp.transpose(foot)[:, 0:1], (LANES, LANES))
        total = jnp.where(same_head(), total, 0.0)
        parts = two_parts(jnp.concatenate([wide_state(packed), total], axis=1))
        query = fq[g]
        query = jnp.where(segc[...] == first_id, query, jnp.zeros_like(query))
        carried = nn(twice(query), jnp.concatenate(parts, axis=0))
        num = num_s[g] + carried[:, :LANES]
        den = den_s[g] + carried[:, LANES:]
        inverse = 1.0 / den
        den_s[g] = inverse
        num_s[g] = num * inverse
        return 0

    lax.fori_loop(0, nt_, outside, 0)
    mixed, rden = num_s, den_s
    for k in range(2, OUTER):
        g1.turn(k)

    def output_weight():
        parts = [held_qo[g, :, :, :, LANES:].reshape(width, LANES) for g in range(nt_)]
        return jnp.concatenate(parts, axis=1)

    def enter(k, _):
        at = pl.ds(pl.multiple_of(k * step, step), step)
        low = jnp.concatenate([mixed[g, at, :].astype(BF16) for g in range(nt_)], axis=1)
        r = tokens[at, :].astype(F32) + mixer_bias[...] + nt(low, output_weight())
        center = r - jnp.mean(r, axis=-1, keepdims=True)
        spread = jnp.mean(center * center, axis=-1, keepdims=True)
        scale = lax.rsqrt(spread + EPSILON)
        n = center * scale
        y = n * gain2[...] + shift2[...]
        res[at, :] = r + outer_bias[...]
        unit[at, :] = n
        inv[at, :] = scale
        h2[at, :] = y.astype(BF16)
        h2t[:, at] = jnp.transpose(y).astype(BF16)
        dh2[at, :] = jnp.zeros((step, width), F32)
        return 0

    lax.fori_loop(0, rows_all // step, enter, 0)
    sums[...] = jnp.zeros_like(sums)
    g2.core_done(0)
    g1.core_done(0)
    tall = width // OUTER

    def feed(g):
        wi = held_1[g].reshape(width, hidden)
        wt = held_2[g].reshape(width, hidden)
        total = jnp.zeros((1, hidden), F32)
        bias = inner_bias[:, pl.ds(pl.multiple_of(g * hidden, LANES), hidden)]
        for start in range(0, rows_all, block):
            end = start + block
            u = nn(h2[start:end, :], wi) + bias
            below = 0.5 * (1.0 + lax.erf(u * 0.7071067811865476))
            slope = below + u * (jnp.exp(-0.5 * (u * u)) * 0.3989422804014327)
            a = (u * below).astype(BF16)
            du = (nn(cotangent[start:end, :], wt) * slope).astype(BF16)
            act[start:end, :] = a
            dhid[start:end, :] = du
            total = total + jnp.sum(du.astype(F32), axis=0, keepdims=True)
            res[start:end, :] += nt(a, wt)
            dh2[start:end, :] += nt(du, wi)
        sums[pl.ds(8 + g, 1), 0:hidden] = total

    shape = (p.inner, part_rows, hidden)

    def feed_grads(y, mine):
        for o in range(OUTER):
            for s, (left, right) in enumerate(((h2t, dhid), (cot, act))):
                lanes = slice(s * hidden, (s + 1) * hidden)
                value = nn(left[o * tall : (o + 1) * tall, :], right[...]).reshape(shape)
                if mine:
                    value = value + sf.core[y, o, :, :, lanes].astype(F32)
                    sf.core[y, o, :, :, lanes] = value.astype(BF16)
                else:
                    sf.give[y, o, :, :, lanes] = value.astype(BF16)

    for dy in range(p.ny):
        y = (p.y + dy) % p.ny
        if dy:
            g2.core_done(dy)
            g1.core_done(dy)
        feed(y * 2 + 1 - p.c)
        feed_grads(y, False)
        sf.core_send(y)
        if not dy:
            for k in range(OUTER):
                g2.corner(k)
                g1.corner(k)
        feed(y * 2 + p.c)
        sf.core_wait(y)
        feed_grads(y, True)
        sf.first_i(dy, 2)
        if dy:
            sf.first_y(dy, 3, 0)
        else:
            sf.first_i(0, 0)

    def leave(k, _):
        at = pl.ds(pl.multiple_of(k * step, step), step)
        out[at, :] = res[at, :].astype(BF16)
        n = unit[at, :]
        grad = dh2[at, :]
        e = cotangent[at, :].astype(F32)
        pushed = grad * gain2[...]
        mean = jnp.mean(pushed, axis=-1, keepdims=True)
        along = jnp.mean(pushed * n, axis=-1, keepdims=True)
        back = e + (pushed - mean - n * along) * inv[at, :]
        dr[at, :] = back
        low = back.astype(BF16)
        wide = low.astype(F32)
        dbt[:, at] = jnp.transpose(wide).astype(BF16)
        pulled = nn(low, output_weight())
        for g in range(nt_):
            do[g, at, :] = pulled[:, g * LANES : (g + 1) * LANES]
        sums[2:3, :] += jnp.sum(grad * n, axis=0, keepdims=True)
        sums[3:4, :] += jnp.sum(grad, axis=0, keepdims=True)
        sums[4:5, :] += jnp.sum(wide, axis=0, keepdims=True)
        sums[5:6, :] += jnp.sum(e, axis=0, keepdims=True)
        return 0

    lax.fori_loop(0, rows_all // step, leave, 0)
    stores[0].start()

    def first(g, _):
        low = (do[g] * rden[g]).astype(BF16)
        gn[g] = low
        product = jnp.concatenate(two_parts(low.astype(F32) * mixed[g]), axis=1)
        minus = jnp.where(same_head(), -1.0, 0.0).astype(BF16)
        slope = nn(product, jnp.concatenate([minus, minus], axis=0))
        gd[g] = slope
        kept = jnp.where(segc[...] == first_id, fq[g], jnp.zeros_like(low))
        total = jnp.sum(kept.astype(F32) * slope, axis=0, keepdims=True)
        xb.put(g, pack_state(tn(kept, low)), total, first_id, last_id)
        return 0

    lax.fori_loop(0, nt_, first, 0)
    xb.step_near()
    for dy in range(1, p.ny):
        for k in range(2):
            sf.first_i(dy, k)
    all_sum.start(sums[...])

    def inside_back(g, _):
        values, keys = vb[g], fk[g]
        key_heads = split_heads(keys, 0.0)
        packed, foot = ex.state(g)
        state = jnp.concatenate(two_parts(wide_state(packed)), axis=1)
        query_t = jnp.transpose(fq[g].astype(F32)).astype(BF16)
        grad_t = jnp.transpose(gn[g].astype(F32)).astype(BF16)
        dk_t = jnp.zeros((LANES, rows_all), F32)
        dv_t = jnp.zeros((LANES, rows_all), F32)
        for start in range(0, rows_all, block):
            end = start + block
            now = mask[start:end, :end]
            query, grad = fq[g, start:end, :], gn[g, start:end, :]
            slope = gd[g, start:end, :]
            query_heads, grad_heads = split_heads(query, 0.0), split_heads(grad, 0.0)
            dq = jnp.where(
                segc[start:end, :] == first_id,
                nt(twice(grad), state) + slope * foot[0:1, :],
                0.0,
            )
            dk_parts, dv_parts = [], []
            for h in range(2):
                lanes = slice(h * HEAD, h * HEAD + 1)
                part = slice(h * HEAD, (h + 1) * HEAD)
                weight = nt(query_heads[h], keys[:end]).astype(BF16) * now
                share = (nt(grad_heads[h], values[:end]) + slope[:, lanes]).astype(BF16) * now
                dq = dq + nn(share, key_heads[h][:end])
                dk_parts.append(nn(query_t[part, start:end], share))
                dv_parts.append(nn(grad_t[part, start:end], weight))
            dk_now = jnp.concatenate(dk_parts, axis=0)
            dv_now = jnp.concatenate(dv_parts, axis=0)
            if end < rows_all:
                pad = jnp.zeros((LANES, rows_all - end), F32)
                dk_now = jnp.concatenate([dk_now, pad], axis=1)
                dv_now = jnp.concatenate([dv_now, pad], axis=1)
            dk_t, dv_t = dk_t + dk_now, dv_t + dv_now
            dq_s[g, start:end, :] = (dq * jnp.minimum(query.astype(F32), 1.0)).astype(BF16)
        dk_s[g] = jnp.transpose(dk_t)
        dv_s[g] = jnp.transpose(dv_t)
        return 0

    quarter = nt_ // 4
    lax.fori_loop(0, quarter, inside_back, 0)
    for dy in range(1, p.ny):
        sf.second_i(2, dy)
        for di in range(1, p.inner):
            sf.first_y(dy, 3, di)
    lax.fori_loop(quarter, 2 * quarter, inside_back, 0)
    xb.step_far()
    all_sum.plane_step()
    sf.second_i(2, 0)
    lax.fori_loop(2 * quarter, nt_, inside_back, 0)
    xb.step_enter()
    sf.third(2)
    for dy in range(1, p.ny):
        sf.second_i(0, dy)
    sf.first_i(0, 1)

    def attention_grads(scatter, dc, joint):
        for dy in list(range(1, p.ny)) + [0]:
            y = (p.y + dy) % p.ny
            g = y * 2 + (p.c + dc) % 2
            values = joint(g)
            if not dc:
                scatter.core_wait(y)
            for s, (left, right) in enumerate(values):
                lanes = slice(s * LANES, (s + 1) * LANES)
                value = nn(left, right).reshape(block_shape + (LANES,))
                if dc:
                    scatter.give[y, :, :, :, lanes] = value.astype(BF16)
                else:
                    value = value + scatter.core[y, :, :, :, lanes].astype(F32)
                    scatter.core[y, :, :, :, lanes] = value.astype(BF16)
            if dc:
                scatter.core_send(y)
            else:
                scatter.first(dy)

    def query_output(g):
        return ((normed_t[...], dq_s[g]), (dbt[...], mixed[g].astype(BF16)))

    attention_grads(sqo, 1, query_output)
    for dy in range(1, p.ny):
        sf.second_i(1, dy)
    sf.second_y(3)
    attention_grads(sqo, 0, query_output)
    sf.second_i(0, 0)
    all_sum.outer_step()

    def query_back(g, _):
        dh1[...] += nt(dq_s[g], held_qo[g, :, :, :, :LANES].reshape(width, LANES))
        return 0

    dh1[...] = jnp.zeros_like(dh1)
    lax.fori_loop(0, nt_, query_back, 0)
    sf.second_i(1, 0)
    xb.arrive()

    def key_value(g):
        packed, foot = xb.state(g)
        parts = two_parts(wide_state(packed))
        keys, values = fk[g], vb[g]
        dk = nt(twice(values), jnp.concatenate(parts, axis=1)) + foot[0:1, :]
        dv = nn(twice(keys), jnp.concatenate(parts, axis=0))
        closing = segc[...] == last_id
        dk = dk_s[g] + jnp.where(closing, dk, 0.0)
        dv = dv_s[g] + jnp.where(closing, dv, 0.0)
        dk = (dk * jnp.minimum(keys.astype(F32), 1.0)).astype(BF16)
        dv = dv.astype(BF16)
        dkv_s[g, :, :LANES] = dk
        dkv_s[g, :, LANES:] = dv
        return ((normed_t[...], dk), (normed_t[...], dv))

    attention_grads(skv, 1, key_value)
    sf.third(1)
    attention_grads(skv, 0, key_value)
    sf.third(3)

    def key_value_back(g, _):
        dh1[...] += nt(dkv_s[g], held_kv[g].reshape(width, 2 * LANES))
        return 0

    lax.fori_loop(0, nt_, key_value_back, 0)
    first_sums[...] = jnp.zeros_like(first_sums)

    def finish(k, _):
        at = pl.ds(pl.multiple_of(k * step, step), step)
        x = tokens[at, :].astype(F32)
        center = x - jnp.mean(x, axis=-1, keepdims=True)
        spread = jnp.mean(center * center, axis=-1, keepdims=True)
        scale = lax.rsqrt(spread + EPSILON)
        n = center * scale
        grad = dh1[at, :]
        pushed = grad * gain1[...]
        mean = jnp.mean(pushed, axis=-1, keepdims=True)
        along = jnp.mean(pushed * n, axis=-1, keepdims=True)
        back = (pushed - mean - n * along) * scale
        grad_tokens[at, :] = (dr[at, :] + back).astype(BF16)
        first_sums[0:1, :] += jnp.sum(grad * n, axis=0, keepdims=True)
        first_sums[8:9, :] += jnp.sum(grad, axis=0, keepdims=True)
        return 0

    lax.fori_loop(0, rows_all // step, finish, 0)
    stores[1].start()
    first_sum.start(first_sums[...])
    sqo.second()
    first_sum.plane_step()
    skv.second()
    for k in (2, 3, 1):
        sqo.third(k)
    first_sum.outer_step()
    for k in (2, 3, 1):
        skv.third(k)
    for scatter in (sf, sqo, skv):
        scatter.third(0)
    all_sum.core_step()
    total = sf.last()
    grad_1[...] = total[:, :hidden]
    grad_2[...] = total[:, hidden:]
    total = sqo.last()
    grad_q[...] = total[:, :head]
    grad_o[...] = total[:, LANES : LANES + head]
    first_sum.core_step()
    total = all_sum.result()
    grad_g2[...] = total[2:3, :]
    grad_s2[...] = total[3:4, :]
    grad_mb[...] = total[4:5, :]
    grad_ob[...] = total[5:6, :]
    for g in range(nt_):
        grad_ib[:, g * hidden : (g + 1) * hidden] = total[8 + g : 9 + g, :hidden]
    total = skv.last()
    grad_k[...] = total[:, :head]
    grad_v[...] = total[:, LANES : LANES + head]
    total = first_sum.result()
    grad_g1[...] = total[0:1, :]
    grad_s1[...] = total[8:9, :]
    for store in stores[2:]:
        store.start()
    for store in stores:
        store.wait()
    for each in (kv, qo, g2, g1, ex, xb, sf, sqo, skv, all_sum, first_sum):
        each.finish()


def kernel_outputs(count, *refs):
    given, made, held = (refs[k * count : (k + 1) * count] for k in range(3))
    loaded, stored = refs[3 * count :]
    loads = [pltpu.make_async_copy(given[k], held[k], loaded.at[k]) for k in range(count)]
    stores = [pltpu.make_async_copy(held[k], made[k], stored.at[k]) for k in range(count)]
    for load in loads:
        load.start()
    for load, store in zip(loads, stores):
        load.wait()
        store.start()
    for store in stores:
        store.wait()


def local(nd, nt_, *args):
    (tokens, segments, wq, wk, wv, wo, w1, w2, inner_bias, *vectors, cotangent) = args
    rows, width = tokens.shape
    inner = nd // OUTER
    part_rows, hidden = w1.shape
    hbm = pl.BlockSpec(memory_space=pl.ANY)
    group = (nt_, rows, LANES)
    total_rows = 8 + max(8, nt_)
    head = wq.shape[1]
    row = jax.ShapeDtypeStruct((1, width), F32)
    narrow = jax.ShapeDtypeStruct((part_rows, head), F32)
    wide = jax.ShapeDtypeStruct((part_rows, hidden), F32)
    outs = [
        jax.ShapeDtypeStruct(tokens.shape, BF16),
        jax.ShapeDtypeStruct(tokens.shape, BF16),
        narrow, narrow, narrow, narrow, wide, wide,
        jax.ShapeDtypeStruct((1, nt_ * hidden), F32),
        *[row] * 6,
    ]
    operands = (
        tokens, segments[None], wq, wk, wv, wo.T, w1, w2.T, inner_bias[None],
        *[v[None] for v in vectors], cotangent,
    )
    held = (nt_, OUTER, inner, part_rows)
    square = (rows, width)
    scratch = [
        pltpu.VMEM(held + (2 * LANES,), BF16),
        pltpu.VMEM(held + (2 * LANES,), BF16),
        pltpu.VMEM(held + (hidden,), BF16),
        pltpu.VMEM(held + (hidden,), BF16),
        *[pltpu.VMEM(v.shape, v.dtype) for v in operands],
        *[pltpu.VMEM(v.shape, v.dtype) for v in outs],
        pltpu.VMEM((rows, 1), F32),
        pltpu.VMEM((rows, rows), BF16),
        pltpu.VMEM(square, BF16),
        pltpu.VMEM((width, rows), BF16),
        pltpu.VMEM(group, BF16),
        pltpu.VMEM(group, BF16),
        pltpu.VMEM(group, BF16),
        pltpu.VMEM(group, F32),
        pltpu.VMEM(group, F32),
        pltpu.VMEM(square, F32),
        pltpu.VMEM(square, F32),
        pltpu.VMEM((rows, 1), F32),
        pltpu.VMEM(square, BF16),
        pltpu.VMEM((width, rows), BF16),
        pltpu.VMEM((width, rows), BF16),
        pltpu.VMEM(square, F32),
        pltpu.VMEM((rows, hidden), BF16),
        pltpu.VMEM((rows, hidden), BF16),
        pltpu.VMEM((width, rows), BF16),
        pltpu.VMEM(group, F32),
        pltpu.VMEM(square, F32),
        pltpu.VMEM(group, BF16),
        pltpu.VMEM(group, F32),
        pltpu.VMEM(group, F32),
        pltpu.VMEM(group, F32),
        pltpu.VMEM(group, BF16),
        pltpu.VMEM((nt_, rows, 2 * LANES), BF16),
        pltpu.VMEM(square, F32),
        pltpu.VMEM((total_rows, width), F32),
        pltpu.VMEM((16, width), F32),
    ]
    for _ in range(2):
        scratch += Exchange.scratch(nd, nt_)
    scratch += Scatter.scratch(nd, nt_, *WIDE_WAYS, part_rows, 2 * hidden)
    scratch += Scatter.scratch(nd, nt_, *EVEN_WAYS, part_rows, 2 * LANES)
    scratch += Scatter.scratch(nd, nt_, *EVEN_WAYS, part_rows, 2 * LANES)
    scratch += Total.scratch(nd, nt_, total_rows, width)
    scratch += Total.scratch(nd, nt_, 16, width)
    for _ in range(4):
        scratch += Gather.semaphores(nd, nt_)
    for _ in range(2):
        scratch += Exchange.semaphores(nd, nt_)
    for ways in (WIDE_WAYS, EVEN_WAYS, EVEN_WAYS):
        scratch += Scatter.semaphores(nd, nt_, *ways)
    for _ in range(2):
        scratch += Total.semaphores(nd, nt_)
    scratch += [pltpu.SemaphoreType.DMA((len(v),)) for v in (operands, outs)]
    results = pl.pallas_call(
        functools.partial(kernel_whole, nd, nt_),
        out_shape=outs,
        in_specs=[hbm] * len(operands),
        out_specs=[hbm] * len(outs),
        scratch_shapes=scratch,
        compiler_params=pltpu.CompilerParams(
            collective_id=0, has_side_effects=True, vmem_limit_bytes=VMEM_LIMIT
        ),
        name="whole_layer",
    )(*operands)
    final = pl.pallas_call(
        functools.partial(kernel_outputs, len(outs)),
        out_shape=outs,
        in_specs=[hbm] * len(outs),
        out_specs=[hbm] * len(outs),
        scratch_shapes=[pltpu.VMEM(o.shape, o.dtype) for o in outs]
        + [pltpu.SemaphoreType.DMA((len(outs),))] * 2,
        name="outputs",
    )(*results)
    return (
        *final[:5], final[5].T, final[6], final[7].T, *[v.reshape(-1) for v in final[8:]],
    )


def solution(mesh):
    rows = P(("dp", "tensor"), None)
    one, two, all_of = P("dp", "tensor"), P("tensor", "dp"), P()
    weights = (one, one, one, two, one, two)
    return jax.shard_map(
        functools.partial(local, mesh.shape["dp"], mesh.shape["tensor"]),
        mesh=mesh,
        in_specs=(rows, P("dp")) + weights + (all_of,) * 7 + (rows,),
        out_specs=(rows, rows) + weights + (all_of,) * 7,
        check_vma=False,
    )
```

```python
import functools

import jax
import jax.numpy as jnp
from jax import lax
from jax.experimental import pallas as pl
from jax.experimental.pallas import tpu as pltpu
from jax.sharding import PartitionSpec as P

HEAD = 64
LANES = 128
EPSILON = 1e-05
MESH = pl.DeviceIdType.MESH
F32 = jnp.float32
BF16 = jnp.bfloat16
OUTER = 4
KV_STRAIGHT = True
EVEN_WAYS = ((0, 1), (2, 3))
WIDE_WAYS = ((2, 0, 1), (3,))
VMEM_LIMIT = 56 << 20


def nn(a, b):
    return lax.dot_general(a, b, (((1,), (0,)), ((), ())), preferred_element_type=F32)


def nt(a, b):
    return lax.dot_general(a, b, (((1,), (1,)), ((), ())), preferred_element_type=F32)


def tn(a, b):
    return lax.dot_general(a, b, (((0,), (0,)), ((), ())), preferred_element_type=F32)


class Place:
    def __init__(self, dp_size, tensor_size):
        self.nd, self.nt = dp_size, tensor_size
        self.inner, self.ny = dp_size // OUTER, tensor_size // 2
        self.d, self.t = lax.axis_index("dp"), lax.axis_index("tensor")
        self.o, self.i = self.d // self.inner, self.d % self.inner
        self.y, self.c = self.t // 2, self.t % 2
        self.barrier = pltpu.get_barrier_semaphore()

    def at(self, do=0, di=0, dy=0, dc=0):
        o, i = (self.o + do) % OUTER, (self.i + di) % self.inner
        return self.to(o, i, (self.y + dy) % self.ny, (self.c + dc) % 2)

    def to(self, o, i, y, c):
        return (o * self.inner + i, y * 2 + c)

    def nearest(self, k):
        if k == 0:
            return self.o
        high = self.o // 2
        edge = self.o + high * (3 - 2 * self.o)
        place = k * (1 - edge) + (k // 2) * k * edge
        return place + high * (3 - 2 * place)

    def outer_peers(self):
        return [(k, 0, 0, 0) for k in range(1, OUTER)]

    def plane_peers(self):
        return [
            (0, di, dy, 0) for di in range(self.inner) for dy in range(self.ny) if di or dy
        ]

    def peers(self):
        return self.outer_peers() + [
            (0, di, dy, dc)
            for di in range(self.inner)
            for dy in range(self.ny)
            for dc in range(2)
            if di or dy or dc
        ]

    def greet(self):
        for peer in self.peers():
            pl.semaphore_signal(
                self.barrier, inc=1, device_id=self.at(*peer), device_id_type=MESH
            )

    def meet(self):
        pl.semaphore_wait(self.barrier, len(self.peers()))


def remote(src, dst, send, recv, peer):
    return pltpu.make_async_remote_copy(
        src_ref=src,
        dst_ref=dst,
        send_sem=send,
        recv_sem=recv,
        device_id=peer,
        device_id_type=MESH,
    )


class Sender:
    def __init__(self, place, send):
        self.p, self.send, self.started = place, send, []

    def go(self, src, dst, recv, peer):
        copy = remote(src, dst, self.send.at[len(self.started)], recv, peer)
        copy.start()
        self.started.append(copy)

    def got(self, block, recv):
        remote(block, block, self.send.at[0], recv, self.p.at()).wait_recv()

    def finish(self):
        for copy in self.started:
            copy.wait_send()


class Gather(Sender):
    def __init__(self, place, held, sems, straight=False):
        super().__init__(place, sems[0])
        self.held, self.straight = held, straight
        self.got_outer, self.got_i, self.got_y, self.got_d, self.got_core = sems[1:]

    def _block(self, k, i, y):
        p = self.p
        return self.held.at[y * 2 + p.c, p.nearest(k), i]

    def outer_start(self):
        p = self.p
        mine = self._block(0, p.i, p.y)
        for k in range(1, OUTER):
            to = p.to(p.nearest(k), p.i, p.y, p.c)
            self.go(mine, mine, self.got_outer.at[p.o], to)

    def spread(self, k):
        p = self.p
        block = self._block(k, p.i, p.y)
        if k:
            self.got(block, self.got_outer.at[p.nearest(k)])
        for di in range(1, p.inner):
            self.go(block, block, self.got_i.at[di - 1, k], p.at(di=di))
        for dy in range(1, p.ny):
            self.go(block, block, self.got_y.at[dy - 1, k], p.at(dy=dy))
            for di in range(1, p.inner) if self.straight else ():
                self.go(block, block, self.got_d.at[di - 1, dy - 1, k], p.at(di=di, dy=dy))
        self.go(block, block, self.got_core.at[p.y], p.at(dc=1))

    def turn(self, k):
        p = self.p
        for di in range(1, p.inner):
            block = self._block(k, (p.i + p.inner - di) % p.inner, p.y)
            self.got(block, self.got_i.at[di - 1, k])
            if k < 2 and not self.straight:
                for dy in range(1, p.ny):
                    self.go(block, block, self.got_d.at[di - 1, dy - 1, k], p.at(dy=dy))
            self.go(block, block, self.got_core.at[p.y], p.at(dc=1))
        for dy in range(1, p.ny):
            y = (p.y + p.ny - dy) % p.ny
            block = self._block(k, p.i, y)
            self.got(block, self.got_y.at[dy - 1, k])
            if k >= 2 and not self.straight:
                for di in range(1, p.inner):
                    self.go(block, block, self.got_d.at[di - 1, dy - 1, k], p.at(di=di))
            self.go(block, block, self.got_core.at[y], p.at(dc=1))

    def corner(self, k):
        p = self.p
        for di in range(1, p.inner):
            for dy in range(1, p.ny):
                y = (p.y + p.ny - dy) % p.ny
                block = self._block(k, (p.i + p.inner - di) % p.inner, y)
                self.got(block, self.got_d.at[di - 1, dy - 1, k])
                self.go(block, block, self.got_core.at[y], p.at(dc=1))

    def core_done(self, dy):
        p = self.p
        y = (p.y + dy) % p.ny
        self.got(self.held.at[y * 2 + 1 - p.c], self.got_core.at[y])

    @staticmethod
    def semaphores(nd, nt_):
        di, dy = nd // OUTER - 1, nt_ // 2 - 1
        sends = (OUTER - 1) + OUTER * (di + dy + 1 + di + dy) + 2 * OUTER * di * dy
        return [
            pltpu.SemaphoreType.DMA((sends,)),
            pltpu.SemaphoreType.DMA((OUTER,)),
            pltpu.SemaphoreType.DMA((di, OUTER)),
            pltpu.SemaphoreType.DMA((dy, OUTER)),
            pltpu.SemaphoreType.DMA((di, dy, OUTER)),
            pltpu.SemaphoreType.DMA((nt_ // 2,)),
        ]


class Scatter(Sender):
    def __init__(self, place, by_i, by_y, bufs, sems):
        super().__init__(place, sems[0])
        self.by_i, self.by_y = by_i, by_y
        (self.give, self.core, self.in_i, self.in_y, self.sum_i, self.sum_y,
         self.then_y, self.then_i, self.own, self.outer) = bufs
        self.got_core, self.got_i, self.got_y, self.got_ty, self.got_ti, self.got_outer = sems[1:]

    def core_send(self, y):
        self.go(self.give.at[y], self.core.at[y], self.got_core.at[y], self.p.at(dc=1))

    def core_wait(self, y):
        self.got(self.core.at[y], self.got_core.at[y])

    def first_i(self, dy, k):
        p, at = self.p, self.by_i.index(k)
        y, o = (p.y + dy) % p.ny, (p.o + k) % OUTER
        for di in range(1, p.inner):
            self.go(
                self.core.at[y, o, (p.i + di) % p.inner], self.in_i.at[di - 1, at, dy],
                self.got_i.at[di - 1, at, dy], p.at(di=di),
            )

    def first_y(self, dy, k, di):
        p, at = self.p, self.by_y.index(k)
        y, o, i = (p.y + dy) % p.ny, (p.o + k) % OUTER, (p.i + di) % p.inner
        self.go(
            self.core.at[y, o, i], self.in_y.at[dy - 1, at, di],
            self.got_y.at[dy - 1, at, di], p.at(dy=dy),
        )

    def first(self, dy):
        for k in self.by_y:
            for di in range(self.p.inner) if dy else ():
                self.first_y(dy, k, di)
        for k in self.by_i:
            self.first_i(dy, k)

    def second_y(self, k):
        p, at = self.p, self.by_y.index(k)
        o = (p.o + k) % OUTER
        for di in list(range(1, p.inner)) + [0]:
            total = self.core[p.y, o, (p.i + di) % p.inner].astype(F32)
            for dy in range(1, p.ny):
                block = self.in_y.at[dy - 1, at, di]
                self.got(block, self.got_y.at[dy - 1, at, di])
                total = total + block[...].astype(F32)
            self.sum_y[at, di] = total.astype(BF16)
            if di:
                self.go(
                    self.sum_y.at[at, di], self.then_i.at[di - 1, at],
                    self.got_ti.at[di - 1, at], p.at(di=di),
                )

    def second_i(self, k, dy):
        p, at = self.p, self.by_i.index(k)
        total = self.core[(p.y + dy) % p.ny, (p.o + k) % OUTER, p.i].astype(F32)
        for di in range(1, p.inner):
            block = self.in_i.at[di - 1, at, dy]
            self.got(block, self.got_i.at[di - 1, at, dy])
            total = total + block[...].astype(F32)
        self.sum_i[at, dy] = total.astype(BF16)
        if dy:
            self.go(
                self.sum_i.at[at, dy], self.then_y.at[dy - 1, at],
                self.got_ty.at[dy - 1, at], p.at(dy=dy),
            )

    def second(self):
        for k in self.by_y:
            self.second_y(k)
        for dy in list(range(1, self.p.ny)) + [0]:
            for k in self.by_i:
                self.second_i(k, dy)

    def third(self, k):
        p = self.p
        if k in self.by_i:
            at, count, place, sems = self.by_i.index(k), p.ny, self.then_y, self.got_ty
            total = self.sum_i[at, 0].astype(F32)
        else:
            at, count, place, sems = self.by_y.index(k), p.inner, self.then_i, self.got_ti
            total = self.sum_y[at, 0].astype(F32)
        for j in range(count - 1):
            self.got(place.at[j, at], sems.at[j, at])
            total = total + place[j, at].astype(F32)
        self.own[k] = total.astype(BF16)
        if k:
            self.go(self.own.at[k], self.outer.at[k - 1], self.got_outer.at[k - 1], p.at(do=k))

    def last(self):
        total = self.own[0].astype(F32)
        for k in range(1, OUTER):
            self.got(self.outer.at[k - 1], self.got_outer.at[k - 1])
            total = total + self.outer[k - 1].astype(F32)
        return total

    @staticmethod
    def scratch(nd, nt_, by_i, by_y, rows, columns):
        inner, ny = nd // OUTER, nt_ // 2
        ki, ky = len(by_i), len(by_y)
        leads = [
            (ny, OUTER, inner), (ny, OUTER, inner), (inner - 1, ki, ny), (ny - 1, ky, inner),
            (ki, ny), (ky, inner), (ny - 1, ki), (inner - 1, ky), (OUTER,), (OUTER - 1,),
        ]
        return [pltpu.VMEM(lead + (rows, columns), BF16) for lead in leads]

    @staticmethod
    def semaphores(nd, nt_, by_i, by_y):
        inner, ny = nd // OUTER, nt_ // 2
        di, dy, ki, ky = inner - 1, ny - 1, len(by_i), len(by_y)
        sends = ny + ky * dy * inner + ki * di * ny + ky * di + ki * dy + OUTER - 1
        shapes = [
            (sends,), (ny,), (di, ki, ny), (dy, ky, inner), (dy, ki), (di, ky), (OUTER - 1,),
        ]
        return [pltpu.SemaphoreType.DMA(shape) for shape in shapes]


class Exchange(Sender):
    def __init__(self, place, back, bufs, sems):
        super().__init__(place, sems[0])
        self.back = back
        self.own, self.near, self.far, self.made, self.entering = bufs
        self.s_near, self.s_far, self.s_enter = sems[1:]
        self.rows = HEAD // place.inner
        self.members = place.inner * place.nt
        self.me = place.i * place.nt + place.t

    def put(self, g, packed, total, edge, inlet):
        p = self.p
        row = lax.broadcasted_iota(jnp.int32, (8, LANES), 0)
        foot = jnp.where(row == 0, total, jnp.where(row == 1, edge, inlet))
        for sub in range(p.inner):
            self.own[g * p.inner + sub, : self.rows, :] = packed[
                sub * self.rows : (sub + 1) * self.rows
            ]
            self.own[g * p.inner + sub, self.rows :, :] = foot

    def state(self, g):
        p = self.p
        at = pl.ds(g * p.inner, p.inner)
        packed = self.entering[at, : self.rows, :].reshape(HEAD, LANES)
        return packed, self.entering[g * p.inner, self.rows :, :]

    def _peers(self):
        p = self.p
        return [
            (di, dy, dc)
            for di in range(p.inner) for dy in range(p.ny) for dc in range(2) if di or dy or dc
        ]

    def _member(self, di, dy, dc):
        p = self.p
        i, y = (p.i + p.inner - di) % p.inner, (p.y + p.ny - dy) % p.ny
        return i * p.nt + y * 2 + (p.c + dc) % 2

    def _edge(self, block):
        return block[self.rows + 1 : self.rows + 2, :]

    def _inlet(self, block):
        return block[self.rows + 2 : self.rows + 3, :]

    def _hand(self, blocks, place, sems):
        p = self.p
        for di, dy, dc in self._peers():
            to = p.at(0, di, dy, dc)
            member = (to[0] % p.inner) * p.nt + to[1]
            self.go(blocks.at[member], place.at[self.me], sems.at[self.me], to)
        place[self.me] = blocks[self.me]

    def step_near(self):
        self._hand(self.own, self.near, self.s_near)

    def step_far(self):
        p = self.p
        for peer in self._peers():
            m = self._member(*peer)
            self.got(self.near.at[m], self.s_near.at[m])
        border = self.near[0 if self.back else self.members - 1]
        total = jnp.zeros_like(border)
        for j in range(self.members):
            block = self.near[j]
            total = total + jnp.where(self._edge(block) == self._edge(border), block, 0.0)
        row = lax.broadcasted_iota(jnp.int32, total.shape, 0)
        self.far[p.o] = jnp.where(row > self.rows, border, total)
        for k in range(OUTER - 1, 0, -1):
            o = p.nearest(k)
            self.go(self.far.at[p.o], self.far.at[p.o], self.s_far.at[p.o], p.to(o, p.i, p.y, p.c))

    def step_enter(self):
        p = self.p
        for k in range(1, OUTER):
            o = p.nearest(k)
            self.got(self.far.at[o], self.s_far.at[o])
        order = list(range(self.members))
        if self.back:
            order.reverse()
        inlet = self._inlet(self.near[order[0]])
        incoming = jnp.zeros(self.near.shape[1:], F32)
        for o in range(OUTER):
            block = self.far[o]
            ids = jnp.where(o > p.o if self.back else o < p.o, self._edge(block), -1.0)
            incoming = incoming + jnp.where(ids == inlet, block, 0.0)
        for place, j in enumerate(order):
            block = self.near[j]
            if place:
                inlet = self._inlet(block)
                incoming = jnp.where(edge == inlet, running, 0.0)
            self.made[j] = incoming
            edge = self._edge(block)
            running = block + jnp.where(edge == inlet, incoming, 0.0)
        self._hand(self.made, self.entering, self.s_enter)

    def arrive(self):
        for peer in self._peers():
            m = self._member(*peer)
            self.got(self.entering.at[m], self.s_enter.at[m])

    @staticmethod
    def scratch(nd, nt_):
        inner = nd // OUTER
        shape = (HEAD // inner + 8, LANES)
        counts = [inner * nt_, inner * nt_, OUTER, inner * nt_, inner * nt_]
        return [pltpu.VMEM((count,) + shape, F32) for count in counts]

    @staticmethod
    def semaphores(nd, nt_):
        members = nd // OUTER * nt_
        counts = [2 * (members - 1) + OUTER - 1, members, OUTER, members]
        return [pltpu.SemaphoreType.DMA((count,)) for count in counts]


def left_lanes(shape):
    return lax.broadcasted_iota(jnp.int32, shape, len(shape) - 1) < HEAD


def split_heads(block, fill):
    left = left_lanes(block.shape)
    other = jnp.full_like(block, fill)
    return jnp.where(left, block, other), jnp.where(left, other, block)


def feature(values):
    return jnp.where(values > 0.0, values + 1.0, jnp.exp(jnp.minimum(values, 0.0)))


def pack_state(product):
    left = left_lanes((HEAD, LANES))
    return jnp.where(left, product[:HEAD], product[HEAD:])


def wide_state(packed):
    left = left_lanes((HEAD, LANES))
    zero = jnp.zeros_like(packed)
    return jnp.concatenate([jnp.where(left, packed, zero), jnp.where(left, zero, packed)], axis=0)


def two_parts(values):
    high = values.astype(BF16)
    return high, (values - high.astype(F32)).astype(BF16)


def twice(values):
    return jnp.concatenate([values, values], axis=1)


def same_head():
    row = lax.broadcasted_iota(jnp.int32, (LANES, LANES), 0) < HEAD
    return row == left_lanes((LANES, LANES))


class Total(Sender):
    def __init__(self, place, bufs, sems):
        super().__init__(place, sems[0])
        self.mine, self.core, self.plane, self.outer, self.whole = bufs
        self.got_core, self.got_plane, self.got_outer, self.got_whole = sems[1:]

    def start(self, value):
        p = self.p
        self.mine[...] = value.reshape(self.mine.shape)
        self.go(self.mine.at[1 - p.c], self.core, self.got_core.at[0], p.at(dc=1))

    def plane_step(self):
        p = self.p
        self.got(self.core, self.got_core.at[0])
        here = p.i * p.ny + p.y
        self.plane[here] = self.mine[p.c] + self.core[...]
        for peer in p.plane_peers():
            self.go(
                self.plane.at[here], self.plane.at[here], self.got_plane.at[here], p.at(*peer)
            )

    def outer_step(self):
        p = self.p
        for _, di, dy, _ in p.plane_peers():
            place = (p.i + p.inner - di) % p.inner * p.ny + (p.y + p.ny - dy) % p.ny
            self.got(self.plane.at[place], self.got_plane.at[place])
        total = self.plane[0]
        for k in range(1, p.inner * p.ny):
            total = total + self.plane[k]
        self.outer[p.o] = total
        for k in range(1, OUTER):
            to = p.to(p.nearest(k), p.i, p.y, p.c)
            self.go(self.outer.at[p.o], self.outer.at[p.o], self.got_outer.at[p.o], to)

    def core_step(self):
        p = self.p
        for k in range(1, OUTER):
            o = p.nearest(k)
            self.got(self.outer.at[o], self.got_outer.at[o])
        total = self.outer[0]
        for k in range(1, OUTER):
            total = total + self.outer[k]
        self.whole[p.c] = total
        self.go(self.whole.at[p.c], self.whole.at[p.c], self.got_whole.at[p.c], p.at(dc=1))

    def result(self):
        other = 1 - self.p.c
        self.got(self.whole.at[other], self.got_whole.at[other])
        return self.whole[...].reshape(-1, self.whole.shape[-1])

    @staticmethod
    def scratch(nd, nt_, rows, columns):
        leads = [(2,), (), (nd // OUTER * (nt_ // 2),), (OUTER,), (2,)]
        return [pltpu.VMEM(lead + (rows // 2, columns), F32) for lead in leads]

    @staticmethod
    def semaphores(nd, nt_):
        plane = nd // OUTER * (nt_ // 2)
        counts = [plane + OUTER, 1, plane, OUTER, 2]
        return [pltpu.SemaphoreType.DMA((count,)) for count in counts]


def kernel_whole(
    nd, nt_,
    *refs,
):
    given, results, scratch = refs[:16], refs[16:31], refs[31:]
    it = iter(scratch)

    def take(count):
        return [next(it) for _ in range(count)]

    (held_kv, held_qo, held_2, held_1) = take(4)
    operands, made = take(16), take(15)
    (tokens, segments, wq, wk, wv, wo, w1, w2, inner_bias,
     gain1, shift1, gain2, shift2, mixer_bias, outer_bias, cotangent) = operands
    (out, grad_tokens, grad_q, grad_k, grad_v, grad_o, grad_1, grad_2,
     grad_ib, grad_g1, grad_s1, grad_g2, grad_s2, grad_mb, grad_ob) = made
    (segc, mask, normed, normed_t, fq, fk, vb, num_s, den_s) = take(9)
    (res, unit, inv, h2, h2t, cot, dh2, act, dhid, dbt) = take(10)
    (do, dr, gn, gd, dk_s, dv_s, dq_s, dkv_s, dh1, sums, first_sums) = take(11)
    bufs_x, bufs_xb = take(5), take(5)
    bufs_f, bufs_qo, bufs_kv = take(10), take(10), take(10)
    bufs_t1, bufs_t2 = take(5), take(5)
    p = Place(nd, nt_)
    kv, qo = Gather(p, held_kv, take(6), KV_STRAIGHT), Gather(p, held_qo, take(6))
    g2, g1 = Gather(p, held_2, take(6)), Gather(p, held_1, take(6))
    ex = Exchange(p, False, bufs_x, take(4))
    xb = Exchange(p, True, bufs_xb, take(4))
    sf = Scatter(p, *WIDE_WAYS, bufs_f, take(7))
    sqo = Scatter(p, *EVEN_WAYS, bufs_qo, take(7))
    skv = Scatter(p, *EVEN_WAYS, bufs_kv, take(7))
    all_sum, first_sum = Total(p, bufs_t1, take(5)), Total(p, bufs_t2, take(5))

    rows_all, width = tokens.shape
    head, hidden = wq.shape[1], w1.shape[1]
    part_rows = wq.shape[0]
    block_shape = (OUTER, p.inner, part_rows)
    step, block, tile = 128, min(512, rows_all), min(256, rows_all)

    (in_sems, out_sems) = take(2)
    p.greet()
    loads = [
        pltpu.make_async_copy(given[n], operands[n], in_sems.at[n]) for n in range(len(given))
    ]
    stores = [
        pltpu.make_async_copy(made[n], results[n], out_sems.at[n]) for n in range(len(made))
    ]
    early = (3, 4)
    for n in early + tuple(n for n in range(len(given)) if n not in early):
        loads[n].start()
    here = (p.t, p.o, p.i)
    if head < LANES:
        blank = jnp.zeros((part_rows, 2 * LANES), BF16)
        held_kv[here] = blank
        held_qo[here] = blank
    for n in early:
        loads[n].wait()
    held_kv[here + (slice(None), slice(0, head))] = wk[...].astype(BF16)
    held_kv[here + (slice(None), slice(LANES, LANES + head))] = wv[...].astype(BF16)
    p.meet()
    kv.outer_start()
    kv.spread(0)
    for n in range(len(loads) - 1):
        if n not in early:
            loads[n].wait()
    held_qo[here + (slice(None), slice(0, head))] = wq[...].astype(BF16)
    held_qo[here + (slice(None), slice(LANES, LANES + head))] = wo[...].astype(BF16)
    held_2[here] = w2[...].astype(BF16)
    held_1[here] = w1[...].astype(BF16)
    segr = segments[:, pl.ds(pl.multiple_of(p.t * rows_all, LANES), rows_all)].astype(F32)
    for start in range(0, rows_all, LANES):
        wide = jnp.broadcast_to(segr[:, start : start + LANES], (8, LANES))
        segc[start : start + LANES, :] = jnp.transpose(wide)[:, 0:1]
    first_id, last_id = segr[:, 0:1], segr[:, rows_all - 1 : rows_all]

    def norm(k, _):
        at = pl.ds(pl.multiple_of(k * step, step), step)
        x = tokens[at, :].astype(F32)
        center = x - jnp.mean(x, axis=-1, keepdims=True)
        spread = jnp.mean(center * center, axis=-1, keepdims=True)
        y = center * lax.rsqrt(spread + EPSILON) * gain1[...] + shift1[...]
        normed[at, :] = y.astype(BF16)
        normed_t[:, at] = jnp.transpose(y).astype(BF16)
        return 0

    lax.fori_loop(0, rows_all // step, norm, 0)
    for start in range(0, rows_all, 128):
        later = lax.broadcasted_iota(jnp.int32, (128, rows_all), 0) + start
        earlier = lax.broadcasted_iota(jnp.int32, (128, rows_all), 1)
        same = segc[start : start + 128, :] == segr
        mask[start : start + 128, :] = jnp.where((later >= earlier) & same, 1.0, 0.0).astype(BF16)
    for k in range(1, OUTER):
        kv.spread(k)
    qo.outer_start()
    qo.spread(0)
    g2.outer_start()
    def keys_values(g):
        w = held_kv[g].reshape(width, 2 * LANES)
        both = nn(normed[...], w)
        keys = feature(both[:, :LANES]).astype(BF16)
        values = both[:, LANES:].astype(BF16)
        fk[g] = keys
        vb[g] = values
        kept = jnp.where(segc[...] == last_id, keys, jnp.zeros_like(keys))
        total = jnp.sum(kept.astype(F32), axis=0, keepdims=True)
        ex.put(g, pack_state(tn(kept, values)), total, last_id, first_id)

    def columns(dy, dc):
        return (p.y + dy) % p.ny * 2 + (p.c + dc) % 2

    for k in range(OUTER):
        kv.turn(k)
    for k in range(1, OUTER):
        qo.spread(k)
    g1.outer_start()
    keys_values(columns(0, 0))
    for k in range(OUTER):
        kv.corner(k)
    g2.spread(0)
    g1.spread(0)
    for dy in range(1, p.ny):
        keys_values(columns(dy, 0))
    for dy in range(p.ny):
        kv.core_done(dy)
        keys_values(columns(dy, 1))

    def queries(g):
        w = held_qo[g].reshape(width, 2 * LANES)
        fq[g] = feature(nn(normed[...], w[:, :LANES])).astype(BF16)

    ex.step_near()
    for k in range(OUTER):
        qo.turn(k)
    queries(columns(0, 0))
    for k in range(1, OUTER):
        g2.spread(k)
    loads[-1].wait()
    for start in range(0, rows_all, step):
        turned = jnp.transpose(cotangent[start : start + step, :].astype(F32))
        cot[:, start : start + step] = turned.astype(BF16)
    ex.step_far()
    g1.spread(1)
    for k in range(OUTER):
        qo.corner(k)
    for dy in range(1, p.ny):
        queries(columns(dy, 0))
    for dy in range(p.ny):
        qo.core_done(dy)
        queries(columns(dy, 1))


    def inside(g, _):
        values = split_heads(vb[g], 1.0)
        for start in range(0, rows_all, tile):
            end = start + tile
            now = mask[start:end, :end]
            query = split_heads(fq[g, start:end, :], 0.0)
            keys = fk[g, :end, :]
            parts = []
            for h in range(2):
                scores = nt(query[h], keys).astype(BF16) * now
                parts.append(nn(scores, values[h][:end]))
            left = left_lanes(parts[0].shape)
            num_s[g, start:end, :] = jnp.where(left, parts[0], parts[1])
            den_s[g, start:end, :] = pltpu.roll(
                jnp.where(left, parts[1], parts[0]), HEAD, 1
            )
        return 0

    lax.fori_loop(0, nt_ // 2, inside, 0)
    ex.step_enter()
    for k in range(2, OUTER):
        g1.spread(k)
    for k in range(OUTER):
        g2.turn(k)
    lax.fori_loop(nt_ // 2, nt_, inside, 0)
    for k in range(2):
        g1.turn(k)
    ex.arrive()

    def outside(g, _):
        packed, foot = ex.state(g)
        total = jnp.broadcast_to(jnp.transpose(foot)[:, 0:1], (LANES, LANES))
        total = jnp.where(same_head(), total, 0.0)
        parts = two_parts(jnp.concatenate([wide_state(packed), total], axis=1))
        query = fq[g]
        query = jnp.where(segc[...] == first_id, query, jnp.zeros_like(query))
        carried = nn(twice(query), jnp.concatenate(parts, axis=0))
        num = num_s[g] + carried[:, :LANES]
        den = den_s[g] + carried[:, LANES:]
        inverse = 1.0 / den
        den_s[g] = inverse
        num_s[g] = num * inverse
        return 0

    lax.fori_loop(0, nt_, outside, 0)
    mixed, rden = num_s, den_s
    for k in range(2, OUTER):
        g1.turn(k)

    def output_weight():
        parts = [held_qo[g, :, :, :, LANES:].reshape(width, LANES) for g in range(nt_)]
        return jnp.concatenate(parts, axis=1)

    def enter(k, _):
        at = pl.ds(pl.multiple_of(k * step, step), step)
        low = jnp.concatenate([mixed[g, at, :].astype(BF16) for g in range(nt_)], axis=1)
        r = tokens[at, :].astype(F32) + mixer_bias[...] + nt(low, output_weight())
        center = r - jnp.mean(r, axis=-1, keepdims=True)
        spread = jnp.mean(center * center, axis=-1, keepdims=True)
        scale = lax.rsqrt(spread + EPSILON)
        n = center * scale
        y = n * gain2[...] + shift2[...]
        res[at, :] = r + outer_bias[...]
        unit[at, :] = n
        inv[at, :] = scale
        h2[at, :] = y.astype(BF16)
        h2t[:, at] = jnp.transpose(y).astype(BF16)
        dh2[at, :] = jnp.zeros((step, width), F32)
        return 0

    lax.fori_loop(0, rows_all // step, enter, 0)
    sums[...] = jnp.zeros_like(sums)
    g2.core_done(0)
    g1.core_done(0)
    tall = width // OUTER

    def feed(g):
        wi = held_1[g].reshape(width, hidden)
        wt = held_2[g].reshape(width, hidden)
        total = jnp.zeros((1, hidden), F32)
        bias = inner_bias[:, pl.ds(pl.multiple_of(g * hidden, LANES), hidden)]
        for start in range(0, rows_all, block):
            end = start + block
            u = nn(h2[start:end, :], wi) + bias
            below = 0.5 * (1.0 + lax.erf(u * 0.7071067811865476))
            slope = below + u * (jnp.exp(-0.5 * (u * u)) * 0.3989422804014327)
            a = (u * below).astype(BF16)
            du = (nn(cotangent[start:end, :], wt) * slope).astype(BF16)
            act[start:end, :] = a
            dhid[start:end, :] = du
            total = total + jnp.sum(du.astype(F32), axis=0, keepdims=True)
            res[start:end, :] += nt(a, wt)
            dh2[start:end, :] += nt(du, wi)
        sums[pl.ds(8 + g, 1), 0:hidden] = total

    shape = (p.inner, part_rows, hidden)

    def feed_grads(y, mine):
        for o in range(OUTER):
            for s, (left, right) in enumerate(((h2t, dhid), (cot, act))):
                lanes = slice(s * hidden, (s + 1) * hidden)
                value = nn(left[o * tall : (o + 1) * tall, :], right[...]).reshape(shape)
                if mine:
                    value = value + sf.core[y, o, :, :, lanes].astype(F32)
                    sf.core[y, o, :, :, lanes] = value.astype(BF16)
                else:
                    sf.give[y, o, :, :, lanes] = value.astype(BF16)

    for dy in range(p.ny):
        y = (p.y + dy) % p.ny
        if dy:
            g2.core_done(dy)
            g1.core_done(dy)
        feed(y * 2 + 1 - p.c)
        feed_grads(y, False)
        sf.core_send(y)
        if not dy:
            for k in range(OUTER):
                g2.corner(k)
                g1.corner(k)
        feed(y * 2 + p.c)
        sf.core_wait(y)
        feed_grads(y, True)
        sf.first_i(dy, 2)
        if dy:
            sf.first_y(dy, 3, 0)
        else:
            sf.first_i(0, 0)

    def leave(k, _):
        at = pl.ds(pl.multiple_of(k * step, step), step)
        out[at, :] = res[at, :].astype(BF16)
        n = unit[at, :]
        grad = dh2[at, :]
        e = cotangent[at, :].astype(F32)
        pushed = grad * gain2[...]
        mean = jnp.mean(pushed, axis=-1, keepdims=True)
        along = jnp.mean(pushed * n, axis=-1, keepdims=True)
        back = e + (pushed - mean - n * along) * inv[at, :]
        dr[at, :] = back
        low = back.astype(BF16)
        wide = low.astype(F32)
        dbt[:, at] = jnp.transpose(wide).astype(BF16)
        pulled = nn(low, output_weight())
        for g in range(nt_):
            do[g, at, :] = pulled[:, g * LANES : (g + 1) * LANES]
        sums[2:3, :] += jnp.sum(grad * n, axis=0, keepdims=True)
        sums[3:4, :] += jnp.sum(grad, axis=0, keepdims=True)
        sums[4:5, :] += jnp.sum(wide, axis=0, keepdims=True)
        sums[5:6, :] += jnp.sum(e, axis=0, keepdims=True)
        return 0

    lax.fori_loop(0, rows_all // step, leave, 0)
    stores[0].start()

    def first(g, _):
        low = (do[g] * rden[g]).astype(BF16)
        gn[g] = low
        product = jnp.concatenate(two_parts(low.astype(F32) * mixed[g]), axis=1)
        minus = jnp.where(same_head(), -1.0, 0.0).astype(BF16)
        slope = nn(product, jnp.concatenate([minus, minus], axis=0))
        gd[g] = slope
        kept = jnp.where(segc[...] == first_id, fq[g], jnp.zeros_like(low))
        total = jnp.sum(kept.astype(F32) * slope, axis=0, keepdims=True)
        xb.put(g, pack_state(tn(kept, low)), total, first_id, last_id)
        return 0

    lax.fori_loop(0, nt_, first, 0)
    xb.step_near()
    for dy in range(1, p.ny):
        for k in range(2):
            sf.first_i(dy, k)
    all_sum.start(sums[...])

    def inside_back(g, _):
        values, keys = vb[g], fk[g]
        key_heads = split_heads(keys, 0.0)
        packed, foot = ex.state(g)
        state = jnp.concatenate(two_parts(wide_state(packed)), axis=1)
        query_t = jnp.transpose(fq[g].astype(F32)).astype(BF16)
        grad_t = jnp.transpose(gn[g].astype(F32)).astype(BF16)
        dk_t = jnp.zeros((LANES, rows_all), F32)
        dv_t = jnp.zeros((LANES, rows_all), F32)
        for start in range(0, rows_all, tile):
            end = start + tile
            now = mask[start:end, :end]
            query, grad = fq[g, start:end, :], gn[g, start:end, :]
            slope = gd[g, start:end, :]
            query_heads, grad_heads = split_heads(query, 0.0), split_heads(grad, 0.0)
            dq = jnp.where(
                segc[start:end, :] == first_id,
                nt(twice(grad), state) + slope * foot[0:1, :],
                0.0,
            )
            dk_parts, dv_parts = [], []
            for h in range(2):
                lanes = slice(h * HEAD, h * HEAD + 1)
                part = slice(h * HEAD, (h + 1) * HEAD)
                weight = nt(query_heads[h], keys[:end]).astype(BF16) * now
                share = (nt(grad_heads[h], values[:end]) + slope[:, lanes]).astype(BF16) * now
                dq = dq + nn(share, key_heads[h][:end])
                dk_parts.append(nn(query_t[part, start:end], share))
                dv_parts.append(nn(grad_t[part, start:end], weight))
            dk_now = jnp.concatenate(dk_parts, axis=0)
            dv_now = jnp.concatenate(dv_parts, axis=0)
            if end < rows_all:
                pad = jnp.zeros((LANES, rows_all - end), F32)
                dk_now = jnp.concatenate([dk_now, pad], axis=1)
                dv_now = jnp.concatenate([dv_now, pad], axis=1)
            dk_t, dv_t = dk_t + dk_now, dv_t + dv_now
            dq_s[g, start:end, :] = (dq * jnp.minimum(query.astype(F32), 1.0)).astype(BF16)
        dk_s[g] = jnp.transpose(dk_t)
        dv_s[g] = jnp.transpose(dv_t)
        return 0

    quarter = nt_ // 4
    lax.fori_loop(0, quarter, inside_back, 0)
    for dy in range(1, p.ny):
        sf.second_i(2, dy)
        for di in range(1, p.inner):
            sf.first_y(dy, 3, di)
    lax.fori_loop(quarter, 2 * quarter, inside_back, 0)
    xb.step_far()
    all_sum.plane_step()
    sf.second_i(2, 0)
    lax.fori_loop(2 * quarter, nt_, inside_back, 0)
    xb.step_enter()
    sf.third(2)
    for dy in range(1, p.ny):
        sf.second_i(0, dy)
    sf.first_i(0, 1)

    def attention_grads(scatter, dc, joint):
        for dy in list(range(1, p.ny)) + [0]:
            y = (p.y + dy) % p.ny
            g = y * 2 + (p.c + dc) % 2
            values = joint(g)
            if not dc:
                scatter.core_wait(y)
            for s, (left, right) in enumerate(values):
                lanes = slice(s * LANES, (s + 1) * LANES)
                value = nn(left, right).reshape(block_shape + (LANES,))
                if dc:
                    scatter.give[y, :, :, :, lanes] = value.astype(BF16)
                else:
                    value = value + scatter.core[y, :, :, :, lanes].astype(F32)
                    scatter.core[y, :, :, :, lanes] = value.astype(BF16)
            if dc:
                scatter.core_send(y)
            else:
                scatter.first(dy)

    def query_output(g):
        return ((normed_t[...], dq_s[g]), (dbt[...], mixed[g].astype(BF16)))

    attention_grads(sqo, 1, query_output)
    for dy in range(1, p.ny):
        sf.second_i(1, dy)
    sf.second_y(3)
    attention_grads(sqo, 0, query_output)
    sf.second_i(0, 0)
    all_sum.outer_step()

    def query_back(g, _):
        dh1[...] += nt(dq_s[g], held_qo[g, :, :, :, :LANES].reshape(width, LANES))
        return 0

    dh1[...] = jnp.zeros_like(dh1)
    lax.fori_loop(0, nt_, query_back, 0)
    sf.second_i(1, 0)
    xb.arrive()

    def key_value(g):
        packed, foot = xb.state(g)
        parts = two_parts(wide_state(packed))
        keys, values = fk[g], vb[g]
        dk = nt(twice(values), jnp.concatenate(parts, axis=1)) + foot[0:1, :]
        dv = nn(twice(keys), jnp.concatenate(parts, axis=0))
        closing = segc[...] == last_id
        dk = dk_s[g] + jnp.where(closing, dk, 0.0)
        dv = dv_s[g] + jnp.where(closing, dv, 0.0)
        dk = (dk * jnp.minimum(keys.astype(F32), 1.0)).astype(BF16)
        dv = dv.astype(BF16)
        dkv_s[g, :, :LANES] = dk
        dkv_s[g, :, LANES:] = dv
        return ((normed_t[...], dk), (normed_t[...], dv))

    attention_grads(skv, 1, key_value)
    sf.third(1)
    attention_grads(skv, 0, key_value)
    sf.third(3)

    def key_value_back(g, _):
        dh1[...] += nt(dkv_s[g], held_kv[g].reshape(width, 2 * LANES))
        return 0

    lax.fori_loop(0, nt_, key_value_back, 0)
    first_sums[...] = jnp.zeros_like(first_sums)

    def finish(k, _):
        at = pl.ds(pl.multiple_of(k * step, step), step)
        x = tokens[at, :].astype(F32)
        center = x - jnp.mean(x, axis=-1, keepdims=True)
        spread = jnp.mean(center * center, axis=-1, keepdims=True)
        scale = lax.rsqrt(spread + EPSILON)
        n = center * scale
        grad = dh1[at, :]
        pushed = grad * gain1[...]
        mean = jnp.mean(pushed, axis=-1, keepdims=True)
        along = jnp.mean(pushed * n, axis=-1, keepdims=True)
        back = (pushed - mean - n * along) * scale
        grad_tokens[at, :] = (dr[at, :] + back).astype(BF16)
        first_sums[0:1, :] += jnp.sum(grad * n, axis=0, keepdims=True)
        first_sums[8:9, :] += jnp.sum(grad, axis=0, keepdims=True)
        return 0

    lax.fori_loop(0, rows_all // step, finish, 0)
    stores[1].start()
    first_sum.start(first_sums[...])
    sqo.second()
    first_sum.plane_step()
    skv.second()
    for k in (2, 3, 1):
        sqo.third(k)
    first_sum.outer_step()
    for k in (2, 3, 1):
        skv.third(k)
    for scatter in (sf, sqo, skv):
        scatter.third(0)
    all_sum.core_step()
    total = sf.last()
    grad_1[...] = total[:, :hidden]
    grad_2[...] = total[:, hidden:]
    total = sqo.last()
    grad_q[...] = total[:, :head]
    grad_o[...] = total[:, LANES : LANES + head]
    first_sum.core_step()
    total = all_sum.result()
    grad_g2[...] = total[2:3, :]
    grad_s2[...] = total[3:4, :]
    grad_mb[...] = total[4:5, :]
    grad_ob[...] = total[5:6, :]
    for g in range(nt_):
        grad_ib[:, g * hidden : (g + 1) * hidden] = total[8 + g : 9 + g, :hidden]
    total = skv.last()
    grad_k[...] = total[:, :head]
    grad_v[...] = total[:, LANES : LANES + head]
    total = first_sum.result()
    grad_g1[...] = total[0:1, :]
    grad_s1[...] = total[8:9, :]
    for store in stores[2:]:
        store.start()
    for store in stores:
        store.wait()
    for each in (kv, qo, g2, g1, ex, xb, sf, sqo, skv, all_sum, first_sum):
        each.finish()


def kernel_outputs(count, *refs):
    given, made, held = (refs[k * count : (k + 1) * count] for k in range(3))
    loaded, stored = refs[3 * count :]
    loads = [pltpu.make_async_copy(given[k], held[k], loaded.at[k]) for k in range(count)]
    stores = [pltpu.make_async_copy(held[k], made[k], stored.at[k]) for k in range(count)]
    for load in loads:
        load.start()
    for load, store in zip(loads, stores):
        load.wait()
        store.start()
    for store in stores:
        store.wait()


def local(nd, nt_, *args):
    (tokens, segments, wq, wk, wv, wo, w1, w2, inner_bias, *vectors, cotangent) = args
    rows, width = tokens.shape
    inner = nd // OUTER
    part_rows, hidden = w1.shape
    hbm = pl.BlockSpec(memory_space=pl.ANY)
    group = (nt_, rows, LANES)
    total_rows = 8 + max(8, nt_)
    head = wq.shape[1]
    row = jax.ShapeDtypeStruct((1, width), F32)
    narrow = jax.ShapeDtypeStruct((part_rows, head), F32)
    wide = jax.ShapeDtypeStruct((part_rows, hidden), F32)
    outs = [
        jax.ShapeDtypeStruct(tokens.shape, BF16),
        jax.ShapeDtypeStruct(tokens.shape, BF16),
        narrow, narrow, narrow, narrow, wide, wide,
        jax.ShapeDtypeStruct((1, nt_ * hidden), F32),
        *[row] * 6,
    ]
    operands = (
        tokens, segments[None], wq, wk, wv, wo.T, w1, w2.T, inner_bias[None],
        *[v[None] for v in vectors], cotangent,
    )
    held = (nt_, OUTER, inner, part_rows)
    square = (rows, width)
    scratch = [
        pltpu.VMEM(held + (2 * LANES,), BF16),
        pltpu.VMEM(held + (2 * LANES,), BF16),
        pltpu.VMEM(held + (hidden,), BF16),
        pltpu.VMEM(held + (hidden,), BF16),
        *[pltpu.VMEM(v.shape, v.dtype) for v in operands],
        *[pltpu.VMEM(v.shape, v.dtype) for v in outs],
        pltpu.VMEM((rows, 1), F32),
        pltpu.VMEM((rows, rows), BF16),
        pltpu.VMEM(square, BF16),
        pltpu.VMEM((width, rows), BF16),
        pltpu.VMEM(group, BF16),
        pltpu.VMEM(group, BF16),
        pltpu.VMEM(group, BF16),
        pltpu.VMEM(group, F32),
        pltpu.VMEM(group, F32),
        pltpu.VMEM(square, F32),
        pltpu.VMEM(square, F32),
        pltpu.VMEM((rows, 1), F32),
        pltpu.VMEM(square, BF16),
        pltpu.VMEM((width, rows), BF16),
        pltpu.VMEM((width, rows), BF16),
        pltpu.VMEM(square, F32),
        pltpu.VMEM((rows, hidden), BF16),
        pltpu.VMEM((rows, hidden), BF16),
        pltpu.VMEM((width, rows), BF16),
        pltpu.VMEM(group, F32),
        pltpu.VMEM(square, F32),
        pltpu.VMEM(group, BF16),
        pltpu.VMEM(group, F32),
        pltpu.VMEM(group, F32),
        pltpu.VMEM(group, F32),
        pltpu.VMEM(group, BF16),
        pltpu.VMEM((nt_, rows, 2 * LANES), BF16),
        pltpu.VMEM(square, F32),
        pltpu.VMEM((total_rows, width), F32),
        pltpu.VMEM((16, width), F32),
    ]
    for _ in range(2):
        scratch += Exchange.scratch(nd, nt_)
    scratch += Scatter.scratch(nd, nt_, *WIDE_WAYS, part_rows, 2 * hidden)
    scratch += Scatter.scratch(nd, nt_, *EVEN_WAYS, part_rows, 2 * LANES)
    scratch += Scatter.scratch(nd, nt_, *EVEN_WAYS, part_rows, 2 * LANES)
    scratch += Total.scratch(nd, nt_, total_rows, width)
    scratch += Total.scratch(nd, nt_, 16, width)
    for _ in range(4):
        scratch += Gather.semaphores(nd, nt_)
    for _ in range(2):
        scratch += Exchange.semaphores(nd, nt_)
    for ways in (WIDE_WAYS, EVEN_WAYS, EVEN_WAYS):
        scratch += Scatter.semaphores(nd, nt_, *ways)
    for _ in range(2):
        scratch += Total.semaphores(nd, nt_)
    scratch += [pltpu.SemaphoreType.DMA((len(v),)) for v in (operands, outs)]
    results = pl.pallas_call(
        functools.partial(kernel_whole, nd, nt_),
        out_shape=outs,
        in_specs=[hbm] * len(operands),
        out_specs=[hbm] * len(outs),
        scratch_shapes=scratch,
        compiler_params=pltpu.CompilerParams(
            collective_id=0, has_side_effects=True, vmem_limit_bytes=VMEM_LIMIT
        ),
        name="whole_layer",
    )(*operands)
    final = pl.pallas_call(
        functools.partial(kernel_outputs, len(outs)),
        out_shape=outs,
        in_specs=[hbm] * len(outs),
        out_specs=[hbm] * len(outs),
        scratch_shapes=[pltpu.VMEM(o.shape, o.dtype) for o in outs]
        + [pltpu.SemaphoreType.DMA((len(outs),))] * 2,
        name="outputs",
    )(*results)
    return (
        *final[:5], final[5].T, final[6], final[7].T, *[v.reshape(-1) for v in final[8:]],
    )


def solution(mesh):
    rows = P(("dp", "tensor"), None)
    one, two, all_of = P("dp", "tensor"), P("tensor", "dp"), P()
    weights = (one, one, one, two, one, two)
    return jax.shard_map(
        functools.partial(local, mesh.shape["dp"], mesh.shape["tensor"]),
        mesh=mesh,
        in_specs=(rows, P("dp")) + weights + (all_of,) * 7 + (rows,),
        out_specs=(rows, rows) + weights + (all_of,) * 7,
        check_vma=False,
    )
```

```python
import functools

import jax
import jax.numpy as jnp
from jax import lax
from jax.experimental import pallas as pl
from jax.experimental.pallas import tpu as pltpu
from jax.sharding import PartitionSpec as P

HEAD = 64
LANES = 128
EPSILON = 1e-05
MESH = pl.DeviceIdType.MESH
F32 = jnp.float32
BF16 = jnp.bfloat16
OUTER = 4
KV_STRAIGHT = True
EVEN_WAYS = ((0, 1), (2, 3))
WIDE_WAYS = ((2, 0, 1), (3,))
VMEM_LIMIT = 56 << 20


def nn(a, b):
    return lax.dot_general(a, b, (((1,), (0,)), ((), ())), preferred_element_type=F32)


def nt(a, b):
    return lax.dot_general(a, b, (((1,), (1,)), ((), ())), preferred_element_type=F32)


def tn(a, b):
    return lax.dot_general(a, b, (((0,), (0,)), ((), ())), preferred_element_type=F32)


class Place:
    def __init__(self, dp_size, tensor_size):
        self.nd, self.nt = dp_size, tensor_size
        self.inner, self.ny = dp_size // OUTER, tensor_size // 2
        self.d, self.t = lax.axis_index("dp"), lax.axis_index("tensor")
        self.o, self.i = self.d // self.inner, self.d % self.inner
        self.y, self.c = self.t // 2, self.t % 2
        self.barrier = pltpu.get_barrier_semaphore()

    def at(self, do=0, di=0, dy=0, dc=0):
        o, i = (self.o + do) % OUTER, (self.i + di) % self.inner
        return self.to(o, i, (self.y + dy) % self.ny, (self.c + dc) % 2)

    def to(self, o, i, y, c):
        return (o * self.inner + i, y * 2 + c)

    def nearest(self, k):
        if k == 0:
            return self.o
        high = self.o // 2
        edge = self.o + high * (3 - 2 * self.o)
        place = k * (1 - edge) + (k // 2) * k * edge
        return place + high * (3 - 2 * place)

    def outer_peers(self):
        return [(k, 0, 0, 0) for k in range(1, OUTER)]

    def plane_peers(self):
        return [
            (0, di, dy, 0) for di in range(self.inner) for dy in range(self.ny) if di or dy
        ]

    def peers(self):
        return self.outer_peers() + [
            (0, di, dy, dc)
            for di in range(self.inner)
            for dy in range(self.ny)
            for dc in range(2)
            if di or dy or dc
        ]

    def greet(self):
        for peer in self.peers():
            pl.semaphore_signal(
                self.barrier, inc=1, device_id=self.at(*peer), device_id_type=MESH
            )

    def meet(self):
        pl.semaphore_wait(self.barrier, len(self.peers()))


def remote(src, dst, send, recv, peer):
    return pltpu.make_async_remote_copy(
        src_ref=src,
        dst_ref=dst,
        send_sem=send,
        recv_sem=recv,
        device_id=peer,
        device_id_type=MESH,
    )


class Sender:
    def __init__(self, place, send):
        self.p, self.send, self.started = place, send, []

    def go(self, src, dst, recv, peer):
        copy = remote(src, dst, self.send.at[len(self.started)], recv, peer)
        copy.start()
        self.started.append(copy)

    def got(self, block, recv):
        remote(block, block, self.send.at[0], recv, self.p.at()).wait_recv()

    def finish(self):
        for copy in self.started:
            copy.wait_send()


class Gather(Sender):
    def __init__(self, place, held, sems, straight=False):
        super().__init__(place, sems[0])
        self.held, self.straight = held, straight
        self.got_outer, self.got_i, self.got_y, self.got_d, self.got_core = sems[1:]

    def _block(self, k, i, y):
        p = self.p
        return self.held.at[y * 2 + p.c, p.nearest(k), i]

    def outer_start(self):
        p = self.p
        mine = self._block(0, p.i, p.y)
        for k in range(1, OUTER):
            to = p.to(p.nearest(k), p.i, p.y, p.c)
            self.go(mine, mine, self.got_outer.at[p.o], to)

    def spread(self, k):
        p = self.p
        block = self._block(k, p.i, p.y)
        if k:
            self.got(block, self.got_outer.at[p.nearest(k)])
        for di in range(1, p.inner):
            self.go(block, block, self.got_i.at[di - 1, k], p.at(di=di))
        for dy in range(1, p.ny):
            self.go(block, block, self.got_y.at[dy - 1, k], p.at(dy=dy))
            for di in range(1, p.inner) if self.straight else ():
                self.go(block, block, self.got_d.at[di - 1, dy - 1, k], p.at(di=di, dy=dy))
        self.go(block, block, self.got_core.at[p.y], p.at(dc=1))

    def turn(self, k):
        p = self.p
        for di in range(1, p.inner):
            block = self._block(k, (p.i + p.inner - di) % p.inner, p.y)
            self.got(block, self.got_i.at[di - 1, k])
            if k < 2 and not self.straight:
                for dy in range(1, p.ny):
                    self.go(block, block, self.got_d.at[di - 1, dy - 1, k], p.at(dy=dy))
            self.go(block, block, self.got_core.at[p.y], p.at(dc=1))
        for dy in range(1, p.ny):
            y = (p.y + p.ny - dy) % p.ny
            block = self._block(k, p.i, y)
            self.got(block, self.got_y.at[dy - 1, k])
            if k >= 2 and not self.straight:
                for di in range(1, p.inner):
                    self.go(block, block, self.got_d.at[di - 1, dy - 1, k], p.at(di=di))
            self.go(block, block, self.got_core.at[y], p.at(dc=1))

    def corner(self, k):
        p = self.p
        for di in range(1, p.inner):
            for dy in range(1, p.ny):
                y = (p.y + p.ny - dy) % p.ny
                block = self._block(k, (p.i + p.inner - di) % p.inner, y)
                self.got(block, self.got_d.at[di - 1, dy - 1, k])
                self.go(block, block, self.got_core.at[y], p.at(dc=1))

    def core_done(self, dy):
        p = self.p
        y = (p.y + dy) % p.ny
        self.got(self.held.at[y * 2 + 1 - p.c], self.got_core.at[y])

    @staticmethod
    def semaphores(nd, nt_):
        di, dy = nd // OUTER - 1, nt_ // 2 - 1
        sends = (OUTER - 1) + OUTER * (di + dy + 1 + di + dy) + 2 * OUTER * di * dy
        return [
            pltpu.SemaphoreType.DMA((sends,)),
            pltpu.SemaphoreType.DMA((OUTER,)),
            pltpu.SemaphoreType.DMA((di, OUTER)),
            pltpu.SemaphoreType.DMA((dy, OUTER)),
            pltpu.SemaphoreType.DMA((di, dy, OUTER)),
            pltpu.SemaphoreType.DMA((nt_ // 2,)),
        ]


class Scatter(Sender):
    def __init__(self, place, by_i, by_y, bufs, sems):
        super().__init__(place, sems[0])
        self.by_i, self.by_y = by_i, by_y
        (self.give, self.core, self.in_i, self.in_y, self.sum_i, self.sum_y,
         self.then_y, self.then_i, self.own, self.outer) = bufs
        self.got_core, self.got_i, self.got_y, self.got_ty, self.got_ti, self.got_outer = sems[1:]

    def core_send(self, y):
        self.go(self.give.at[y], self.core.at[y], self.got_core.at[y], self.p.at(dc=1))

    def core_wait(self, y):
        self.got(self.core.at[y], self.got_core.at[y])

    def first_i(self, dy, k):
        p, at = self.p, self.by_i.index(k)
        y, o = (p.y + dy) % p.ny, (p.o + k) % OUTER
        for di in range(1, p.inner):
            self.go(
                self.core.at[y, o, (p.i + di) % p.inner], self.in_i.at[di - 1, at, dy],
                self.got_i.at[di - 1, at, dy], p.at(di=di),
            )

    def first_y(self, dy, k, di):
        p, at = self.p, self.by_y.index(k)
        y, o, i = (p.y + dy) % p.ny, (p.o + k) % OUTER, (p.i + di) % p.inner
        self.go(
            self.core.at[y, o, i], self.in_y.at[dy - 1, at, di],
            self.got_y.at[dy - 1, at, di], p.at(dy=dy),
        )

    def first(self, dy):
        for k in self.by_y:
            for di in range(self.p.inner) if dy else ():
                self.first_y(dy, k, di)
        for k in self.by_i:
            self.first_i(dy, k)

    def second_y(self, k):
        p, at = self.p, self.by_y.index(k)
        o = (p.o + k) % OUTER
        for di in list(range(1, p.inner)) + [0]:
            total = self.core[p.y, o, (p.i + di) % p.inner].astype(F32)
            for dy in range(1, p.ny):
                block = self.in_y.at[dy - 1, at, di]
                self.got(block, self.got_y.at[dy - 1, at, di])
                total = total + block[...].astype(F32)
            self.sum_y[at, di] = total.astype(BF16)
            if di:
                self.go(
                    self.sum_y.at[at, di], self.then_i.at[di - 1, at],
                    self.got_ti.at[di - 1, at], p.at(di=di),
                )

    def second_i(self, k, dy):
        p, at = self.p, self.by_i.index(k)
        total = self.core[(p.y + dy) % p.ny, (p.o + k) % OUTER, p.i].astype(F32)
        for di in range(1, p.inner):
            block = self.in_i.at[di - 1, at, dy]
            self.got(block, self.got_i.at[di - 1, at, dy])
            total = total + block[...].astype(F32)
        self.sum_i[at, dy] = total.astype(BF16)
        if dy:
            self.go(
                self.sum_i.at[at, dy], self.then_y.at[dy - 1, at],
                self.got_ty.at[dy - 1, at], p.at(dy=dy),
            )

    def second(self):
        for k in self.by_y:
            self.second_y(k)
        for dy in list(range(1, self.p.ny)) + [0]:
            for k in self.by_i:
                self.second_i(k, dy)

    def third(self, k):
        p = self.p
        if k in self.by_i:
            at, count, place, sems = self.by_i.index(k), p.ny, self.then_y, self.got_ty
            total = self.sum_i[at, 0].astype(F32)
        else:
            at, count, place, sems = self.by_y.index(k), p.inner, self.then_i, self.got_ti
            total = self.sum_y[at, 0].astype(F32)
        for j in range(count - 1):
            self.got(place.at[j, at], sems.at[j, at])
            total = total + place[j, at].astype(F32)
        self.own[k] = total.astype(BF16)
        if k:
            self.go(self.own.at[k], self.outer.at[k - 1], self.got_outer.at[k - 1], p.at(do=k))

    def last(self):
        total = self.own[0].astype(F32)
        for k in range(1, OUTER):
            self.got(self.outer.at[k - 1], self.got_outer.at[k - 1])
            total = total + self.outer[k - 1].astype(F32)
        return total

    @staticmethod
    def scratch(nd, nt_, by_i, by_y, rows, columns):
        inner, ny = nd // OUTER, nt_ // 2
        ki, ky = len(by_i), len(by_y)
        leads = [
            (ny, OUTER, inner), (ny, OUTER, inner), (inner - 1, ki, ny), (ny - 1, ky, inner),
            (ki, ny), (ky, inner), (ny - 1, ki), (inner - 1, ky), (OUTER,), (OUTER - 1,),
        ]
        return [pltpu.VMEM(lead + (rows, columns), BF16) for lead in leads]

    @staticmethod
    def semaphores(nd, nt_, by_i, by_y):
        inner, ny = nd // OUTER, nt_ // 2
        di, dy, ki, ky = inner - 1, ny - 1, len(by_i), len(by_y)
        sends = ny + ky * dy * inner + ki * di * ny + ky * di + ki * dy + OUTER - 1
        shapes = [
            (sends,), (ny,), (di, ki, ny), (dy, ky, inner), (dy, ki), (di, ky), (OUTER - 1,),
        ]
        return [pltpu.SemaphoreType.DMA(shape) for shape in shapes]


class Exchange(Sender):
    def __init__(self, place, back, bufs, sems):
        super().__init__(place, sems[0])
        self.back = back
        self.own, self.near, self.far, self.made, self.entering = bufs
        self.s_near, self.s_far, self.s_enter = sems[1:]
        self.rows = HEAD // place.inner
        self.members = place.inner * place.nt
        self.me = place.i * place.nt + place.t

    def put(self, g, packed, total, edge, inlet):
        p = self.p
        row = lax.broadcasted_iota(jnp.int32, (8, LANES), 0)
        foot = jnp.where(row == 0, total, jnp.where(row == 1, edge, inlet))
        for sub in range(p.inner):
            self.own[g * p.inner + sub, : self.rows, :] = packed[
                sub * self.rows : (sub + 1) * self.rows
            ]
            self.own[g * p.inner + sub, self.rows :, :] = foot

    def state(self, g):
        p = self.p
        at = pl.ds(g * p.inner, p.inner)
        packed = self.entering[at, : self.rows, :].reshape(HEAD, LANES)
        return packed, self.entering[g * p.inner, self.rows :, :]

    def _peers(self):
        p = self.p
        return [
            (di, dy, dc)
            for di in range(p.inner) for dy in range(p.ny) for dc in range(2) if di or dy or dc
        ]

    def _member(self, di, dy, dc):
        p = self.p
        i, y = (p.i + p.inner - di) % p.inner, (p.y + p.ny - dy) % p.ny
        return i * p.nt + y * 2 + (p.c + dc) % 2

    def _edge(self, block):
        return block[self.rows + 1 : self.rows + 2, :]

    def _inlet(self, block):
        return block[self.rows + 2 : self.rows + 3, :]

    def _hand(self, blocks, place, sems):
        p = self.p
        for di, dy, dc in self._peers():
            to = p.at(0, di, dy, dc)
            member = (to[0] % p.inner) * p.nt + to[1]
            self.go(blocks.at[member], place.at[self.me], sems.at[self.me], to)
        place[self.me] = blocks[self.me]

    def step_near(self):
        self._hand(self.own, self.near, self.s_near)

    def step_far(self):
        p = self.p
        for peer in self._peers():
            m = self._member(*peer)
            self.got(self.near.at[m], self.s_near.at[m])
        border = self.near[0 if self.back else self.members - 1]
        total = jnp.zeros_like(border)
        for j in range(self.members):
            block = self.near[j]
            total = total + jnp.where(self._edge(block) == self._edge(border), block, 0.0)
        row = lax.broadcasted_iota(jnp.int32, total.shape, 0)
        self.far[p.o] = jnp.where(row > self.rows, border, total)
        for k in range(OUTER - 1, 0, -1):
            o = p.nearest(k)
            self.go(self.far.at[p.o], self.far.at[p.o], self.s_far.at[p.o], p.to(o, p.i, p.y, p.c))

    def step_enter(self):
        p = self.p
        for k in range(1, OUTER):
            o = p.nearest(k)
            self.got(self.far.at[o], self.s_far.at[o])
        order = list(range(self.members))
        if self.back:
            order.reverse()
        inlet = self._inlet(self.near[order[0]])
        incoming = jnp.zeros(self.near.shape[1:], F32)
        for o in range(OUTER):
            block = self.far[o]
            ids = jnp.where(o > p.o if self.back else o < p.o, self._edge(block), -1.0)
            incoming = incoming + jnp.where(ids == inlet, block, 0.0)
        for place, j in enumerate(order):
            block = self.near[j]
            if place:
                inlet = self._inlet(block)
                incoming = jnp.where(edge == inlet, running, 0.0)
            self.made[j] = incoming
            edge = self._edge(block)
            running = block + jnp.where(edge == inlet, incoming, 0.0)
        self._hand(self.made, self.entering, self.s_enter)

    def arrive(self):
        for peer in self._peers():
            m = self._member(*peer)
            self.got(self.entering.at[m], self.s_enter.at[m])

    @staticmethod
    def scratch(nd, nt_):
        inner = nd // OUTER
        shape = (HEAD // inner + 8, LANES)
        counts = [inner * nt_, inner * nt_, OUTER, inner * nt_, inner * nt_]
        return [pltpu.VMEM((count,) + shape, F32) for count in counts]

    @staticmethod
    def semaphores(nd, nt_):
        members = nd // OUTER * nt_
        counts = [2 * (members - 1) + OUTER - 1, members, OUTER, members]
        return [pltpu.SemaphoreType.DMA((count,)) for count in counts]


def left_lanes(shape):
    return lax.broadcasted_iota(jnp.int32, shape, len(shape) - 1) < HEAD


def split_heads(block, fill):
    left = left_lanes(block.shape)
    other = jnp.full_like(block, fill)
    return jnp.where(left, block, other), jnp.where(left, other, block)


def feature(values):
    return jnp.where(values > 0.0, values + 1.0, jnp.exp(jnp.minimum(values, 0.0)))


def pack_state(product):
    left = left_lanes((HEAD, LANES))
    return jnp.where(left, product[:HEAD], product[HEAD:])


def wide_state(packed):
    left = left_lanes((HEAD, LANES))
    zero = jnp.zeros_like(packed)
    return jnp.concatenate([jnp.where(left, packed, zero), jnp.where(left, zero, packed)], axis=0)


def two_parts(values):
    high = values.astype(BF16)
    return high, (values - high.astype(F32)).astype(BF16)


def twice(values):
    return jnp.concatenate([values, values], axis=1)


def same_head():
    row = lax.broadcasted_iota(jnp.int32, (LANES, LANES), 0) < HEAD
    return row == left_lanes((LANES, LANES))


class Total(Sender):
    def __init__(self, place, bufs, sems):
        super().__init__(place, sems[0])
        self.mine, self.core, self.plane, self.outer, self.whole = bufs
        self.got_core, self.got_plane, self.got_outer, self.got_whole = sems[1:]

    def start(self, value):
        p = self.p
        self.mine[...] = value.reshape(self.mine.shape)
        self.go(self.mine.at[1 - p.c], self.core, self.got_core.at[0], p.at(dc=1))

    def plane_step(self):
        p = self.p
        self.got(self.core, self.got_core.at[0])
        here = p.i * p.ny + p.y
        self.plane[here] = self.mine[p.c] + self.core[...]
        for peer in p.plane_peers():
            self.go(
                self.plane.at[here], self.plane.at[here], self.got_plane.at[here], p.at(*peer)
            )

    def outer_step(self):
        p = self.p
        for _, di, dy, _ in p.plane_peers():
            place = (p.i + p.inner - di) % p.inner * p.ny + (p.y + p.ny - dy) % p.ny
            self.got(self.plane.at[place], self.got_plane.at[place])
        total = self.plane[0]
        for k in range(1, p.inner * p.ny):
            total = total + self.plane[k]
        self.outer[p.o] = total
        for k in range(1, OUTER):
            to = p.to(p.nearest(k), p.i, p.y, p.c)
            self.go(self.outer.at[p.o], self.outer.at[p.o], self.got_outer.at[p.o], to)

    def core_step(self):
        p = self.p
        for k in range(1, OUTER):
            o = p.nearest(k)
            self.got(self.outer.at[o], self.got_outer.at[o])
        total = self.outer[0]
        for k in range(1, OUTER):
            total = total + self.outer[k]
        self.whole[p.c] = total
        self.go(self.whole.at[p.c], self.whole.at[p.c], self.got_whole.at[p.c], p.at(dc=1))

    def result(self):
        other = 1 - self.p.c
        self.got(self.whole.at[other], self.got_whole.at[other])
        return self.whole[...].reshape(-1, self.whole.shape[-1])

    @staticmethod
    def scratch(nd, nt_, rows, columns):
        leads = [(2,), (), (nd // OUTER * (nt_ // 2),), (OUTER,), (2,)]
        return [pltpu.VMEM(lead + (rows // 2, columns), F32) for lead in leads]

    @staticmethod
    def semaphores(nd, nt_):
        plane = nd // OUTER * (nt_ // 2)
        counts = [plane + OUTER, 1, plane, OUTER, 2]
        return [pltpu.SemaphoreType.DMA((count,)) for count in counts]


def kernel_whole(
    nd, nt_,
    *refs,
):
    given, results, scratch = refs[:16], refs[16:31], refs[31:]
    it = iter(scratch)

    def take(count):
        return [next(it) for _ in range(count)]

    (held_kv, held_qo, held_2, held_1) = take(4)
    operands, made = take(16), take(15)
    (tokens, segments, wq, wk, wv, wo, w1, w2, inner_bias,
     gain1, shift1, gain2, shift2, mixer_bias, outer_bias, cotangent) = operands
    (out, grad_tokens, grad_q, grad_k, grad_v, grad_o, grad_1, grad_2,
     grad_ib, grad_g1, grad_s1, grad_g2, grad_s2, grad_mb, grad_ob) = made
    (segc, mask, normed, normed_t, fq, fk, vb, num_s, den_s) = take(9)
    (res, unit, inv, h2, h2t, cot, dh2, act, dhid, dbt) = take(10)
    (do, dr, gn, gd, dk_s, dv_s, dq_s, dkv_s, dh1, sums, first_sums) = take(11)
    bufs_x, bufs_xb = take(5), take(5)
    bufs_f, bufs_qo, bufs_kv = take(10), take(10), take(10)
    bufs_t1, bufs_t2 = take(5), take(5)
    p = Place(nd, nt_)
    kv, qo = Gather(p, held_kv, take(6), KV_STRAIGHT), Gather(p, held_qo, take(6))
    g2, g1 = Gather(p, held_2, take(6)), Gather(p, held_1, take(6))
    ex = Exchange(p, False, bufs_x, take(4))
    xb = Exchange(p, True, bufs_xb, take(4))
    sf = Scatter(p, *WIDE_WAYS, bufs_f, take(7))
    sqo = Scatter(p, *EVEN_WAYS, bufs_qo, take(7))
    skv = Scatter(p, *EVEN_WAYS, bufs_kv, take(7))
    all_sum, first_sum = Total(p, bufs_t1, take(5)), Total(p, bufs_t2, take(5))

    rows_all, width = tokens.shape
    head, hidden = wq.shape[1], w1.shape[1]
    part_rows = wq.shape[0]
    block_shape = (OUTER, p.inner, part_rows)
    step, block, tile = 128, min(512, rows_all), min(512, rows_all)

    (in_sems, out_sems) = take(2)
    p.greet()
    loads = [
        pltpu.make_async_copy(given[n], operands[n], in_sems.at[n]) for n in range(len(given))
    ]
    stores = [
        pltpu.make_async_copy(made[n], results[n], out_sems.at[n]) for n in range(len(made))
    ]
    early = (3, 4)
    for n in early + tuple(n for n in range(len(given)) if n not in early):
        loads[n].start()
    here = (p.t, p.o, p.i)
    if head < LANES:
        blank = jnp.zeros((part_rows, 2 * LANES), BF16)
        held_kv[here] = blank
        held_qo[here] = blank
    for n in early:
        loads[n].wait()
    held_kv[here + (slice(None), slice(0, head))] = wk[...].astype(BF16)
    held_kv[here + (slice(None), slice(LANES, LANES + head))] = wv[...].astype(BF16)
    p.meet()
    kv.outer_start()
    kv.spread(0)
    for n in range(len(loads) - 1):
        if n not in early:
            loads[n].wait()
    held_qo[here + (slice(None), slice(0, head))] = wq[...].astype(BF16)
    held_qo[here + (slice(None), slice(LANES, LANES + head))] = wo[...].astype(BF16)
    held_2[here] = w2[...].astype(BF16)
    held_1[here] = w1[...].astype(BF16)
    segr = segments[:, pl.ds(pl.multiple_of(p.t * rows_all, LANES), rows_all)].astype(F32)
    for start in range(0, rows_all, LANES):
        wide = jnp.broadcast_to(segr[:, start : start + LANES], (8, LANES))
        segc[start : start + LANES, :] = jnp.transpose(wide)[:, 0:1]
    first_id, last_id = segr[:, 0:1], segr[:, rows_all - 1 : rows_all]

    def norm(k, _):
        at = pl.ds(pl.multiple_of(k * step, step), step)
        x = tokens[at, :].astype(F32)
        center = x - jnp.mean(x, axis=-1, keepdims=True)
        spread = jnp.mean(center * center, axis=-1, keepdims=True)
        y = center * lax.rsqrt(spread + EPSILON) * gain1[...] + shift1[...]
        normed[at, :] = y.astype(BF16)
        normed_t[:, at] = jnp.transpose(y).astype(BF16)
        return 0

    lax.fori_loop(0, rows_all // step, norm, 0)
    for start in range(0, rows_all, 128):
        later = lax.broadcasted_iota(jnp.int32, (128, rows_all), 0) + start
        earlier = lax.broadcasted_iota(jnp.int32, (128, rows_all), 1)
        same = segc[start : start + 128, :] == segr
        mask[start : start + 128, :] = jnp.where((later >= earlier) & same, 1.0, 0.0).astype(BF16)
    for k in range(1, OUTER):
        kv.spread(k)
    qo.outer_start()
    qo.spread(0)
    g2.outer_start()
    def keys_values(g):
        w = held_kv[g].reshape(width, 2 * LANES)
        both = nn(normed[...], w)
        keys = feature(both[:, :LANES]).astype(BF16)
        values = both[:, LANES:].astype(BF16)
        fk[g] = keys
        vb[g] = values
        kept = jnp.where(segc[...] == last_id, keys, jnp.zeros_like(keys))
        total = jnp.sum(kept.astype(F32), axis=0, keepdims=True)
        ex.put(g, pack_state(tn(kept, values)), total, last_id, first_id)

    def columns(dy, dc):
        return (p.y + dy) % p.ny * 2 + (p.c + dc) % 2

    for k in range(OUTER):
        kv.turn(k)
    for k in range(1, OUTER):
        qo.spread(k)
    g1.outer_start()
    keys_values(columns(0, 0))
    for k in range(OUTER):
        kv.corner(k)
    g2.spread(0)
    g1.spread(0)
    for dy in range(1, p.ny):
        keys_values(columns(dy, 0))
    for dy in range(p.ny):
        kv.core_done(dy)
        keys_values(columns(dy, 1))

    def queries(g):
        w = held_qo[g].reshape(width, 2 * LANES)
        fq[g] = feature(nn(normed[...], w[:, :LANES])).astype(BF16)

    ex.step_near()
    for k in range(OUTER):
        qo.turn(k)
    queries(columns(0, 0))
    for k in range(1, OUTER):
        g2.spread(k)
    loads[-1].wait()
    for start in range(0, rows_all, step):
        turned = jnp.transpose(cotangent[start : start + step, :].astype(F32))
        cot[:, start : start + step] = turned.astype(BF16)
    ex.step_far()
    g1.spread(1)
    for k in range(OUTER):
        qo.corner(k)
    for dy in range(1, p.ny):
        queries(columns(dy, 0))
    for dy in range(p.ny):
        qo.core_done(dy)
        queries(columns(dy, 1))


    def inside(g, _):
        values = split_heads(vb[g], 1.0)
        for start in range(0, rows_all, tile):
            end = start + tile
            now = mask[start:end, :end]
            query = split_heads(fq[g, start:end, :], 0.0)
            keys = fk[g, :end, :]
            parts = []
            for h in range(2):
                scores = nt(query[h], keys).astype(BF16) * now
                parts.append(nn(scores, values[h][:end]))
            left = left_lanes(parts[0].shape)
            num_s[g, start:end, :] = jnp.where(left, parts[0], parts[1])
            den_s[g, start:end, :] = pltpu.roll(
                jnp.where(left, parts[1], parts[0]), HEAD, 1
            )
        return 0

    lax.fori_loop(0, nt_ // 2, inside, 0)
    ex.step_enter()
    for k in range(2, OUTER):
        g1.spread(k)
    for k in range(OUTER):
        g2.turn(k)
    lax.fori_loop(nt_ // 2, nt_, inside, 0)
    for k in range(2):
        g1.turn(k)
    ex.arrive()

    def outside(g, _):
        packed, foot = ex.state(g)
        total = jnp.broadcast_to(jnp.transpose(foot)[:, 0:1], (LANES, LANES))
        total = jnp.where(same_head(), total, 0.0)
        parts = two_parts(jnp.concatenate([wide_state(packed), total], axis=1))
        query = fq[g]
        query = jnp.where(segc[...] == first_id, query, jnp.zeros_like(query))
        carried = nn(twice(query), jnp.concatenate(parts, axis=0))
        num = num_s[g] + carried[:, :LANES]
        den = den_s[g] + carried[:, LANES:]
        inverse = 1.0 / den
        den_s[g] = inverse
        num_s[g] = num * inverse
        return 0

    lax.fori_loop(0, nt_, outside, 0)
    mixed, rden = num_s, den_s
    for k in range(2, OUTER):
        g1.turn(k)

    def output_weight():
        parts = [held_qo[g, :, :, :, LANES:].reshape(width, LANES) for g in range(nt_)]
        return jnp.concatenate(parts, axis=1)

    def enter(k, _):
        at = pl.ds(pl.multiple_of(k * step, step), step)
        low = jnp.concatenate([mixed[g, at, :].astype(BF16) for g in range(nt_)], axis=1)
        r = tokens[at, :].astype(F32) + mixer_bias[...] + nt(low, output_weight())
        center = r - jnp.mean(r, axis=-1, keepdims=True)
        spread = jnp.mean(center * center, axis=-1, keepdims=True)
        scale = lax.rsqrt(spread + EPSILON)
        n = center * scale
        y = n * gain2[...] + shift2[...]
        res[at, :] = r + outer_bias[...]
        unit[at, :] = n
        inv[at, :] = scale
        h2[at, :] = y.astype(BF16)
        h2t[:, at] = jnp.transpose(y).astype(BF16)
        dh2[at, :] = jnp.zeros((step, width), F32)
        return 0

    lax.fori_loop(0, rows_all // step, enter, 0)
    sums[...] = jnp.zeros_like(sums)
    g2.core_done(0)
    g1.core_done(0)
    tall = width // OUTER

    def feed(g):
        wi = held_1[g].reshape(width, hidden)
        wt = held_2[g].reshape(width, hidden)
        total = jnp.zeros((1, hidden), F32)
        bias = inner_bias[:, pl.ds(pl.multiple_of(g * hidden, LANES), hidden)]
        for start in range(0, rows_all, block):
            end = start + block
            u = nn(h2[start:end, :], wi) + bias
            below = 0.5 * (1.0 + lax.erf(u * 0.7071067811865476))
            slope = below + u * (jnp.exp(-0.5 * (u * u)) * 0.3989422804014327)
            a = (u * below).astype(BF16)
            du = (nn(cotangent[start:end, :], wt) * slope).astype(BF16)
            act[start:end, :] = a
            dhid[start:end, :] = du
            total = total + jnp.sum(du.astype(F32), axis=0, keepdims=True)
            res[start:end, :] += nt(a, wt)
            dh2[start:end, :] += nt(du, wi)
        sums[pl.ds(8 + g, 1), 0:hidden] = total

    shape = (p.inner, part_rows, hidden)

    def feed_grads(y, mine):
        for o in range(OUTER):
            for s, (left, right) in enumerate(((h2t, dhid), (cot, act))):
                lanes = slice(s * hidden, (s + 1) * hidden)
                value = nn(left[o * tall : (o + 1) * tall, :], right[...]).reshape(shape)
                if mine:
                    value = value + sf.core[y, o, :, :, lanes].astype(F32)
                    sf.core[y, o, :, :, lanes] = value.astype(BF16)
                else:
                    sf.give[y, o, :, :, lanes] = value.astype(BF16)

    for dy in range(p.ny):
        y = (p.y + dy) % p.ny
        if dy:
            g2.core_done(dy)
            g1.core_done(dy)
        feed(y * 2 + 1 - p.c)
        feed_grads(y, False)
        sf.core_send(y)
        if not dy:
            for k in range(OUTER):
                g2.corner(k)
                g1.corner(k)
        feed(y * 2 + p.c)
        sf.core_wait(y)
        feed_grads(y, True)
        sf.first_i(dy, 2)
        if dy:
            sf.first_y(dy, 3, 0)
        else:
            sf.first_i(0, 0)

    def leave(k, _):
        at = pl.ds(pl.multiple_of(k * step, step), step)
        out[at, :] = res[at, :].astype(BF16)
        n = unit[at, :]
        grad = dh2[at, :]
        e = cotangent[at, :].astype(F32)
        pushed = grad * gain2[...]
        mean = jnp.mean(pushed, axis=-1, keepdims=True)
        along = jnp.mean(pushed * n, axis=-1, keepdims=True)
        back = e + (pushed - mean - n * along) * inv[at, :]
        dr[at, :] = back
        low = back.astype(BF16)
        wide = low.astype(F32)
        dbt[:, at] = jnp.transpose(wide).astype(BF16)
        pulled = nn(low, output_weight())
        for g in range(nt_):
            do[g, at, :] = pulled[:, g * LANES : (g + 1) * LANES]
        sums[2:3, :] += jnp.sum(grad * n, axis=0, keepdims=True)
        sums[3:4, :] += jnp.sum(grad, axis=0, keepdims=True)
        sums[4:5, :] += jnp.sum(wide, axis=0, keepdims=True)
        sums[5:6, :] += jnp.sum(e, axis=0, keepdims=True)
        return 0

    lax.fori_loop(0, rows_all // step, leave, 0)
    stores[0].start()

    def first(g, _):
        low = (do[g] * rden[g]).astype(BF16)
        gn[g] = low
        product = jnp.concatenate(two_parts(low.astype(F32) * mixed[g]), axis=1)
        minus = jnp.where(same_head(), -1.0, 0.0).astype(BF16)
        slope = nn(product, jnp.concatenate([minus, minus], axis=0))
        gd[g] = slope
        kept = jnp.where(segc[...] == first_id, fq[g], jnp.zeros_like(low))
        total = jnp.sum(kept.astype(F32) * slope, axis=0, keepdims=True)
        xb.put(g, pack_state(tn(kept, low)), total, first_id, last_id)
        return 0

    lax.fori_loop(0, nt_, first, 0)
    xb.step_near()
    for dy in range(1, p.ny):
        for k in range(2):
            sf.first_i(dy, k)
    all_sum.start(sums[...])

    def inside_back(g, _):
        values, keys = vb[g], fk[g]
        key_heads = split_heads(keys, 0.0)
        packed, foot = ex.state(g)
        state = jnp.concatenate(two_parts(wide_state(packed)), axis=1)
        query_t = jnp.transpose(fq[g].astype(F32)).astype(BF16)
        grad_t = jnp.transpose(gn[g].astype(F32)).astype(BF16)
        dk_t = jnp.zeros((LANES, rows_all), F32)
        dv_t = jnp.zeros((LANES, rows_all), F32)
        for start in range(0, rows_all, tile):
            end = start + tile
            now = mask[start:end, :end]
            query, grad = fq[g, start:end, :], gn[g, start:end, :]
            slope = gd[g, start:end, :]
            query_heads, grad_heads = split_heads(query, 0.0), split_heads(grad, 0.0)
            dq = jnp.where(
                segc[start:end, :] == first_id,
                nt(twice(grad), state) + slope * foot[0:1, :],
                0.0,
            )
            dk_parts, dv_parts = [], []
            for h in range(2):
                lanes = slice(h * HEAD, h * HEAD + 1)
                part = slice(h * HEAD, (h + 1) * HEAD)
                weight = nt(query_heads[h], keys[:end]).astype(BF16) * now
                share = (nt(grad_heads[h], values[:end]) + slope[:, lanes]).astype(BF16) * now
                dq = dq + nn(share, key_heads[h][:end])
                dk_parts.append(nn(query_t[part, start:end], share))
                dv_parts.append(nn(grad_t[part, start:end], weight))
            dk_now = jnp.concatenate(dk_parts, axis=0)
            dv_now = jnp.concatenate(dv_parts, axis=0)
            if end < rows_all:
                pad = jnp.zeros((LANES, rows_all - end), F32)
                dk_now = jnp.concatenate([dk_now, pad], axis=1)
                dv_now = jnp.concatenate([dv_now, pad], axis=1)
            dk_t, dv_t = dk_t + dk_now, dv_t + dv_now
            dq_s[g, start:end, :] = (dq * jnp.minimum(query.astype(F32), 1.0)).astype(BF16)
        dk_s[g] = jnp.transpose(dk_t)
        dv_s[g] = jnp.transpose(dv_t)
        return 0

    quarter = nt_ // 4
    lax.fori_loop(0, quarter, inside_back, 0)
    for dy in range(1, p.ny):
        sf.second_i(2, dy)
        for di in range(1, p.inner):
            sf.first_y(dy, 3, di)
    lax.fori_loop(quarter, 2 * quarter, inside_back, 0)
    xb.step_far()
    all_sum.plane_step()
    sf.second_i(2, 0)
    lax.fori_loop(2 * quarter, nt_, inside_back, 0)
    xb.step_enter()
    sf.third(2)
    for dy in range(1, p.ny):
        sf.second_i(0, dy)
    sf.first_i(0, 1)

    def attention_grads(scatter, dc, joint):
        for dy in list(range(1, p.ny)) + [0]:
            y = (p.y + dy) % p.ny
            g = y * 2 + (p.c + dc) % 2
            values = joint(g)
            if not dc:
                scatter.core_wait(y)
            for s, (left, right) in enumerate(values):
                lanes = slice(s * LANES, (s + 1) * LANES)
                value = nn(left, right).reshape(block_shape + (LANES,))
                if dc:
                    scatter.give[y, :, :, :, lanes] = value.astype(BF16)
                else:
                    value = value + scatter.core[y, :, :, :, lanes].astype(F32)
                    scatter.core[y, :, :, :, lanes] = value.astype(BF16)
            if dc:
                scatter.core_send(y)
            else:
                scatter.first(dy)

    def query_output(g):
        return ((normed_t[...], dq_s[g]), (dbt[...], mixed[g].astype(BF16)))

    attention_grads(sqo, 1, query_output)
    for dy in range(1, p.ny):
        sf.second_i(1, dy)
    sf.second_y(3)
    attention_grads(sqo, 0, query_output)
    sf.second_i(0, 0)
    all_sum.outer_step()

    def query_back(g, _):
        dh1[...] += nt(dq_s[g], held_qo[g, :, :, :, :LANES].reshape(width, LANES))
        return 0

    dh1[...] = jnp.zeros_like(dh1)
    lax.fori_loop(0, nt_, query_back, 0)
    sf.second_i(1, 0)
    xb.arrive()

    def key_value(g):
        packed, foot = xb.state(g)
        parts = two_parts(wide_state(packed))
        keys, values = fk[g], vb[g]
        dk = nt(twice(values), jnp.concatenate(parts, axis=1)) + foot[0:1, :]
        dv = nn(twice(keys), jnp.concatenate(parts, axis=0))
        closing = segc[...] == last_id
        dk = dk_s[g] + jnp.where(closing, dk, 0.0)
        dv = dv_s[g] + jnp.where(closing, dv, 0.0)
        dk = (dk * jnp.minimum(keys.astype(F32), 1.0)).astype(BF16)
        dv = dv.astype(BF16)
        dkv_s[g, :, :LANES] = dk
        dkv_s[g, :, LANES:] = dv
        return ((normed_t[...], dk), (normed_t[...], dv))

    attention_grads(skv, 1, key_value)
    sf.third(1)
    attention_grads(skv, 0, key_value)
    sf.third(3)

    def key_value_back(g, _):
        dh1[...] += nt(dkv_s[g], held_kv[g].reshape(width, 2 * LANES))
        return 0

    lax.fori_loop(0, nt_, key_value_back, 0)
    first_sums[...] = jnp.zeros_like(first_sums)

    def finish(k, _):
        at = pl.ds(pl.multiple_of(k * step, step), step)
        x = tokens[at, :].astype(F32)
        center = x - jnp.mean(x, axis=-1, keepdims=True)
        spread = jnp.mean(center * center, axis=-1, keepdims=True)
        scale = lax.rsqrt(spread + EPSILON)
        n = center * scale
        grad = dh1[at, :]
        pushed = grad * gain1[...]
        mean = jnp.mean(pushed, axis=-1, keepdims=True)
        along = jnp.mean(pushed * n, axis=-1, keepdims=True)
        back = (pushed - mean - n * along) * scale
        grad_tokens[at, :] = (dr[at, :] + back).astype(BF16)
        first_sums[0:1, :] += jnp.sum(grad * n, axis=0, keepdims=True)
        first_sums[8:9, :] += jnp.sum(grad, axis=0, keepdims=True)
        return 0

    lax.fori_loop(0, rows_all // step, finish, 0)
    stores[1].start()
    first_sum.start(first_sums[...])
    sqo.second()
    first_sum.plane_step()
    skv.second()
    for k in (2, 3, 1):
        sqo.third(k)
    first_sum.outer_step()
    for k in (2, 3, 1):
        skv.third(k)
    for scatter in (sf, sqo, skv):
        scatter.third(0)
    all_sum.core_step()
    total = sf.last()
    grad_1[...] = total[:, :hidden]
    grad_2[...] = total[:, hidden:]
    total = sqo.last()
    grad_q[...] = total[:, :head]
    grad_o[...] = total[:, LANES : LANES + head]
    first_sum.core_step()
    total = all_sum.result()
    grad_g2[...] = total[2:3, :]
    grad_s2[...] = total[3:4, :]
    grad_mb[...] = total[4:5, :]
    grad_ob[...] = total[5:6, :]
    for g in range(nt_):
        grad_ib[:, g * hidden : (g + 1) * hidden] = total[8 + g : 9 + g, :hidden]
    total = skv.last()
    grad_k[...] = total[:, :head]
    grad_v[...] = total[:, LANES : LANES + head]
    total = first_sum.result()
    grad_g1[...] = total[0:1, :]
    grad_s1[...] = total[8:9, :]
    for store in stores[2:]:
        store.start()
    for store in stores:
        store.wait()
    for each in (kv, qo, g2, g1, ex, xb, sf, sqo, skv, all_sum, first_sum):
        each.finish()


def kernel_outputs(count, *refs):
    given, made, held = (refs[k * count : (k + 1) * count] for k in range(3))
    loaded, stored = refs[3 * count :]
    loads = [pltpu.make_async_copy(given[k], held[k], loaded.at[k]) for k in range(count)]
    stores = [pltpu.make_async_copy(held[k], made[k], stored.at[k]) for k in range(count)]
    for load in loads:
        load.start()
    for load, store in zip(loads, stores):
        load.wait()
        store.start()
    for store in stores:
        store.wait()


def local(nd, nt_, *args):
    (tokens, segments, wq, wk, wv, wo, w1, w2, inner_bias, *vectors, cotangent) = args
    rows, width = tokens.shape
    inner = nd // OUTER
    part_rows, hidden = w1.shape
    hbm = pl.BlockSpec(memory_space=pl.ANY)
    group = (nt_, rows, LANES)
    total_rows = 8 + max(8, nt_)
    head = wq.shape[1]
    row = jax.ShapeDtypeStruct((1, width), F32)
    narrow = jax.ShapeDtypeStruct((part_rows, head), F32)
    wide = jax.ShapeDtypeStruct((part_rows, hidden), F32)
    outs = [
        jax.ShapeDtypeStruct(tokens.shape, BF16),
        jax.ShapeDtypeStruct(tokens.shape, BF16),
        narrow, narrow, narrow, narrow, wide, wide,
        jax.ShapeDtypeStruct((1, nt_ * hidden), F32),
        *[row] * 6,
    ]
    operands = (
        tokens, segments[None], wq, wk, wv, wo.T, w1, w2.T, inner_bias[None],
        *[v[None] for v in vectors], cotangent,
    )
    held = (nt_, OUTER, inner, part_rows)
    square = (rows, width)
    scratch = [
        pltpu.VMEM(held + (2 * LANES,), BF16),
        pltpu.VMEM(held + (2 * LANES,), BF16),
        pltpu.VMEM(held + (hidden,), BF16),
        pltpu.VMEM(held + (hidden,), BF16),
        *[pltpu.VMEM(v.shape, v.dtype) for v in operands],
        *[pltpu.VMEM(v.shape, v.dtype) for v in outs],
        pltpu.VMEM((rows, 1), F32),
        pltpu.VMEM((rows, rows), BF16),
        pltpu.VMEM(square, BF16),
        pltpu.VMEM((width, rows), BF16),
        pltpu.VMEM(group, BF16),
        pltpu.VMEM(group, BF16),
        pltpu.VMEM(group, BF16),
        pltpu.VMEM(group, F32),
        pltpu.VMEM(group, F32),
        pltpu.VMEM(square, F32),
        pltpu.VMEM(square, F32),
        pltpu.VMEM((rows, 1), F32),
        pltpu.VMEM(square, BF16),
        pltpu.VMEM((width, rows), BF16),
        pltpu.VMEM((width, rows), BF16),
        pltpu.VMEM(square, F32),
        pltpu.VMEM((rows, hidden), BF16),
        pltpu.VMEM((rows, hidden), BF16),
        pltpu.VMEM((width, rows), BF16),
        pltpu.VMEM(group, F32),
        pltpu.VMEM(square, F32),
        pltpu.VMEM(group, BF16),
        pltpu.VMEM(group, F32),
        pltpu.VMEM(group, F32),
        pltpu.VMEM(group, F32),
        pltpu.VMEM(group, BF16),
        pltpu.VMEM((nt_, rows, 2 * LANES), BF16),
        pltpu.VMEM(square, F32),
        pltpu.VMEM((total_rows, width), F32),
        pltpu.VMEM((16, width), F32),
    ]
    for _ in range(2):
        scratch += Exchange.scratch(nd, nt_)
    scratch += Scatter.scratch(nd, nt_, *WIDE_WAYS, part_rows, 2 * hidden)
    scratch += Scatter.scratch(nd, nt_, *EVEN_WAYS, part_rows, 2 * LANES)
    scratch += Scatter.scratch(nd, nt_, *EVEN_WAYS, part_rows, 2 * LANES)
    scratch += Total.scratch(nd, nt_, total_rows, width)
    scratch += Total.scratch(nd, nt_, 16, width)
    for _ in range(4):
        scratch += Gather.semaphores(nd, nt_)
    for _ in range(2):
        scratch += Exchange.semaphores(nd, nt_)
    for ways in (WIDE_WAYS, EVEN_WAYS, EVEN_WAYS):
        scratch += Scatter.semaphores(nd, nt_, *ways)
    for _ in range(2):
        scratch += Total.semaphores(nd, nt_)
    scratch += [pltpu.SemaphoreType.DMA((len(v),)) for v in (operands, outs)]
    results = pl.pallas_call(
        functools.partial(kernel_whole, nd, nt_),
        out_shape=outs,
        in_specs=[hbm] * len(operands),
        out_specs=[hbm] * len(outs),
        scratch_shapes=scratch,
        compiler_params=pltpu.CompilerParams(
            collective_id=0, has_side_effects=True, vmem_limit_bytes=VMEM_LIMIT
        ),
        name="whole_layer",
    )(*operands)
    final = pl.pallas_call(
        functools.partial(kernel_outputs, len(outs)),
        out_shape=outs,
        in_specs=[hbm] * len(outs),
        out_specs=[hbm] * len(outs),
        scratch_shapes=[pltpu.VMEM(o.shape, o.dtype) for o in outs]
        + [pltpu.SemaphoreType.DMA((len(outs),))] * 2,
        name="outputs",
    )(*results)
    return (
        *final[:5], final[5].T, final[6], final[7].T, *[v.reshape(-1) for v in final[8:]],
    )


def solution(mesh):
    rows = P(("dp", "tensor"), None)
    one, two, all_of = P("dp", "tensor"), P("tensor", "dp"), P()
    weights = (one, one, one, two, one, two)
    return jax.shard_map(
        functools.partial(local, mesh.shape["dp"], mesh.shape["tensor"]),
        mesh=mesh,
        in_specs=(rows, P("dp")) + weights + (all_of,) * 7 + (rows,),
        out_specs=(rows, rows) + weights + (all_of,) * 7,
        check_vma=False,
    )
```
